32 devices in a mesh: wide: 8 (over z, y), blk: 4 (over x, core).
Axes of the slice: x: 2, y: 2, z: 4, core: 2. Of those that a mesh axis runs over, the one named last changes fastest.
Arguments:
- embeddings: bfloat16 [4096, 768], P(('wide', 'blk')), may hold values from -100 to 100
- bucket_ids: int32 [4096], P(('wide', 'blk')), may hold values from 0 to 7, as said below
- slot_ids: int32 [4096], P(('wide', 'blk')), may hold values from 0 to 31, as said below
- valid_rows: int32 [4096], P(('wide', 'blk')), may hold values 0 or 1
Outputs:
- neighbour_mean: bfloat16 [4096, 768], P(('wide', 'blk'))
- max_cosine: bfloat16 [4096], P(('wide', 'blk'))
The draws below stay inside these ranges and needn't reach their ends.
Inputs may be any that keep to these rules, and one draw needn't show every extreme that they name: `bucket_ids`: bucket of each row. Every bucket holds at most 32 rows of one device; some bucket holds exactly 32 rows of every device. `slot_ids`: no two rows of one device share both bucket and slot.
All inputs are finite; a program needn't handle non-finite values. No bound on the sum of `valid_rows` on one device may be relied on, other than what follows from the above.
Results may differ from the reference program's by a relative error of at most 0.003.
Values may be sent and summed in bfloat16 or wider, within the bound.
A program may use at most 64 MiB of HBM per device.

```python
import jax
import jax.numpy as jnp
from jax import lax

D = 768
ROW_DEV = 128
BUCKETS = 8
SLOTS = 32
ROWS = 4096
N_WIDE = 8
N_BLK = 4


def chosen_cells(key):
    base_key = jax.random.fold_in(key, 7)
    key_parts = jax.random.split(base_key, 5)
    device_count = ROWS // ROW_DEV
    cell_count = BUCKETS * SLOTS
    bucket_of_cell = jnp.arange(cell_count, dtype=jnp.int32) // SLOTS
    popular = jax.random.randint(key_parts[0], (BUCKETS,), 0, 4)
    hot_bucket = jax.random.randint(key_parts[1], (), 0, BUCKETS)
    own_bucket = jax.random.randint(key_parts[2], (device_count, 1), 0, BUCKETS)
    jitter = jax.random.randint(key_parts[3], (device_count, cell_count), 0, 4096)
    forced = (bucket_of_cell[None, :] == hot_bucket) | (bucket_of_cell[None, :] == own_bucket)
    scores = jitter + popular[bucket_of_cell][None, :] * 2048 + forced.astype(jnp.int32) * 16384
    scores = scores * cell_count + jnp.arange(cell_count, dtype=jnp.int32)[None, :]
    picked = lax.top_k(scores, ROW_DEV)[1]
    order_keys = jax.random.randint(key_parts[4], (device_count, ROW_DEV), 0, 65536) * ROW_DEV + jnp.arange(ROW_DEV, dtype=jnp.int32)[None, :]
    order = lax.top_k(order_keys, ROW_DEV)[1]
    return jnp.take_along_axis(picked, order, axis=1).reshape(ROWS).astype(jnp.int32)


def draw_bucket_ids(key, part):
    return (chosen_cells(key) // SLOTS).astype(jnp.int32)


def draw_slot_ids(key, part):
    return (chosen_cells(key) % SLOTS).astype(jnp.int32)


def draw_embeddings(key, part):
    cell_ids = chosen_cells(key)
    bucket_rows = cell_ids // SLOTS
    key_parts = jax.random.split(jax.random.fold_in(key, 13), 4)
    centers = jax.random.truncated_normal(key_parts[0], -4.0, 4.0, (BUCKETS, D), jnp.float32)
    sub_centers = jax.random.truncated_normal(key_parts[1], -4.0, 4.0, (BUCKETS * 16, D), jnp.float32)
    sub_ids = jax.random.randint(key_parts[2], (ROWS,), 0, 16)
    noise = jax.random.truncated_normal(key_parts[3], -4.0, 4.0, (ROWS, D), jnp.float32)
    float_rows = 0.8 * centers[bucket_rows] + sub_centers[bucket_rows * 16 + sub_ids] + 0.7 * noise
    return float_rows.astype(jnp.bfloat16)


def touch_ends(drawn, rng, smallest, top_value):
    index_at = [jax.random.randint(jax.random.fold_in(rng, axis), (), 0, length) for axis, length in enumerate(drawn.shape)]
    longest = drawn.shape.index(max(drawn.shape))
    beside = index_at[:longest] + [(index_at[longest] + 1) % drawn.shape[longest]] + index_at[longest + 1:]
    return drawn.at[tuple(index_at)].set(smallest).at[tuple(beside)].set(top_value)


def setup_inputs(seed: int = 0) -> dict:
    key_list = jax.random.split(jax.random.key(seed), 5)
    embeddings = draw_embeddings(jax.random.fold_in(key_list[4], 71), 0)
    bucket_ids = draw_bucket_ids(jax.random.fold_in(key_list[4], 71), 0)
    slot_ids = draw_slot_ids(jax.random.fold_in(key_list[4], 71), 0)
    valid_rows = touch_ends((jax.random.randint(key_list[3], (ROWS,), 0, 8) < 7).astype(jnp.int32), jax.random.fold_in(key_list[3], 1), 0, 1)
    return dict(embeddings=embeddings, bucket_ids=bucket_ids, slot_ids=slot_ids, valid_rows=valid_rows)


sharpness = 10.0

def unit_rows(embeddings):
    float_rows = embeddings.astype(jnp.float32)
    inverse_norm = lax.rsqrt(lax.optimization_barrier(jnp.mean(float_rows * float_rows, axis=1, keepdims=True)) + 1e-06)
    return (float_rows * inverse_norm).astype(jnp.bfloat16)

def bucket_stats(queries, query_pos, key_rows, key_flags, key_pos):
    feature_count = queries.shape[1]
    cosine = lax.dot_general(queries, key_rows, (((1,), (1,)), ((), ())), preferred_element_type=jnp.float32) / feature_count
    usable = (key_flags[None, :] > 0) & (query_pos[:, None] != key_pos[None, :])
    best_cos = lax.optimization_barrier(jnp.max(jnp.where(usable, cosine, -1.0), axis=1))
    weights = jnp.where(usable, jnp.exp(sharpness * (cosine - 1.0)), 0.0)
    weight_total = lax.optimization_barrier(jnp.sum(weights, axis=1))
    summed = jnp.dot(weights.astype(jnp.bfloat16), key_rows, preferred_element_type=jnp.float32)
    return (best_cos, weight_total, summed)

def reference(embeddings, bucket_ids, slot_ids, valid_rows):
    unit_vectors = unit_rows(embeddings)
    row_index = jnp.arange(ROWS, dtype=jnp.int32)
    device = row_index // ROW_DEV
    source = device // N_BLK
    block_index = device % N_BLK
    per_bucket = N_BLK * N_WIDE * SLOTS
    position = (bucket_ids * per_bucket + (block_index * N_WIDE + source) * SLOTS + slot_ids).astype(jnp.int32)
    bucket_grid = jnp.zeros((BUCKETS * per_bucket, D), jnp.bfloat16).at[position].set(unit_vectors)
    bucket_flags = jnp.zeros((BUCKETS * per_bucket,), jnp.bfloat16).at[position].set(valid_rows.astype(jnp.bfloat16))
    bucket_grid = bucket_grid.reshape(BUCKETS, per_bucket, D)
    bucket_flags = bucket_flags.reshape(BUCKETS, per_bucket)

    def one_bucket(bucket_pair):
        member_rows, member_flags = bucket_pair
        positions = jnp.arange(per_bucket, dtype=jnp.int32)
        best_cos, weight_total, summed = bucket_stats(member_rows, positions, member_rows, member_flags, positions)
        mean_rows = ((member_rows.astype(jnp.float32) + summed) / (1.0 + weight_total[:, None])).astype(jnp.bfloat16)
        return (mean_rows, best_cos.astype(jnp.bfloat16))
    mean_grid, best_grid = lax.map(one_bucket, (bucket_grid, bucket_flags))
    neighbour_mean = mean_grid.reshape(BUCKETS * per_bucket, D)[position]
    max_cosine = best_grid.reshape(BUCKETS * per_bucket)[position]
    return (neighbour_mean, max_cosine)
```

```python
import functools

import jax
import jax.numpy as jnp
from jax import lax
from jax.experimental import pallas as pl
from jax.experimental.pallas import tpu as pltpu
from jax.sharding import PartitionSpec as P

sharpness = 10.0


def from_behind(value, axis, steps):
    count = lax.axis_size(axis)
    pairs = [(source, (source + steps) % count) for source in range(count)]
    return lax.ppermute(value, axis, pairs)


def unit_rows(embeddings):
    float_rows = embeddings.astype(jnp.float32)
    inverse_norm = lax.rsqrt(jnp.mean(float_rows * float_rows, axis=1, keepdims=True) + 1e-06)
    return (float_rows * inverse_norm).astype(jnp.bfloat16)


def bucket_stats(queries, query_pos, key_rows, key_flags, key_pos):
    feature_count = queries.shape[1]
    cosine = (
        lax.dot_general(
            queries, key_rows, (((1,), (1,)), ((), ())), preferred_element_type=jnp.float32
        )
        / feature_count
    )
    usable = (key_flags[None, :] > 0) & (query_pos[:, None] != key_pos[None, :])
    best_cos = jnp.max(jnp.where(usable, cosine, -1.0), axis=1)
    weights = jnp.where(usable, jnp.exp(sharpness * (cosine - 1.0)), 0.0)
    weight_total = jnp.sum(weights, axis=1)
    summed = jnp.dot(weights.astype(jnp.bfloat16), key_rows, preferred_element_type=jnp.float32)
    return (best_cos, weight_total, summed)


def by_bucket(embeddings, bucket_ids, slot_ids, valid_rows):
    unit_vectors = unit_rows(embeddings)
    row_count, feature_count = unit_vectors.shape
    groups = lax.axis_size("wide")
    blocks = lax.axis_size("blk")
    slot_count = 2 * row_count // groups
    block_rows = groups * slot_count
    cell_ids = bucket_ids * slot_count + slot_ids
    outgoing = jnp.zeros((block_rows, feature_count), jnp.bfloat16).at[cell_ids].set(unit_vectors)
    flag_rows = (
        jnp.zeros((block_rows,), jnp.bfloat16).at[cell_ids].set(valid_rows.astype(jnp.bfloat16))
    )
    arrived, arrived_flags = (
        lax.all_to_all(
            outgoing.reshape(groups, slot_count, feature_count),
            "wide",
            split_axis=0,
            concat_axis=0,
            tiled=True,
        ),
        lax.all_to_all(
            flag_rows.reshape(groups, slot_count), "wide", split_axis=0, concat_axis=0, tiled=True
        ),
    )
    queries = arrived.reshape(block_rows, feature_count)
    query_flags = arrived_flags.reshape(block_rows)
    my_block = lax.axis_index("blk")
    query_pos = my_block * block_rows + jnp.arange(block_rows, dtype=jnp.int32)

    def absorb(running, key_rows, key_flags, key_start):
        key_pos = key_start + jnp.arange(key_rows.shape[0], dtype=jnp.int32)
        best_cos, weight_total, summed = bucket_stats(
            queries, query_pos, key_rows, key_flags, key_pos
        )
        return (jnp.maximum(running[0], best_cos), running[1] + weight_total, running[2] + summed)

    initial = (
        jnp.full((block_rows,), -1.0, jnp.float32),
        jnp.zeros((block_rows,), jnp.float32),
        jnp.zeros((block_rows, feature_count), jnp.float32),
    )
    key_rows, key_flags = (queries, query_flags)
    running = absorb(initial, key_rows, key_flags, my_block * block_rows)
    for turn_index in range(1, blocks):
        key_rows, key_flags = from_behind((key_rows, key_flags), "blk", 1)
        running = absorb(
            running, key_rows, key_flags, (my_block - turn_index) % blocks * block_rows
        )
    best_cos, weight_total, summed = running
    mean_rows = ((queries.astype(jnp.float32) + summed) / (1.0 + weight_total[:, None])).astype(
        jnp.bfloat16
    )
    back_mean, back_best = (
        lax.all_to_all(
            mean_rows.reshape(groups, slot_count, feature_count),
            "wide",
            split_axis=0,
            concat_axis=0,
            tiled=True,
        ),
        lax.all_to_all(
            best_cos.astype(jnp.bfloat16).reshape(groups, slot_count),
            "wide",
            split_axis=0,
            concat_axis=0,
            tiled=True,
        ),
    )
    neighbour_mean = back_mean.reshape(block_rows, feature_count)[cell_ids]
    max_cosine = back_best.reshape(block_rows)[cell_ids]
    return (neighbour_mean, max_cosine)


PAIR = 2
PIECES = 4
GRANT = 56_240_000


def arrival_order(place, count):
    low, high = place, count - 1 - place
    order = []
    for distance in range(1, count):
        if distance <= low:
            order.append(place - distance)
        if distance <= high:
            order.append(place + distance)
    if low == 0 or high == 0:
        order = [order[1], order[1]] + order[2:]
    return order


def dense_kernel(
    planes, emb_hbm, bucket_hbm, valid_hbm, mean_ref, best_ref,
    emb_ref, bucket_ref, valid_ref, load_sem,
    keys, key_meta, queries, query_meta, query_col, total, peak, weight,
    part_out, part_in, stat_out, stat_in,
    plane_keys, plane_meta, help_total, help_peak, help_weight,
    help_out, help_in, help_stat_out, help_stat_in,
    z_send, z_recv, zm_send, zm_recv, c_send, c_recv, cm_send, cm_recv,
    q_send, q_recv, qm_send, qm_recv, p_send, p_recv, s_send, s_recv,
    f_send, f_recv, fm_send, fm_recv, h_send, h_recv,
):
    rows, features = emb_ref.shape
    spots = queries.shape[0]
    wide, blk = lax.axis_index("wide"), lax.axis_index("blk")
    z, y = lax.div(wide, PAIR), lax.rem(wide, PAIR)
    x, core = lax.div(blk, PAIR), lax.rem(blk, PAIR)
    other = 1 - core
    columns = spots // PAIR
    piece = rows // PIECES

    def at(z_at, y_at, x_at, core_at):
        return (z_at * PAIR + y_at, x_at * PAIR + core_at)

    def spot_device(spot):
        dy, dx = divmod(spot, columns)
        return at(z, lax.rem(y + dy, PAIR), lax.rem(x + dx, columns), core)

    def seen_from(spot):
        dy, dx = divmod(spot, columns)
        return (-dy) % PAIR * columns + (-dx) % columns

    def remote(source, target, send, recv, device):
        return pltpu.make_async_remote_copy(
            src_ref=source, dst_ref=target, send_sem=send, recv_sem=recv,
            device_id=device, device_id_type=pl.DeviceIdType.MESH,
        )

    partner = at(z, y, x, other)
    has_low, has_high = z > 0, z < planes - 1

    loads = [
        pltpu.make_async_copy(source, target, load_sem.at[index])
        for index, (source, target) in enumerate(
            ((emb_hbm, emb_ref), (bucket_hbm, bucket_ref), (valid_hbm, valid_ref))
        )
    ]
    for load in loads:
        load.start()

    barrier = pltpu.get_barrier_semaphore()

    def greet(device):
        pl.semaphore_signal(barrier, inc=1, device_id=device, device_id_type=pl.DeviceIdType.MESH)

    greet(partner)
    for spot in range(1, spots):
        greet(spot_device(spot))

    @pl.when(has_low)
    def _():
        greet(at(z - 1, y, x, core))

    @pl.when(has_high)
    def _():
        greet(at(z + 1, y, x, core))

    for load in loads:
        load.wait()
    floats = emb_ref[...].astype(jnp.float32)
    inverse = lax.rsqrt(jnp.mean(floats * floats, axis=1, keepdims=True) + 1e-06)
    unit = (floats * inverse).astype(jnp.bfloat16)
    keys[z, core] = unit
    queries[0] = unit
    meta = jnp.concatenate([bucket_ref[...], valid_ref[...]], axis=0).astype(jnp.float32)
    key_meta[z, core] = meta
    query_meta[0] = meta

    pl.semaphore_wait(barrier, jnp.where(has_low & has_high, spots + 2, spots + 1))

    def z_meta(source, way, to):
        ref = key_meta.at[source, core]
        return remote(
            ref, ref, zm_send.at[source, way], zm_recv.at[source], at(to, y, x, core)
        )

    def z_copy(source, way, to, part):
        ref = keys.at[source, core, pl.ds(part * piece, piece)]
        return remote(
            ref, ref, z_send.at[source, way, part], z_recv.at[source, part], at(to, y, x, core)
        )

    def c_meta(source, side):
        ref = key_meta.at[source, side]
        return remote(ref, ref, cm_send.at[source], cm_recv.at[source], partner)

    def c_copy(source, side, part):
        ref = keys.at[source, side, pl.ds(part * piece, piece)]
        return remote(ref, ref, c_send.at[source, part], c_recv.at[source, part], partner)

    def q_meta(spot):
        mine = seen_from(spot)
        return remote(
            query_meta.at[0], query_meta.at[mine], qm_send.at[spot], qm_recv.at[mine],
            spot_device(spot),
        )

    def q_copy(spot):
        mine = seen_from(spot)
        return remote(
            queries.at[0], queries.at[mine], q_send.at[spot], q_recv.at[mine], spot_device(spot)
        )

    def send_ways(source, act):
        @pl.when(has_high & ((source < z) | ((source == z) & (z < planes - 2))))
        def _():
            act(1, z + 1)

        @pl.when(has_low & ((source > z) | ((source == z) & (z > 1))))
        def _():
            act(0, z - 1)

    send_ways(z, lambda way, to: z_meta(z, way, to).start())
    for part in range(PIECES):
        send_ways(z, lambda way, to: z_copy(z, way, to, part).start())
    c_meta(z, core).start()
    for part in range(PIECES):
        c_copy(z, core, part).start()
    for spot in range(spots - 1, 0, -1):
        q_meta(spot).start()
        q_copy(spot).start()

    def column_of(spot):
        row = query_meta[spot, 0:1, :]
        query_col[spot] = jnp.transpose(jnp.broadcast_to(row, (rows, rows)))

    def terms(chosen, buckets, block, metas, own_keys):
        count = chosen.shape[0]
        cosine = lax.dot_general(
            chosen, block, (((1,), (1,)), ((), ())), preferred_element_type=jnp.float32
        ) * (1.0 / features)
        line = lax.broadcasted_iota(jnp.int32, (count, rows), 0)
        lane = lax.broadcasted_iota(jnp.int32, (count, rows), 1)
        factors = []
        peaks = None
        sums = None
        for index, (meta, own) in enumerate(zip(metas, own_keys)):
            wanted = jnp.where(meta[1:2, :] > 0, meta[0:1, :], -1.0)
            usable = buckets == wanted
            if own is not None:
                shift = jnp.where(own, 0, count + rows)
                usable = usable & (line + shift != lane)
            values = cosine[:, index * rows : (index + 1) * rows]
            best = jnp.where(usable, values, -1.0)
            factor = jnp.where(usable, jnp.exp(sharpness * (values - 1.0)), 0.0)
            factors.append(factor.astype(jnp.bfloat16))
            peaks = best if peaks is None else jnp.maximum(peaks, best)
            sums = factor if sums is None else sums + factor
        summed = jnp.dot(
            jnp.concatenate(factors, axis=1), block, preferred_element_type=jnp.float32
        )
        return peaks, sums, summed

    def absorb(first, last, source, fresh, sides=tuple(range(PAIR))):
        count = (last - first) * rows
        if len(sides) == PAIR:
            block = keys[source].reshape(PAIR * rows, features)
        else:
            block = keys[source, sides[0]]
        peaks, sums, summed = terms(
            queries[first:last].reshape(count, features),
            query_col[first:last].reshape(count, rows),
            block,
            [key_meta[source, side] for side in sides],
            [(source == z) & (core == side) if first == 0 else None for side in sides],
        )
        part = (last - first, rows)
        if fresh:
            peak[first:last] = peaks.reshape(*part, rows)
            weight[first:last] = sums.reshape(*part, rows)
            total[first:last] = summed.reshape(*part, features)
        else:
            peak[first:last] = jnp.maximum(peak[first:last], peaks.reshape(*part, rows))
            weight[first:last] += sums.reshape(*part, rows)
            total[first:last] += summed.reshape(*part, features)

    def wait_partner(source):
        c_meta(source, other).wait_recv()
        for part in range(PIECES):
            c_copy(source, other, part).wait_recv()

    def take(*arriving):
        for source in arriving:
            z_meta(source, 0, z).wait_recv()
            send_ways(source, lambda way, to: z_meta(source, way, to).start())
            c_meta(source, core).start()
        for part in range(PIECES):
            for source in arriving:
                z_copy(source, 0, z, part).wait_recv()
                send_ways(source, lambda way, to: z_copy(source, way, to, part).start())
                c_copy(source, core, part).start()

    orders = [arrival_order(place, planes) for place in range(planes)]

    def source_at(turn):
        source = jnp.int32(orders[0][turn])
        for place in range(1, planes):
            source = jnp.where(z == place, orders[place][turn], source)
        return source

    sources = [source_at(turn) for turn in range(planes - 1)]
    inner = has_low & has_high
    final = sources[-1]

    def at_end(source):
        @pl.when(jnp.logical_not(inner))
        def _():
            take(source)

    column_of(0)
    wait_partner(z)
    absorb(0, 1, z, True)

    @pl.when(inner)
    def _():
        take(*sources[:2])
        for source in sources[2:]:
            take(source)

    def each_source(act):
        for turn, source in enumerate(sources[:-1]):
            if turn == 1:

                @pl.when(inner)
                def _():
                    act(source)
            else:
                act(source)

    at_end(sources[0])
    for source in sources[2:-1]:
        at_end(source)

    def own_rows(source):
        wait_partner(source)
        absorb(0, 1, source, False)

    each_source(own_rows)

    def f_copies(spot):
        return (
            remote(
                query_meta.at[spot], plane_meta.at[spot], fm_send.at[spot], fm_recv.at[spot], partner
            ),
            remote(queries.at[spot], plane_keys.at[spot], f_send.at[spot], f_recv.at[spot], partner),
        )

    helper = (z == 1) | (z == planes - 2)
    end_z = jnp.where(z == 1, 0, planes - 1)

    for spot in range(1, spots):
        q_meta(seen_from(spot)).wait_recv()
        column_of(spot)
        q_copy(seen_from(spot)).wait_recv()

        @pl.when(helper)
        def _():
            for copy in f_copies(spot):
                copy.start()

    def h_copies():
        device = at(jnp.where(helper, end_z, z), y, x, core)
        return (
            remote(help_stat_out, help_stat_in, h_send.at[0], h_recv.at[0], device),
            remote(help_out, help_in, h_send.at[1], h_recv.at[1], device),
        )

    absorb(1, spots, z, True)

    each_source(lambda source: absorb(1, spots, source, False))
    at_end(final)
    absorb(1, spots, final, False, (core,))
    wait_partner(final)

    def stat_rows(spot):
        top = jnp.max(jnp.transpose(peak[spot]), axis=0, keepdims=True)
        mass = jnp.sum(jnp.transpose(weight[spot]), axis=0, keepdims=True)
        return top, mass

    across, along = columns, 1
    corner = across + along
    half = rows // 2
    halves = (pl.ds(0, half), pl.ds(half, half))

    def p_copy(spot, side):
        mine = seen_from(spot)
        return remote(
            part_out.at[spot, halves[side]], part_in.at[mine, halves[side]],
            p_send.at[spot, side], p_recv.at[mine, side], spot_device(spot),
        )

    def corner_copy(side):
        spot = (along, across)[side]
        return remote(
            part_out.at[corner, halves[side]], part_in.at[corner, halves[side]],
            p_send.at[corner, side], p_recv.at[corner, side], spot_device(spot),
        )

    def s_copy(spot):
        mine = seen_from(spot)
        return remote(
            stat_out.at[spot], stat_in.at[mine], s_send.at[spot], s_recv.at[mine],
            spot_device(spot),
        )

    absorb(corner, corner + 1, final, False, (other,))
    part_out[corner] = total[corner].astype(jnp.bfloat16)
    corner_copy(0).start()
    corner_copy(1).start()
    passing = ((along, 1), (across, 0))
    for spot, side in passing:
        absorb(spot, spot + 1, final, False, (other,))
        part_out[spot, halves[1 - side]] = total[spot, halves[1 - side]].astype(jnp.bfloat16)
        p_copy(spot, 1 - side).start()
    for spot in range(spots - 1, 0, -1):
        stat_out[spot] = jnp.concatenate(stat_rows(spot), axis=0)
        s_copy(spot).start()
    @pl.when(helper)
    def _():
        row = key_meta[end_z, core, 0:1, :]
        column = jnp.transpose(jnp.broadcast_to(row, (rows, rows)))
        for spot in range(spots):
            if spot == 0:
                second, second_meta = keys[z, other], key_meta[z, other]
            else:
                for copy in f_copies(spot):
                    copy.wait_recv()
                second, second_meta = plane_keys[spot], plane_meta[spot]
            peaks, sums, summed = terms(
                keys[end_z, core],
                column,
                jnp.concatenate([queries[spot], second], axis=0),
                [query_meta[spot], second_meta],
                [None, None],
            )
            if spot == 0:
                help_peak[...] = peaks
                help_weight[...] = sums
                help_total[...] = summed
            else:
                help_peak[...] = jnp.maximum(help_peak[...], peaks)
                help_weight[...] += sums
                help_total[...] += summed
        help_out[...] = help_total[...].astype(jnp.bfloat16)
        top = jnp.max(jnp.transpose(help_peak[...]), axis=0, keepdims=True)
        mass = jnp.sum(jnp.transpose(help_weight[...]), axis=0, keepdims=True)
        help_stat_out[...] = jnp.concatenate([top, mass], axis=0)
        for copy in h_copies():
            copy.start()

    for spot, side in passing:
        corner_copy(side).wait_recv()
        part_out[spot, halves[side]] = (
            total[spot, halves[side]] + part_in[corner, halves[side]].astype(jnp.float32)
        ).astype(jnp.bfloat16)
        p_copy(spot, side).start()

    absorb(0, 1, final, False)
    stat_in[0] = jnp.concatenate(stat_rows(0), axis=0)
    total[0] += queries[0].astype(jnp.float32)

    @pl.when(jnp.logical_not(inner))
    def _():
        for copy in h_copies():
            copy.wait_recv()
        stat_in[0] = jnp.concatenate(
            [
                jnp.maximum(stat_in[0, 0:1, :], help_stat_in[0:1, :]),
                stat_in[0, 1:2, :] + help_stat_in[1:2, :],
            ],
            axis=0,
        )
        total[0] += help_in[...].astype(jnp.float32)

    top, mass = stat_in[0, 0:1, :], stat_in[0, 1:2, :]
    for spot in range(1, spots):
        s_copy(seen_from(spot)).wait_recv()
        top = jnp.maximum(top, stat_in[spot, 0:1, :])
        mass = mass + stat_in[spot, 1:2, :]
    best_ref[...] = top
    below = jnp.transpose(jnp.broadcast_to(1.0 + mass, (rows, rows)))[:, 0:1]
    for spot, _ in passing:
        for side in range(2):
            p_copy(seen_from(spot), side).wait_recv()
    result = total[0]
    for spot, _ in passing:
        result = result + part_in[spot].astype(jnp.float32)
    mean_ref[...] = (result / below).astype(jnp.bfloat16)

    send_ways(z, lambda way, to: z_meta(z, way, to).wait_send())
    for part in range(PIECES):
        send_ways(z, lambda way, to: z_copy(z, way, to, part).wait_send())
    c_meta(z, core).wait_send()
    for part in range(PIECES):
        c_copy(z, core, part).wait_send()
    def sent(source):
        send_ways(source, lambda way, to: z_meta(source, way, to).wait_send())
        c_meta(source, core).wait_send()
        for part in range(PIECES):
            send_ways(source, lambda way, to: z_copy(source, way, to, part).wait_send())
            c_copy(source, core, part).wait_send()

    each_source(sent)
    sent(final)

    @pl.when(helper)
    def _():
        for spot in range(1, spots):
            for copy in f_copies(spot):
                copy.wait_send()
        for copy in h_copies():
            copy.wait_send()

    for spot in range(1, spots):
        q_meta(spot).wait_send()
        q_copy(spot).wait_send()
        s_copy(spot).wait_send()
    for side in range(2):
        corner_copy(side).wait_send()
        for spot, _ in passing:
            p_copy(spot, side).wait_send()


def finish_kernel(mean_ref, best_ref, mean_out, best_out, line, sem):
    line[...] = best_ref[0].astype(jnp.bfloat16)
    copies = [
        pltpu.make_async_copy(mean_ref, mean_out, sem.at[0]),
        pltpu.make_async_copy(line, best_out, sem.at[1]),
    ]
    for copy in copies:
        copy.start()
    for copy in copies:
        copy.wait()


def finish(mean, best):
    rows, features = mean.shape
    vmem = pl.BlockSpec(memory_space=pltpu.VMEM)
    hbm = pl.BlockSpec(memory_space=pltpu.HBM)
    return pl.pallas_call(
        finish_kernel,
        out_shape=(
            jax.ShapeDtypeStruct((rows, features), jnp.bfloat16),
            jax.ShapeDtypeStruct((rows,), jnp.bfloat16),
        ),
        in_specs=[vmem, vmem],
        out_specs=(hbm, hbm),
        scratch_shapes=[pltpu.VMEM((rows,), jnp.bfloat16), pltpu.SemaphoreType.DMA((2,))],
        compiler_params=pltpu.CompilerParams(vmem_limit_bytes=4_000_000),
    )(mean, best)


def dense(embeddings, bucket_ids, valid_rows):
    rows, features = embeddings.shape
    planes = lax.axis_size("wide") // PAIR
    spots = lax.axis_size("blk")
    dma = pltpu.SemaphoreType.DMA
    vmem = pl.BlockSpec(memory_space=pltpu.VMEM)
    mean, best = pl.pallas_call(
        functools.partial(dense_kernel, planes),
        out_shape=(
            jax.ShapeDtypeStruct((rows, features), jnp.bfloat16),
            jax.ShapeDtypeStruct((1, rows), jnp.float32),
        ),
        in_specs=[pl.BlockSpec(memory_space=pltpu.HBM)] * 3,
        out_specs=(vmem, vmem),
        scratch_shapes=[
            pltpu.VMEM((rows, features), jnp.bfloat16),
            pltpu.VMEM((1, rows), jnp.int32),
            pltpu.VMEM((1, rows), jnp.int32),
            dma((3,)),
            pltpu.VMEM((planes, PAIR, rows, features), jnp.bfloat16),
            pltpu.VMEM((planes, PAIR, 2, rows), jnp.float32),
            pltpu.VMEM((spots, rows, features), jnp.bfloat16),
            pltpu.VMEM((spots, 2, rows), jnp.float32),
            pltpu.VMEM((spots, rows, rows), jnp.float32),
            pltpu.VMEM((spots, rows, features), jnp.float32),
            pltpu.VMEM((spots, rows, rows), jnp.float32),
            pltpu.VMEM((spots, rows, rows), jnp.float32),
            pltpu.VMEM((spots, rows, features), jnp.bfloat16),
            pltpu.VMEM((spots, rows, features), jnp.bfloat16),
            pltpu.VMEM((spots, 2, rows), jnp.float32),
            pltpu.VMEM((spots, 2, rows), jnp.float32),
            pltpu.VMEM((spots, rows, features), jnp.bfloat16),
            pltpu.VMEM((spots, 2, rows), jnp.float32),
            pltpu.VMEM((rows, features), jnp.float32),
            pltpu.VMEM((rows, rows), jnp.float32),
            pltpu.VMEM((rows, rows), jnp.float32),
            pltpu.VMEM((rows, features), jnp.bfloat16),
            pltpu.VMEM((rows, features), jnp.bfloat16),
            pltpu.VMEM((2, rows), jnp.float32),
            pltpu.VMEM((2, rows), jnp.float32),
            dma((planes, 2, PIECES)), dma((planes, PIECES)), dma((planes, 2)), dma((planes,)),
            dma((planes, PIECES)), dma((planes, PIECES)), dma((planes,)), dma((planes,)),
            dma((spots,)), dma((spots,)), dma((spots,)), dma((spots,)),
            dma((spots, 2)), dma((spots, 2)), dma((spots,)), dma((spots,)),
            dma((spots,)), dma((spots,)), dma((spots,)), dma((spots,)), dma((2,)), dma((2,)),
        ],
        compiler_params=pltpu.CompilerParams(
            collective_id=0, has_side_effects=True, vmem_limit_bytes=GRANT
        ),
    )(*[pltpu.with_memory_space_constraint(v, pltpu.HBM) for v in (embeddings, bucket_ids.reshape(1, rows), valid_rows.reshape(1, rows))])
    return finish(mean, best)


def on_device(embeddings, bucket_ids, slot_ids, valid_rows):
    rows = embeddings.shape[0]
    groups = lax.axis_size("wide")
    blocks = lax.axis_size("blk")
    bucket_work = blocks * (2 * rows) ** 2
    dense_work = groups * blocks * rows**2
    fits = groups % PAIR == 0 and groups >= 4 * PAIR and blocks == PAIR * PAIR and rows == 128
    if fits and dense_work <= 4 * bucket_work:
        return dense(embeddings, bucket_ids, valid_rows)
    return by_bucket(embeddings, bucket_ids, slot_ids, valid_rows)


def solution(mesh):
    in_specs = (
        P(("wide", "blk"), None),
        P(("wide", "blk")),
        P(("wide", "blk")),
        P(("wide", "blk")),
    )
    out_specs = (P(("wide", "blk"), None), P(("wide", "blk")))
    return jax.shard_map(
        on_device, mesh=mesh, in_specs=in_specs, out_specs=out_specs, check_vma=False
    )
```

```python
import functools

import jax
import jax.numpy as jnp
from jax import lax
from jax.experimental import pallas as pl
from jax.experimental.pallas import tpu as pltpu
from jax.sharding import PartitionSpec as P

sharpness = 10.0


def from_behind(value, axis, steps):
    count = lax.axis_size(axis)
    pairs = [(source, (source + steps) % count) for source in range(count)]
    return lax.ppermute(value, axis, pairs)


def unit_rows(embeddings):
    float_rows = embeddings.astype(jnp.float32)
    inverse_norm = lax.rsqrt(jnp.mean(float_rows * float_rows, axis=1, keepdims=True) + 1e-06)
    return (float_rows * inverse_norm).astype(jnp.bfloat16)


def bucket_stats(queries, query_pos, key_rows, key_flags, key_pos):
    feature_count = queries.shape[1]
    cosine = (
        lax.dot_general(
            queries, key_rows, (((1,), (1,)), ((), ())), preferred_element_type=jnp.float32
        )
        / feature_count
    )
    usable = (key_flags[None, :] > 0) & (query_pos[:, None] != key_pos[None, :])
    best_cos = jnp.max(jnp.where(usable, cosine, -1.0), axis=1)
    weights = jnp.where(usable, jnp.exp(sharpness * (cosine - 1.0)), 0.0)
    weight_total = jnp.sum(weights, axis=1)
    summed = jnp.dot(weights.astype(jnp.bfloat16), key_rows, preferred_element_type=jnp.float32)
    return (best_cos, weight_total, summed)


def by_bucket(embeddings, bucket_ids, slot_ids, valid_rows):
    unit_vectors = unit_rows(embeddings)
    row_count, feature_count = unit_vectors.shape
    groups = lax.axis_size("wide")
    blocks = lax.axis_size("blk")
    slot_count = 2 * row_count // groups
    block_rows = groups * slot_count
    cell_ids = bucket_ids * slot_count + slot_ids
    outgoing = jnp.zeros((block_rows, feature_count), jnp.bfloat16).at[cell_ids].set(unit_vectors)
    flag_rows = (
        jnp.zeros((block_rows,), jnp.bfloat16).at[cell_ids].set(valid_rows.astype(jnp.bfloat16))
    )
    arrived, arrived_flags = (
        lax.all_to_all(
            outgoing.reshape(groups, slot_count, feature_count),
            "wide",
            split_axis=0,
            concat_axis=0,
            tiled=True,
        ),
        lax.all_to_all(
            flag_rows.reshape(groups, slot_count), "wide", split_axis=0, concat_axis=0, tiled=True
        ),
    )
    queries = arrived.reshape(block_rows, feature_count)
    query_flags = arrived_flags.reshape(block_rows)
    my_block = lax.axis_index("blk")
    query_pos = my_block * block_rows + jnp.arange(block_rows, dtype=jnp.int32)

    def absorb(running, key_rows, key_flags, key_start):
        key_pos = key_start + jnp.arange(key_rows.shape[0], dtype=jnp.int32)
        best_cos, weight_total, summed = bucket_stats(
            queries, query_pos, key_rows, key_flags, key_pos
        )
        return (jnp.maximum(running[0], best_cos), running[1] + weight_total, running[2] + summed)

    initial = (
        jnp.full((block_rows,), -1.0, jnp.float32),
        jnp.zeros((block_rows,), jnp.float32),
        jnp.zeros((block_rows, feature_count), jnp.float32),
    )
    key_rows, key_flags = (queries, query_flags)
    running = absorb(initial, key_rows, key_flags, my_block * block_rows)
    for turn_index in range(1, blocks):
        key_rows, key_flags = from_behind((key_rows, key_flags), "blk", 1)
        running = absorb(
            running, key_rows, key_flags, (my_block - turn_index) % blocks * block_rows
        )
    best_cos, weight_total, summed = running
    mean_rows = ((queries.astype(jnp.float32) + summed) / (1.0 + weight_total[:, None])).astype(
        jnp.bfloat16
    )
    back_mean, back_best = (
        lax.all_to_all(
            mean_rows.reshape(groups, slot_count, feature_count),
            "wide",
            split_axis=0,
            concat_axis=0,
            tiled=True,
        ),
        lax.all_to_all(
            best_cos.astype(jnp.bfloat16).reshape(groups, slot_count),
            "wide",
            split_axis=0,
            concat_axis=0,
            tiled=True,
        ),
    )
    neighbour_mean = back_mean.reshape(block_rows, feature_count)[cell_ids]
    max_cosine = back_best.reshape(block_rows)[cell_ids]
    return (neighbour_mean, max_cosine)


PAIR = 2
PLANES = 4
SPOTS = PAIR * PAIR
PIECES = 4
GRANT = 56_240_000


def dense_kernel(
    emb_hbm, bucket_hbm, valid_hbm, mean_ref, best_ref,
    emb_ref, bucket_ref, valid_ref,
    keys, key_meta, plane, spot_meta, plane_meta, query_col, total, peak, weight,
    part_out, part_in, stat_out, stat_in, help_out, help_in, help_stat_out, help_stat_in,
    load_sem, z_send, z_recv, zm_send, zm_recv, c_send, c_recv, cm_send, cm_recv,
    q_send, q_recv, qm_send, qm_recv, f_send, f_recv,
    p_send, corner_recv, p_recv, s_send, sc_recv, s_recv, h_send, h_recv,
):
    rows, features = emb_ref.shape
    piece = rows // PIECES
    half = rows // 2
    halves = (pl.ds(0, half), pl.ds(half, half))
    wide, blk = lax.axis_index("wide"), lax.axis_index("blk")
    z, y = lax.div(wide, PAIR), lax.rem(wide, PAIR)
    x, core = lax.div(blk, PAIR), lax.rem(blk, PAIR)
    beside_x, beside_y, corner = 1, 2, 3

    def at(z_at, y_at, x_at, core_at):
        return (z_at * PAIR + y_at, x_at * PAIR + core_at)

    partner = at(z, y, x, 1 - core)
    x_device = at(z, y, 1 - x, core)
    y_device = at(z, 1 - y, x, core)
    inner = (z > 0) & (z < PLANES - 1)
    lower = z < PLANES // 2
    across_z = PLANES - 1 - z
    end_device = at(jnp.where(lower, 0, PLANES - 1), y, x, core)
    next_device = at(jnp.where(lower, 1, PLANES - 2), y, x, core)
    far_device = at(across_z, y, x, core)

    def remote(source, target, send, recv, device):
        return pltpu.make_async_remote_copy(
            src_ref=source, dst_ref=target, send_sem=send, recv_sem=recv,
            device_id=device, device_id_type=pl.DeviceIdType.MESH,
        )

    def arrived(ref, recv):
        remote(ref, ref, recv, recv, partner).wait_recv()

    def sent(ref, send):
        remote(ref, ref, send, send, partner).wait_send()

    loads = [
        pltpu.make_async_copy(source, target, load_sem.at[index])
        for index, (source, target) in enumerate(
            ((emb_hbm, emb_ref), (bucket_hbm, bucket_ref), (valid_hbm, valid_ref))
        )
    ]
    for load in loads:
        load.start()

    barrier = pltpu.get_barrier_semaphore()

    def greet(device):
        pl.semaphore_signal(barrier, inc=1, device_id=device, device_id_type=pl.DeviceIdType.MESH)

    greet(x_device)
    greet(y_device)
    greet(partner)

    @pl.when(inner)
    def _():
        greet(far_device)
        greet(end_device)

    @pl.when(jnp.logical_not(inner))
    def _():
        greet(next_device)

    for load in loads:
        load.wait()
    floats = emb_ref[...].astype(jnp.float32)
    inverse = lax.rsqrt(jnp.mean(floats * floats, axis=1, keepdims=True) + 1e-06)
    unit = (floats * inverse).astype(jnp.bfloat16)
    own = jnp.where(inner, 1, 0)
    keys[own, 0] = unit
    buckets = bucket_ref[...].astype(jnp.float32)
    meta = jnp.concatenate([buckets, jnp.where(valid_ref[...] > 0, buckets, -1.0)], axis=0)
    key_meta[own, 0] = meta
    spot_meta[0] = meta

    pl.semaphore_wait(barrier, jnp.where(inner, 5, 4))

    def column(row):
        return jnp.transpose(jnp.broadcast_to(row, (rows, rows)))

    def terms(chosen, buckets, block, metas, itself):
        cosine = lax.dot_general(
            chosen, block, (((1,), (1,)), ((), ())), preferred_element_type=jnp.float32
        ) * (1.0 / features)
        factors = []
        peaks = None
        sums = None
        for index, meta in enumerate(metas):
            usable = buckets == meta[1:2, :]
            if index == itself:
                line = lax.broadcasted_iota(jnp.int32, (rows, rows), 0)
                lane = lax.broadcasted_iota(jnp.int32, (rows, rows), 1)
                usable = usable & (line != lane)
            values = cosine[:, index * rows : (index + 1) * rows]
            best = jnp.where(usable, values, -1.0)
            factor = jnp.where(usable, jnp.exp(sharpness * (values - 1.0)), 0.0)
            factors.append(factor.astype(jnp.bfloat16))
            peaks = best if peaks is None else jnp.maximum(peaks, best)
            sums = factor if sums is None else sums + factor
        summed = jnp.dot(
            jnp.concatenate(factors, axis=1), block, preferred_element_type=jnp.float32
        )
        return peaks, sums, summed

    def stat_rows(peaks, sums):
        top = jnp.max(jnp.transpose(peaks), axis=0, keepdims=True)
        mass = jnp.sum(jnp.transpose(sums), axis=0, keepdims=True)
        return jnp.concatenate([top, mass], axis=0)

    def run(is_inner):
        me = 1 if is_inner else 0
        slots = 4 if is_inner else 3
        last = slots - 1
        own_rows = keys.at[me, 0]

        def z_copy(slot, target, part, device):
            ref = pl.ds(part * piece, piece)
            return remote(
                keys.at[slot, 0, ref], keys.at[target, 0, ref], z_send, z_recv.at[target, part],
                device,
            )

        def z_meta(slot, target, device):
            return remote(
                key_meta.at[slot, 0], key_meta.at[target, 0], zm_send, zm_recv.at[target], device
            )

        def c_copy(slot, part=None):
            ref = pl.ds(0, rows) if part is None else pl.ds(part * piece, piece)
            return remote(
                keys.at[slot, 0, ref], keys.at[slot, 1, ref], c_send, c_recv.at[slot], partner
            )

        def c_meta(slot):
            return remote(
                key_meta.at[slot, 0], key_meta.at[slot, 1], cm_send, cm_recv.at[slot], partner
            )

        def wait_partner(slot):
            arrived(key_meta.at[slot, 1], cm_recv.at[slot])
            arrived(keys.at[slot, 1], c_recv.at[slot])

        if is_inner:
            onward = {1: (2, far_device), 0: (3, far_device), 2: (1, end_device), 3: (2, end_device)}
        else:
            onward = {0: (0, next_device)}

        def take_meta(slot):
            arrived(key_meta.at[slot, 0], zm_recv.at[slot])
            if slot in onward:
                z_meta(slot, *onward[slot]).start()
            c_meta(slot).start()

        def take(slot, part):
            ref = keys.at[slot, 0, pl.ds(part * piece, piece)]
            arrived(ref, z_recv.at[slot, part])
            if slot in onward:
                target, device = onward[slot]
                z_copy(slot, target, part, device).start()
            c_copy(slot, part).start()

        def q_copy(source, spot, side, recv, device, send=1):
            return remote(
                source.at[halves[side]], plane.at[spot - 1, 0, halves[side]], q_send.at[send],
                q_recv.at[recv], device,
            )

        def q_arrived(spot, side, recv):
            arrived(plane.at[spot - 1, 0, halves[side]], q_recv.at[recv])

        def q_meta(source, spot, device):
            return remote(
                spot_meta.at[source], spot_meta.at[spot], qm_send, qm_recv.at[spot - 1], device
            )

        def q_meta_arrived(spot):
            arrived(spot_meta.at[spot], qm_recv.at[spot - 1])

        target, device = onward[me]
        z_meta(me, target, device).start()
        for part in range(PIECES):
            z_copy(me, target, part, device).start()
        q_meta(0, beside_x, x_device).start()
        q_meta(0, beside_y, y_device).start()
        q_copy(own_rows, beside_x, 0, 0, x_device, 0).start()
        q_copy(own_rows, beside_y, 1, 3, y_device, 0).start()
        c_meta(me).start()
        c_copy(me).start()
        query_col[0] = column(spot_meta[0, 0:1, :])
        sent(own_rows, q_send.at[0])
        q_copy(own_rows, beside_x, 1, 1, x_device).start()
        q_copy(own_rows, beside_y, 0, 2, y_device).start()

        def relay_q():
            q_meta_arrived(beside_x)
            q_meta(beside_x, corner, y_device).start()
            q_arrived(beside_x, 0, 0)
            q_copy(plane.at[beside_x - 1, 0], corner, 0, 4, y_device).start()
            q_meta_arrived(beside_y)
            q_arrived(beside_y, 1, 3)
            q_copy(plane.at[beside_y - 1, 0], corner, 1, 5, x_device).start()

        def pass_on(spot):
            if is_inner:
                remote(
                    plane.at[spot - 1, 0], plane.at[spot - 1, 1], f_send.at[0], f_recv.at[0], partner
                ).start()

        def finish_q(spot):
            if spot == beside_x:
                q_arrived(beside_x, 1, 1)
            elif spot == beside_y:
                q_arrived(beside_y, 0, 2)
            else:
                q_meta_arrived(corner)
                q_arrived(corner, 0, 4)
                q_arrived(corner, 1, 5)
                if is_inner:
                    remote(
                        spot_meta.at[1:SPOTS], plane_meta, f_send.at[1], f_recv.at[1], partner
                    ).start()
            pass_on(spot)
            query_col[spot] = column(spot_meta[spot, 0:1, :])

        def batch(spot, first, end):
            chosen = keys[me, 0] if spot == 0 else plane[spot - 1, 0]
            count = end - first
            itself = (me - first) * PAIR if spot == 0 and first <= me < end else None
            return terms(
                chosen,
                query_col[spot],
                keys[first:end].reshape(count * PAIR * rows, features),
                [key_meta[slot, side] for slot in range(first, end) for side in range(PAIR)],
                itself,
            )

        def early(spot):
            peak[spot], weight[spot], total[spot] = batch(spot, 0, last)

        if is_inner:
            take_meta(0)
            take_meta(2)
            for part in range(PIECES):
                take(0, part)
                take(2, part)
                if part == 0:
                    relay_q()
            wait_partner(me)
            wait_partner(0)
            finish_q(beside_x)
            finish_q(beside_y)
            wait_partner(2)
        else:
            relay_q()
            finish_q(beside_x)
            finish_q(beside_y)
            wait_partner(me)
            take_meta(1)
            for part in range(PIECES):
                take(1, part)
            wait_partner(1)
        if not is_inner:
            early(0)
        take_meta(last)
        todo = (beside_x, beside_y, corner)
        for part in range(PIECES):
            take(last, part)
            if part % (PIECES // 4) == 0 and part // (PIECES // 4) < len(todo):
                spot = todo[part // (PIECES // 4)]
                if spot == corner:
                    finish_q(corner)
                early(spot)
        if is_inner:
            early(0)

        def h_copies():
            return (
                remote(help_stat_out, help_stat_in, h_send.at[0], h_recv.at[0], end_device),
                remote(help_out, help_in, h_send.at[1], h_recv.at[1], end_device),
            )

        wait_partner(last)

        def p_copy(spot, side):
            return remote(
                part_out.at[spot - 1, halves[side]], part_in.at[spot - 1, halves[side]],
                p_send.at[1], p_recv, x_device if spot == beside_x else y_device,
            )

        def corner_copy(side):
            return remote(
                part_out.at[corner - 1, halves[side]], part_in.at[corner - 1, halves[side]],
                p_send.at[0], corner_recv.at[side], (x_device, y_device)[side],
            )

        def s_copy(spot, device, recv):
            return remote(stat_out.at[spot - 1], stat_in.at[spot - 1], s_send, recv, device)

        def final(spot):
            peaks, sums, summed = batch(spot, last, slots)
            return jnp.maximum(peak[spot], peaks), weight[spot] + sums, total[spot] + summed

        block = keys[last].reshape(PAIR * rows, features)
        metas = [key_meta[last, side] for side in range(PAIR)]
        others = plane[:, 0].reshape((SPOTS - 1) * rows, features)
        columns = query_col[1:SPOTS].reshape((SPOTS - 1) * rows, rows)
        peaks, sums, summed = terms(others, columns, block, metas, None)
        stats = {}
        for spot in (corner, beside_x, beside_y):
            of = slice((spot - 1) * rows, spot * rows)
            whole = total[spot] + summed[of]
            if spot == corner:
                part_out[spot - 1] = whole.astype(jnp.bfloat16)
                corner_copy(0).start()
                corner_copy(1).start()
            else:
                total[spot] = whole
            stats[spot] = stat_rows(jnp.maximum(peak[spot], peaks[of]), weight[spot] + sums[of])
            if spot != beside_y:
                stat_out[spot - 1] = stats[spot]
                s_copy(spot, x_device, sc_recv if spot == corner else s_recv).start()
        for spot, side in ((beside_x, 0), (beside_y, 1)):
            part_out[spot - 1, halves[side]] = total[spot, halves[side]].astype(jnp.bfloat16)
        peaks, sums, summed = final(0)
        own_stats = stat_rows(peaks, sums)
        total[0] = summed + keys[me, 0].astype(jnp.float32)

        if is_inner:
            for ref, index in ((plane_meta, 1), (plane.at[:, 1], 0)):
                arrived(ref, f_recv.at[index])
            chosen = keys[0, 0]
            buckets = column(key_meta[0, 0, 0:1, :])
            near = terms(
                chosen, buckets, keys[me].reshape(PAIR * rows, features),
                [key_meta[me, side] for side in range(PAIR)], None,
            )
            wider = terms(
                chosen, buckets, plane[...].reshape((SPOTS - 1) * PAIR * rows, features),
                [ref[spot] for spot in range(SPOTS - 1) for ref in (spot_meta.at[1:SPOTS], plane_meta)],
                None,
            )
            help_out[...] = (near[2] + wider[2]).astype(jnp.bfloat16)
            help_stat_out[...] = stat_rows(jnp.maximum(near[0], wider[0]), near[1] + wider[1])
            for copy in h_copies():
                copy.start()

        sent(part_out.at[corner - 1], p_send.at[0])
        for spot, side in ((beside_x, 0), (beside_y, 1)):
            p_copy(spot, side).start()
        arrived(stat_in.at[corner - 1], sc_recv)
        stat_out[beside_y - 1] = jnp.concatenate(
            [
                jnp.maximum(stats[beside_y][0:1], stat_in[corner - 1, 0:1]),
                stats[beside_y][1:2] + stat_in[corner - 1, 1:2],
            ],
            axis=0,
        )
        s_copy(beside_y, y_device, s_recv).start()
        for spot, side in ((beside_x, 1), (beside_y, 0)):
            arrived(part_in.at[corner - 1, halves[side]], corner_recv.at[side])
            part_out[spot - 1, halves[side]] = (
                total[spot, halves[side]] + part_in[corner - 1, halves[side]].astype(jnp.float32)
            ).astype(jnp.bfloat16)
            p_copy(spot, side).start()

        top, mass = own_stats[0:1], own_stats[1:2]
        if not is_inner:
            for copy in h_copies():
                copy.wait_recv()
            top = jnp.maximum(top, help_stat_in[0:1])
            mass = mass + help_stat_in[1:2]
            total[0] += help_in[...].astype(jnp.float32)
        arrived(stat_in.at[0 : corner - 1], s_recv)
        for spot in (beside_x, beside_y):
            top = jnp.maximum(top, stat_in[spot - 1, 0:1])
            mass = mass + stat_in[spot - 1, 1:2]
        best_ref[...] = top
        below = column(1.0 + mass)[:, 0:1]
        arrived(part_in.at[0 : corner - 1], p_recv)
        result = total[0]
        for spot in (beside_x, beside_y):
            result = result + part_in[spot - 1].astype(jnp.float32)
        mean_ref[...] = (result / below).astype(jnp.bfloat16)

        blocks = keys.at[0:slots, 0]
        metas = key_meta.at[0:slots, 0]
        sent(blocks if is_inner else keys.at[0, 0], z_send)
        sent(metas if is_inner else key_meta.at[0, 0], zm_send)
        sent(blocks, c_send)
        sent(metas, cm_send)
        sent(plane.at[0 : corner - 1, 0], q_send.at[1])
        sent(spot_meta.at[1:SPOTS], qm_send)
        sent(part_out.at[0 : corner - 1], p_send.at[1])
        sent(stat_out, s_send)
        if is_inner:
            sent(plane.at[:, 0], f_send.at[0])
            sent(plane_meta, f_send.at[1])
            for copy in h_copies():
                copy.wait_send()

    @pl.when(inner)
    def _():
        run(True)

    @pl.when(jnp.logical_not(inner))
    def _():
        run(False)


def finish_kernel(mean_ref, best_ref, mean_out, best_out, line, sem):
    line[...] = best_ref[0].astype(jnp.bfloat16)
    copies = [
        pltpu.make_async_copy(mean_ref, mean_out, sem.at[0]),
        pltpu.make_async_copy(line, best_out, sem.at[1]),
    ]
    for copy in copies:
        copy.start()
    for copy in copies:
        copy.wait()


def finish(mean, best):
    rows, features = mean.shape
    vmem = pl.BlockSpec(memory_space=pltpu.VMEM)
    hbm = pl.BlockSpec(memory_space=pltpu.HBM)
    return pl.pallas_call(
        finish_kernel,
        out_shape=(
            jax.ShapeDtypeStruct((rows, features), jnp.bfloat16),
            jax.ShapeDtypeStruct((rows,), jnp.bfloat16),
        ),
        in_specs=[vmem, vmem],
        out_specs=(hbm, hbm),
        scratch_shapes=[pltpu.VMEM((rows,), jnp.bfloat16), pltpu.SemaphoreType.DMA((2,))],
        compiler_params=pltpu.CompilerParams(vmem_limit_bytes=4_000_000),
    )(mean, best)


def dense(embeddings, bucket_ids, valid_rows):
    rows, features = embeddings.shape
    dma = pltpu.SemaphoreType.DMA
    vmem = pl.BlockSpec(memory_space=pltpu.VMEM)
    others = SPOTS - 1

    def bf16(*shape):
        return pltpu.VMEM((*shape, rows, features), jnp.bfloat16)

    def f32(*shape):
        return pltpu.VMEM(shape, jnp.float32)

    mean, best = pl.pallas_call(
        dense_kernel,
        out_shape=(
            jax.ShapeDtypeStruct((rows, features), jnp.bfloat16),
            jax.ShapeDtypeStruct((1, rows), jnp.float32),
        ),
        in_specs=[pl.BlockSpec(memory_space=pltpu.HBM)] * 3,
        out_specs=(vmem, vmem),
        scratch_shapes=[
            bf16(), pltpu.VMEM((1, rows), jnp.int32), pltpu.VMEM((1, rows), jnp.int32),
            bf16(PLANES, PAIR), f32(PLANES, PAIR, 2, rows), bf16(others, PAIR),
            f32(SPOTS, 2, rows), f32(others, 2, rows), f32(SPOTS, rows, rows),
            f32(SPOTS, rows, features), f32(SPOTS, rows, rows), f32(SPOTS, rows, rows),
            bf16(others), bf16(others), f32(others, 2, rows), f32(others, 2, rows),
            bf16(), bf16(), f32(2, rows), f32(2, rows),
            dma((3,)), dma, dma((PLANES, PIECES)), dma, dma((PLANES,)),
            dma, dma((PLANES,)), dma, dma((PLANES,)),
            dma((2,)), dma((6,)), dma, dma((others,)), dma((2,)), dma((2,)),
            dma((2,)), dma((2,)), dma, dma, dma, dma, dma((2,)), dma((2,)),
        ],
        compiler_params=pltpu.CompilerParams(
            collective_id=0, has_side_effects=True, vmem_limit_bytes=GRANT
        ),
    )(
        *[
            pltpu.with_memory_space_constraint(value, pltpu.HBM)
            for value in (embeddings, bucket_ids.reshape(1, rows), valid_rows.reshape(1, rows))
        ]
    )
    return finish(mean, best)


def on_device(embeddings, bucket_ids, slot_ids, valid_rows):
    rows = embeddings.shape[0]
    groups = lax.axis_size("wide")
    blocks = lax.axis_size("blk")
    bucket_work = blocks * (2 * rows) ** 2
    dense_work = groups * blocks * rows**2
    fits = groups % PAIR == 0 and groups == PLANES * PAIR and blocks == PAIR * PAIR and rows == 128
    if fits and dense_work <= 4 * bucket_work:
        return dense(embeddings, bucket_ids, valid_rows)
    return by_bucket(embeddings, bucket_ids, slot_ids, valid_rows)


def solution(mesh):
    in_specs = (
        P(("wide", "blk"), None),
        P(("wide", "blk")),
        P(("wide", "blk")),
        P(("wide", "blk")),
    )
    out_specs = (P(("wide", "blk"), None), P(("wide", "blk")))
    return jax.shard_map(
        on_device, mesh=mesh, in_specs=in_specs, out_specs=out_specs, check_vma=False
    )
```

```python
import functools

import jax
import jax.numpy as jnp
from jax import lax
from jax.experimental import pallas as pl
from jax.experimental.pallas import tpu as pltpu
from jax.sharding import PartitionSpec as P

sharpness = 10.0


def from_behind(value, axis, steps):
    count = lax.axis_size(axis)
    pairs = [(source, (source + steps) % count) for source in range(count)]
    return lax.ppermute(value, axis, pairs)


def unit_rows(embeddings):
    float_rows = embeddings.astype(jnp.float32)
    inverse_norm = lax.rsqrt(jnp.mean(float_rows * float_rows, axis=1, keepdims=True) + 1e-06)
    return (float_rows * inverse_norm).astype(jnp.bfloat16)


def bucket_stats(queries, query_pos, key_rows, key_flags, key_pos):
    feature_count = queries.shape[1]
    cosine = (
        lax.dot_general(
            queries, key_rows, (((1,), (1,)), ((), ())), preferred_element_type=jnp.float32
        )
        / feature_count
    )
    usable = (key_flags[None, :] > 0) & (query_pos[:, None] != key_pos[None, :])
    best_cos = jnp.max(jnp.where(usable, cosine, -1.0), axis=1)
    weights = jnp.where(usable, jnp.exp(sharpness * (cosine - 1.0)), 0.0)
    weight_total = jnp.sum(weights, axis=1)
    summed = jnp.dot(weights.astype(jnp.bfloat16), key_rows, preferred_element_type=jnp.float32)
    return (best_cos, weight_total, summed)


def by_bucket(embeddings, bucket_ids, slot_ids, valid_rows):
    unit_vectors = unit_rows(embeddings)
    row_count, feature_count = unit_vectors.shape
    groups = lax.axis_size("wide")
    blocks = lax.axis_size("blk")
    slot_count = 2 * row_count // groups
    block_rows = groups * slot_count
    cell_ids = bucket_ids * slot_count + slot_ids
    outgoing = jnp.zeros((block_rows, feature_count), jnp.bfloat16).at[cell_ids].set(unit_vectors)
    flag_rows = (
        jnp.zeros((block_rows,), jnp.bfloat16).at[cell_ids].set(valid_rows.astype(jnp.bfloat16))
    )
    arrived, arrived_flags = (
        lax.all_to_all(
            outgoing.reshape(groups, slot_count, feature_count),
            "wide",
            split_axis=0,
            concat_axis=0,
            tiled=True,
        ),
        lax.all_to_all(
            flag_rows.reshape(groups, slot_count), "wide", split_axis=0, concat_axis=0, tiled=True
        ),
    )
    queries = arrived.reshape(block_rows, feature_count)
    query_flags = arrived_flags.reshape(block_rows)
    my_block = lax.axis_index("blk")
    query_pos = my_block * block_rows + jnp.arange(block_rows, dtype=jnp.int32)

    def absorb(running, key_rows, key_flags, key_start):
        key_pos = key_start + jnp.arange(key_rows.shape[0], dtype=jnp.int32)
        best_cos, weight_total, summed = bucket_stats(
            queries, query_pos, key_rows, key_flags, key_pos
        )
        return (jnp.maximum(running[0], best_cos), running[1] + weight_total, running[2] + summed)

    initial = (
        jnp.full((block_rows,), -1.0, jnp.float32),
        jnp.zeros((block_rows,), jnp.float32),
        jnp.zeros((block_rows, feature_count), jnp.float32),
    )
    key_rows, key_flags = (queries, query_flags)
    running = absorb(initial, key_rows, key_flags, my_block * block_rows)
    for turn_index in range(1, blocks):
        key_rows, key_flags = from_behind((key_rows, key_flags), "blk", 1)
        running = absorb(
            running, key_rows, key_flags, (my_block - turn_index) % blocks * block_rows
        )
    best_cos, weight_total, summed = running
    mean_rows = ((queries.astype(jnp.float32) + summed) / (1.0 + weight_total[:, None])).astype(
        jnp.bfloat16
    )
    back_mean, back_best = (
        lax.all_to_all(
            mean_rows.reshape(groups, slot_count, feature_count),
            "wide",
            split_axis=0,
            concat_axis=0,
            tiled=True,
        ),
        lax.all_to_all(
            best_cos.astype(jnp.bfloat16).reshape(groups, slot_count),
            "wide",
            split_axis=0,
            concat_axis=0,
            tiled=True,
        ),
    )
    neighbour_mean = back_mean.reshape(block_rows, feature_count)[cell_ids]
    max_cosine = back_best.reshape(block_rows)[cell_ids]
    return (neighbour_mean, max_cosine)


PAIR = 2
PLANES = 4
SPOTS = PAIR * PAIR
PIECES = 4
GRANT = 56_240_000


def dense_kernel(
    emb_hbm, bucket_hbm, valid_hbm, mean_ref, best_ref,
    emb_ref, bucket_ref, valid_ref,
    keys, key_meta, plane, spot_meta, plane_meta, query_col, total, peak, weight,
    part_out, part_in, stat_out, stat_in, help_out, help_in, help_stat_out, help_stat_in,
    load_sem, z_send, z_recv, zm_send, zm_recv, c_send, c_recv, cm_send, cm_recv,
    q_send, q_recv, qm_send, qm_recv, f_send, f_recv,
    p_send, corner_recv, p_recv, s_send, sc_recv, s_recv, h_send, h_recv,
):
    rows, features = emb_ref.shape
    piece = rows // PIECES
    half = rows // 2
    halves = (pl.ds(0, half), pl.ds(half, half))
    wide, blk = lax.axis_index("wide"), lax.axis_index("blk")
    z, y = lax.div(wide, PAIR), lax.rem(wide, PAIR)
    x, core = lax.div(blk, PAIR), lax.rem(blk, PAIR)
    beside_x, beside_y, corner = 1, 2, 3

    def at(z_at, y_at, x_at, core_at):
        return (z_at * PAIR + y_at, x_at * PAIR + core_at)

    partner = at(z, y, x, 1 - core)
    x_device = at(z, y, 1 - x, core)
    y_device = at(z, 1 - y, x, core)
    inner = (z > 0) & (z < PLANES - 1)
    lower = z < PLANES // 2
    across_z = PLANES - 1 - z
    end_device = at(jnp.where(lower, 0, PLANES - 1), y, x, core)
    next_device = at(jnp.where(lower, 1, PLANES - 2), y, x, core)
    far_device = at(across_z, y, x, core)
    first_device = at(0, y, x, core)
    top_device = at(PLANES - 1, y, x, core)

    def remote(source, target, send, recv, device):
        return pltpu.make_async_remote_copy(
            src_ref=source, dst_ref=target, send_sem=send, recv_sem=recv,
            device_id=device, device_id_type=pl.DeviceIdType.MESH,
        )

    def arrived(ref, recv):
        remote(ref, ref, recv, recv, partner).wait_recv()

    def sent(ref, send):
        remote(ref, ref, send, send, partner).wait_send()

    loads = [
        pltpu.make_async_copy(source, target, load_sem.at[index])
        for index, (source, target) in enumerate(
            ((emb_hbm, emb_ref), (bucket_hbm, bucket_ref), (valid_hbm, valid_ref))
        )
    ]
    for load in loads:
        load.start()

    barrier = pltpu.get_barrier_semaphore()

    def greet(device):
        pl.semaphore_signal(barrier, inc=1, device_id=device, device_id_type=pl.DeviceIdType.MESH)

    greet(x_device)
    greet(y_device)
    greet(partner)

    @pl.when(inner)
    def _():
        greet(far_device)
        greet(end_device)

    @pl.when(jnp.logical_not(inner))
    def _():
        greet(next_device)

    @pl.when(z == 0)
    def _():
        greet(top_device)

    for load in loads:
        load.wait()
    floats = emb_ref[...].astype(jnp.float32)
    inverse = lax.rsqrt(jnp.mean(floats * floats, axis=1, keepdims=True) + 1e-06)
    unit = (floats * inverse).astype(jnp.bfloat16)
    own = jnp.where(inner, 1, 0)
    keys[own, 0] = unit
    buckets = bucket_ref[...].astype(jnp.float32)
    meta = jnp.concatenate([buckets, jnp.where(valid_ref[...] > 0, buckets, -1.0)], axis=0)
    key_meta[own, 0] = meta
    spot_meta[0] = meta

    pl.semaphore_wait(barrier, jnp.where(z > 0, 5, 4))

    def column(row):
        return jnp.transpose(jnp.broadcast_to(row, (rows, rows)))

    def terms(chosen, buckets, block, metas, itself):
        cosine = lax.dot_general(
            chosen, block, (((1,), (1,)), ((), ())), preferred_element_type=jnp.float32
        ) * (1.0 / features)
        factors = []
        peaks = None
        sums = None
        for index, meta in enumerate(metas):
            usable = buckets == meta[1:2, :]
            if index == itself:
                line = lax.broadcasted_iota(jnp.int32, (rows, rows), 0)
                lane = lax.broadcasted_iota(jnp.int32, (rows, rows), 1)
                usable = usable & (line != lane)
            values = cosine[:, index * rows : (index + 1) * rows]
            best = jnp.where(usable, values, -1.0)
            factor = jnp.where(usable, jnp.exp(sharpness * (values - 1.0)), 0.0)
            factors.append(factor.astype(jnp.bfloat16))
            peaks = best if peaks is None else jnp.maximum(peaks, best)
            sums = factor if sums is None else sums + factor
        summed = jnp.dot(
            jnp.concatenate(factors, axis=1), block, preferred_element_type=jnp.float32
        )
        return peaks, sums, summed

    def stat_rows(peaks, sums):
        top = jnp.max(jnp.transpose(peaks), axis=0, keepdims=True)
        mass = jnp.sum(jnp.transpose(sums), axis=0, keepdims=True)
        return jnp.concatenate([top, mass], axis=0)

    def run(place):
        is_inner = 0 < place < PLANES - 1
        me = 1 if is_inner else 0
        slots = (2, 4, 4, 3)[place]
        last = slots - 1
        own_rows = keys.at[me, 0]

        def z_copy(slot, target, part, device):
            ref = pl.ds(part * piece, piece)
            return remote(
                keys.at[slot, 0, ref], keys.at[target, 0, ref], z_send, z_recv.at[target, part],
                device,
            )

        def z_meta(slot, target, device):
            return remote(
                key_meta.at[slot, 0], key_meta.at[target, 0], zm_send, zm_recv.at[target], device
            )

        def c_copy(slot, part=None):
            ref = pl.ds(0, rows) if part is None else pl.ds(part * piece, piece)
            return remote(
                keys.at[slot, 0, ref], keys.at[slot, 1, ref], c_send, c_recv.at[slot], partner
            )

        def c_meta(slot):
            return remote(
                key_meta.at[slot, 0], key_meta.at[slot, 1], cm_send, cm_recv.at[slot], partner
            )

        def wait_partner(slot):
            arrived(key_meta.at[slot, 1], cm_recv.at[slot])
            arrived(keys.at[slot, 1], c_recv.at[slot])

        if is_inner:
            onward = {1: (2, far_device), 0: (3, far_device), 2: (1, end_device)}
            if place > 1:
                onward[3] = (2, end_device)
        else:
            onward = {0: (0, next_device)}

        def take_meta(slot):
            arrived(key_meta.at[slot, 0], zm_recv.at[slot])
            if slot in onward:
                z_meta(slot, *onward[slot]).start()
            c_meta(slot).start()

        def take(slot, part):
            ref = keys.at[slot, 0, pl.ds(part * piece, piece)]
            arrived(ref, z_recv.at[slot, part])
            if slot in onward:
                target, device = onward[slot]
                z_copy(slot, target, part, device).start()
            c_copy(slot, part).start()

        def q_copy(source, spot, side, recv, device, send=1):
            return remote(
                source.at[halves[side]], plane.at[spot - 1, 0, halves[side]], q_send.at[send],
                q_recv.at[recv], device,
            )

        def q_arrived(spot, side, recv):
            arrived(plane.at[spot - 1, 0, halves[side]], q_recv.at[recv])

        def q_meta(source, spot, device):
            return remote(
                spot_meta.at[source], spot_meta.at[spot], qm_send, qm_recv.at[spot - 1], device
            )

        def q_meta_arrived(spot):
            arrived(spot_meta.at[spot], qm_recv.at[spot - 1])

        target, device = onward[me]
        z_meta(me, target, device).start()
        for part in range(PIECES):
            z_copy(me, target, part, device).start()
        q_meta(0, beside_x, x_device).start()
        q_meta(0, beside_y, y_device).start()
        q_copy(own_rows, beside_x, 0, 0, x_device, 0).start()
        q_copy(own_rows, beside_y, 1, 3, y_device, 0).start()
        c_meta(me).start()
        c_copy(me).start()
        query_col[0] = column(spot_meta[0, 0:1, :])
        sent(own_rows, q_send.at[0])
        q_copy(own_rows, beside_x, 1, 1, x_device).start()
        q_copy(own_rows, beside_y, 0, 2, y_device).start()

        def relay_q():
            q_meta_arrived(beside_x)
            q_meta(beside_x, corner, y_device).start()
            q_arrived(beside_x, 0, 0)
            q_copy(plane.at[beside_x - 1, 0], corner, 0, 4, y_device).start()
            q_meta_arrived(beside_y)
            q_arrived(beside_y, 1, 3)
            q_copy(plane.at[beside_y - 1, 0], corner, 1, 5, x_device).start()

        def pass_on(spot):
            if place > 0:
                remote(
                    plane.at[spot - 1, 0], plane.at[spot - 1, 1], f_send.at[0], f_recv.at[0], partner
                ).start()

        def finish_q(spot):
            if spot == beside_x:
                q_arrived(beside_x, 1, 1)
            elif spot == beside_y:
                q_arrived(beside_y, 0, 2)
            else:
                q_meta_arrived(corner)
                q_arrived(corner, 0, 4)
                q_arrived(corner, 1, 5)
                if place > 0:
                    remote(
                        spot_meta.at[1:SPOTS], plane_meta, f_send.at[1], f_recv.at[1], partner
                    ).start()
            pass_on(spot)
            query_col[spot] = column(spot_meta[spot, 0:1, :])

        def batch(spot, first, end):
            chosen = keys[me, 0] if spot == 0 else plane[spot - 1, 0]
            count = end - first
            itself = (me - first) * PAIR if spot == 0 and first <= me < end else None
            return terms(
                chosen,
                query_col[spot],
                keys[first:end].reshape(count * PAIR * rows, features),
                [key_meta[slot, side] for slot in range(first, end) for side in range(PAIR)],
                itself,
            )

        def early(spot):
            peak[spot], weight[spot], total[spot] = batch(spot, 0, last)

        def h_copies(giver, taker):
            return (
                remote(help_stat_out, help_stat_in.at[giver], h_send.at[0], h_recv.at[giver, 0], taker),
                remote(help_out, help_in.at[giver], h_send.at[1], h_recv.at[giver, 1], taker),
            )

        if place > 0:
            helped = h_copies(0, end_device) if is_inner else h_copies(1, first_device)

        def assist():
            slot = 0 if is_inner else last
            for ref, index in ((plane_meta, 1), (plane.at[:, 1], 0)):
                arrived(ref, f_recv.at[index])
            chosen = keys[slot, 0]
            buckets = column(key_meta[slot, 0, 0:1, :])
            near = terms(
                chosen, buckets, keys[me].reshape(PAIR * rows, features),
                [key_meta[me, side] for side in range(PAIR)], None,
            )
            wider = terms(
                chosen, buckets, plane[...].reshape((SPOTS - 1) * PAIR * rows, features),
                [ref[spot] for spot in range(SPOTS - 1) for ref in (spot_meta.at[1:SPOTS], plane_meta)],
                None,
            )
            help_out[...] = (near[2] + wider[2]).astype(jnp.bfloat16)
            help_stat_out[...] = stat_rows(jnp.maximum(near[0], wider[0]), near[1] + wider[1])
            for copy in helped:
                copy.start()

        def take_all(*order):
            for slot, part in order:
                take(slot, part)

        if place == 0:
            relay_q()
            finish_q(beside_x)
            finish_q(beside_y)
            wait_partner(0)
            for spot in (0, beside_x, beside_y):
                early(spot)
            take_meta(1)
            take(1, 0)
            finish_q(corner)
            early(corner)
            take_all((1, 1), (1, 2), (1, 3))
        elif place == 1:
            take_meta(0)
            take(0, 0)
            take_meta(2)
            take_all((0, 1), (2, 0))
            relay_q()
            take_all((0, 2), (2, 1), (0, 3), (2, 2), (2, 3))
            finish_q(beside_x)
            finish_q(beside_y)
            for slot in range(last):
                wait_partner(slot)
            early(0)
            take_meta(3)
            take(3, 0)
            finish_q(corner)
            assist()
            take(3, 1)
            early(beside_x)
            take(3, 2)
            early(beside_y)
            take(3, 3)
            early(corner)
        elif place == 2:
            take_meta(2)
            take(2, 0)
            take_meta(0)
            take_all((2, 1), (0, 0), (2, 2))
            relay_q()
            take_all((0, 1), (2, 3))
            take_meta(3)
            take_all((3, 0), (0, 2), (3, 1), (0, 3), (3, 2))
            finish_q(beside_x)
            finish_q(beside_y)
            for slot in range(last):
                wait_partner(slot)
            early(0)
            take(3, 3)
            early(beside_x)
            early(beside_y)
            finish_q(corner)
            early(corner)
        else:
            relay_q()
            finish_q(beside_x)
            finish_q(beside_y)
            wait_partner(0)
            take_meta(1)
            take_all((1, 0), (1, 1), (1, 2), (1, 3))
            wait_partner(1)
            early(0)
            early(beside_x)
            take_meta(2)
            take(2, 0)
            early(beside_y)
            take(2, 1)
            finish_q(corner)
            early(corner)
            take_all((2, 2), (2, 3))
            assist()

        wait_partner(last)

        def p_copy(spot, side):
            return remote(
                part_out.at[spot - 1, halves[side]], part_in.at[spot - 1, halves[side]],
                p_send.at[1], p_recv, x_device if spot == beside_x else y_device,
            )

        def corner_copy(side):
            return remote(
                part_out.at[corner - 1, halves[side]], part_in.at[corner - 1, halves[side]],
                p_send.at[0], corner_recv.at[side], (x_device, y_device)[side],
            )

        def s_copy(spot, device, recv):
            return remote(stat_out.at[spot - 1], stat_in.at[spot - 1], s_send, recv, device)

        def final(spot):
            peaks, sums, summed = batch(spot, last, slots)
            return jnp.maximum(peak[spot], peaks), weight[spot] + sums, total[spot] + summed

        block = keys[last].reshape(PAIR * rows, features)
        metas = [key_meta[last, side] for side in range(PAIR)]
        others = plane[:, 0].reshape((SPOTS - 1) * rows, features)
        columns = query_col[1:SPOTS].reshape((SPOTS - 1) * rows, rows)
        peaks, sums, summed = terms(others, columns, block, metas, None)
        stats = {}
        for spot in (corner, beside_x, beside_y):
            of = slice((spot - 1) * rows, spot * rows)
            whole = total[spot] + summed[of]
            if spot == corner:
                part_out[spot - 1] = whole.astype(jnp.bfloat16)
                corner_copy(0).start()
                corner_copy(1).start()
            else:
                total[spot] = whole
            stats[spot] = stat_rows(jnp.maximum(peak[spot], peaks[of]), weight[spot] + sums[of])
            if spot != beside_y:
                stat_out[spot - 1] = stats[spot]
                s_copy(spot, x_device, sc_recv if spot == corner else s_recv).start()
        for spot, side in ((beside_x, 0), (beside_y, 1)):
            part_out[spot - 1, halves[side]] = total[spot, halves[side]].astype(jnp.bfloat16)
        peaks, sums, summed = final(0)
        own_stats = stat_rows(peaks, sums)
        total[0] = summed + keys[me, 0].astype(jnp.float32)

        if place == 2:
            assist()
        sent(part_out.at[corner - 1], p_send.at[0])
        for spot, side in ((beside_x, 0), (beside_y, 1)):
            p_copy(spot, side).start()
        arrived(stat_in.at[corner - 1], sc_recv)
        stat_out[beside_y - 1] = jnp.concatenate(
            [
                jnp.maximum(stats[beside_y][0:1], stat_in[corner - 1, 0:1]),
                stats[beside_y][1:2] + stat_in[corner - 1, 1:2],
            ],
            axis=0,
        )
        s_copy(beside_y, y_device, s_recv).start()
        for spot, side in ((beside_x, 1), (beside_y, 0)):
            arrived(part_in.at[corner - 1, halves[side]], corner_recv.at[side])
            part_out[spot - 1, halves[side]] = (
                total[spot, halves[side]] + part_in[corner - 1, halves[side]].astype(jnp.float32)
            ).astype(jnp.bfloat16)
            p_copy(spot, side).start()

        top, mass = own_stats[0:1], own_stats[1:2]
        for giver in {0: (0, 1), 3: (0,)}.get(place, ()):
            for copy in h_copies(giver, partner):
                copy.wait_recv()
            top = jnp.maximum(top, help_stat_in[giver, 0:1])
            mass = mass + help_stat_in[giver, 1:2]
            total[0] += help_in[giver].astype(jnp.float32)
        arrived(stat_in.at[0 : corner - 1], s_recv)
        for spot in (beside_x, beside_y):
            top = jnp.maximum(top, stat_in[spot - 1, 0:1])
            mass = mass + stat_in[spot - 1, 1:2]
        best_ref[...] = top
        below = column(1.0 + mass)[:, 0:1]
        arrived(part_in.at[0 : corner - 1], p_recv)
        result = total[0]
        for spot in (beside_x, beside_y):
            result = result + part_in[spot - 1].astype(jnp.float32)
        mean_ref[...] = (result / below).astype(jnp.bfloat16)

        blocks = keys.at[0:slots, 0]
        metas = key_meta.at[0:slots, 0]
        sent(keys.at[0 : len(onward), 0], z_send)
        sent(key_meta.at[0 : len(onward), 0], zm_send)
        sent(blocks, c_send)
        sent(metas, cm_send)
        sent(plane.at[0 : corner - 1, 0], q_send.at[1])
        sent(spot_meta.at[1:SPOTS], qm_send)
        sent(part_out.at[0 : corner - 1], p_send.at[1])
        sent(stat_out, s_send)
        if place > 0:
            sent(plane.at[:, 0], f_send.at[0])
            sent(plane_meta, f_send.at[1])
            for copy in helped:
                copy.wait_send()

    for place in range(PLANES):
        pl.when(z == place)(functools.partial(run, place))


def finish_kernel(mean_ref, best_ref, mean_out, best_out, line, sem):
    line[...] = best_ref[0].astype(jnp.bfloat16)
    copies = [
        pltpu.make_async_copy(mean_ref, mean_out, sem.at[0]),
        pltpu.make_async_copy(line, best_out, sem.at[1]),
    ]
    for copy in copies:
        copy.start()
    for copy in copies:
        copy.wait()


def finish(mean, best):
    rows, features = mean.shape
    vmem = pl.BlockSpec(memory_space=pltpu.VMEM)
    hbm = pl.BlockSpec(memory_space=pltpu.HBM)
    return pl.pallas_call(
        finish_kernel,
        out_shape=(
            jax.ShapeDtypeStruct((rows, features), jnp.bfloat16),
            jax.ShapeDtypeStruct((rows,), jnp.bfloat16),
        ),
        in_specs=[vmem, vmem],
        out_specs=(hbm, hbm),
        scratch_shapes=[pltpu.VMEM((rows,), jnp.bfloat16), pltpu.SemaphoreType.DMA((2,))],
        compiler_params=pltpu.CompilerParams(vmem_limit_bytes=4_000_000),
    )(mean, best)


def dense(embeddings, bucket_ids, valid_rows):
    rows, features = embeddings.shape
    dma = pltpu.SemaphoreType.DMA
    vmem = pl.BlockSpec(memory_space=pltpu.VMEM)
    others = SPOTS - 1

    def bf16(*shape):
        return pltpu.VMEM((*shape, rows, features), jnp.bfloat16)

    def f32(*shape):
        return pltpu.VMEM(shape, jnp.float32)

    mean, best = pl.pallas_call(
        dense_kernel,
        out_shape=(
            jax.ShapeDtypeStruct((rows, features), jnp.bfloat16),
            jax.ShapeDtypeStruct((1, rows), jnp.float32),
        ),
        in_specs=[pl.BlockSpec(memory_space=pltpu.HBM)] * 3,
        out_specs=(vmem, vmem),
        scratch_shapes=[
            bf16(), pltpu.VMEM((1, rows), jnp.int32), pltpu.VMEM((1, rows), jnp.int32),
            bf16(PLANES, PAIR), f32(PLANES, PAIR, 2, rows), bf16(others, PAIR),
            f32(SPOTS, 2, rows), f32(others, 2, rows), f32(SPOTS, rows, rows),
            f32(SPOTS, rows, features), f32(SPOTS, rows, rows), f32(SPOTS, rows, rows),
            bf16(others), bf16(others), f32(others, 2, rows), f32(others, 2, rows),
            bf16(), bf16(2), f32(2, rows), f32(2, 2, rows),
            dma((3,)), dma, dma((PLANES, PIECES)), dma, dma((PLANES,)),
            dma, dma((PLANES,)), dma, dma((PLANES,)),
            dma((2,)), dma((6,)), dma, dma((others,)), dma((2,)), dma((2,)),
            dma((2,)), dma((2,)), dma, dma, dma, dma, dma((2,)), dma((2, 2)),
        ],
        compiler_params=pltpu.CompilerParams(
            collective_id=0, has_side_effects=True, vmem_limit_bytes=GRANT
        ),
    )(
        *[
            pltpu.with_memory_space_constraint(value, pltpu.HBM)
            for value in (embeddings, bucket_ids.reshape(1, rows), valid_rows.reshape(1, rows))
        ]
    )
    return finish(mean, best)


def on_device(embeddings, bucket_ids, slot_ids, valid_rows):
    rows = embeddings.shape[0]
    groups = lax.axis_size("wide")
    blocks = lax.axis_size("blk")
    bucket_work = blocks * (2 * rows) ** 2
    dense_work = groups * blocks * rows**2
    fits = groups % PAIR == 0 and groups == PLANES * PAIR and blocks == PAIR * PAIR and rows == 128
    if fits and dense_work <= 4 * bucket_work:
        return dense(embeddings, bucket_ids, valid_rows)
    return by_bucket(embeddings, bucket_ids, slot_ids, valid_rows)


def solution(mesh):
    in_specs = (
        P(("wide", "blk"), None),
        P(("wide", "blk")),
        P(("wide", "blk")),
        P(("wide", "blk")),
    )
    out_specs = (P(("wide", "blk"), None), P(("wide", "blk")))
    return jax.shard_map(
        on_device, mesh=mesh, in_specs=in_specs, out_specs=out_specs, check_vma=False
    )
```

```python
import functools

import jax
import jax.numpy as jnp
from jax import lax
from jax.experimental import pallas as pl
from jax.experimental.pallas import tpu as pltpu
from jax.sharding import PartitionSpec as P

sharpness = 10.0


def from_behind(value, axis, steps):
    count = lax.axis_size(axis)
    pairs = [(source, (source + steps) % count) for source in range(count)]
    return lax.ppermute(value, axis, pairs)


def unit_rows(embeddings):
    float_rows = embeddings.astype(jnp.float32)
    inverse_norm = lax.rsqrt(jnp.mean(float_rows * float_rows, axis=1, keepdims=True) + 1e-06)
    return (float_rows * inverse_norm).astype(jnp.bfloat16)


def bucket_stats(queries, query_pos, key_rows, key_flags, key_pos):
    feature_count = queries.shape[1]
    cosine = (
        lax.dot_general(
            queries, key_rows, (((1,), (1,)), ((), ())), preferred_element_type=jnp.float32
        )
        / feature_count
    )
    usable = (key_flags[None, :] > 0) & (query_pos[:, None] != key_pos[None, :])
    best_cos = jnp.max(jnp.where(usable, cosine, -1.0), axis=1)
    weights = jnp.where(usable, jnp.exp(sharpness * (cosine - 1.0)), 0.0)
    weight_total = jnp.sum(weights, axis=1)
    summed = jnp.dot(weights.astype(jnp.bfloat16), key_rows, preferred_element_type=jnp.float32)
    return (best_cos, weight_total, summed)


def by_bucket(embeddings, bucket_ids, slot_ids, valid_rows):
    unit_vectors = unit_rows(embeddings)
    row_count, feature_count = unit_vectors.shape
    groups = lax.axis_size("wide")
    blocks = lax.axis_size("blk")
    slot_count = 2 * row_count // groups
    block_rows = groups * slot_count
    cell_ids = bucket_ids * slot_count + slot_ids
    outgoing = jnp.zeros((block_rows, feature_count), jnp.bfloat16).at[cell_ids].set(unit_vectors)
    flag_rows = (
        jnp.zeros((block_rows,), jnp.bfloat16).at[cell_ids].set(valid_rows.astype(jnp.bfloat16))
    )
    arrived, arrived_flags = (
        lax.all_to_all(
            outgoing.reshape(groups, slot_count, feature_count),
            "wide",
            split_axis=0,
            concat_axis=0,
            tiled=True,
        ),
        lax.all_to_all(
            flag_rows.reshape(groups, slot_count), "wide", split_axis=0, concat_axis=0, tiled=True
        ),
    )
    queries = arrived.reshape(block_rows, feature_count)
    query_flags = arrived_flags.reshape(block_rows)
    my_block = lax.axis_index("blk")
    query_pos = my_block * block_rows + jnp.arange(block_rows, dtype=jnp.int32)

    def absorb(running, key_rows, key_flags, key_start):
        key_pos = key_start + jnp.arange(key_rows.shape[0], dtype=jnp.int32)
        best_cos, weight_total, summed = bucket_stats(
            queries, query_pos, key_rows, key_flags, key_pos
        )
        return (jnp.maximum(running[0], best_cos), running[1] + weight_total, running[2] + summed)

    initial = (
        jnp.full((block_rows,), -1.0, jnp.float32),
        jnp.zeros((block_rows,), jnp.float32),
        jnp.zeros((block_rows, feature_count), jnp.float32),
    )
    key_rows, key_flags = (queries, query_flags)
    running = absorb(initial, key_rows, key_flags, my_block * block_rows)
    for turn_index in range(1, blocks):
        key_rows, key_flags = from_behind((key_rows, key_flags), "blk", 1)
        running = absorb(
            running, key_rows, key_flags, (my_block - turn_index) % blocks * block_rows
        )
    best_cos, weight_total, summed = running
    mean_rows = ((queries.astype(jnp.float32) + summed) / (1.0 + weight_total[:, None])).astype(
        jnp.bfloat16
    )
    back_mean, back_best = (
        lax.all_to_all(
            mean_rows.reshape(groups, slot_count, feature_count),
            "wide",
            split_axis=0,
            concat_axis=0,
            tiled=True,
        ),
        lax.all_to_all(
            best_cos.astype(jnp.bfloat16).reshape(groups, slot_count),
            "wide",
            split_axis=0,
            concat_axis=0,
            tiled=True,
        ),
    )
    neighbour_mean = back_mean.reshape(block_rows, feature_count)[cell_ids]
    max_cosine = back_best.reshape(block_rows)[cell_ids]
    return (neighbour_mean, max_cosine)


PAIR = 2
PLANES = 4
SPOTS = PAIR * PAIR
PIECES = 4
GRANT = 56_240_000


def dense_kernel(
    emb_hbm, bucket_hbm, valid_hbm, mean_ref, best_ref,
    emb_ref, bucket_ref, valid_ref,
    keys, key_meta, plane, spot_meta, plane_meta, query_col, total, peak, weight,
    part_out, part_in, stat_out, stat_in, help_terms, help_out, help_in, help_stat_out, help_stat_in,
    load_sem, z_send, z_recv, zm_send, zm_recv, c_send, c_recv, cm_send, cm_recv,
    q_send, q_recv, qm_send, qm_recv, f_send, f_recv,
    p_send, corner_recv, p_recv, s_send, sc_recv, s_recv, h_send, h_recv,
):
    rows, features = emb_ref.shape
    piece = rows // PIECES
    half, quarter = rows // 2, rows // 4
    halves = (pl.ds(0, half), pl.ds(half, half))
    wide, blk = lax.axis_index("wide"), lax.axis_index("blk")
    z, y = lax.div(wide, PAIR), lax.rem(wide, PAIR)
    x, core = lax.div(blk, PAIR), lax.rem(blk, PAIR)
    beside_x, beside_y, corner = 1, 2, 3

    def at(z_at, y_at, x_at, core_at):
        return (z_at * PAIR + y_at, x_at * PAIR + core_at)

    partner = at(z, y, x, 1 - core)
    x_device = at(z, y, 1 - x, core)
    y_device = at(z, 1 - y, x, core)
    inner = (z > 0) & (z < PLANES - 1)
    lower = z < PLANES // 2
    across_z = PLANES - 1 - z
    end_device = at(jnp.where(lower, 0, PLANES - 1), y, x, core)
    next_device = at(jnp.where(lower, 1, PLANES - 2), y, x, core)
    far_device = at(across_z, y, x, core)
    first_device = at(0, y, x, core)
    top_device = at(PLANES - 1, y, x, core)

    def remote(source, target, send, recv, device):
        return pltpu.make_async_remote_copy(
            src_ref=source, dst_ref=target, send_sem=send, recv_sem=recv,
            device_id=device, device_id_type=pl.DeviceIdType.MESH,
        )

    def arrived(ref, recv):
        remote(ref, ref, recv, recv, partner).wait_recv()

    def sent(ref, send):
        remote(ref, ref, send, send, partner).wait_send()

    loads = [
        pltpu.make_async_copy(source, target, load_sem.at[index])
        for index, (source, target) in enumerate(
            ((emb_hbm, emb_ref), (bucket_hbm, bucket_ref), (valid_hbm, valid_ref))
        )
    ]
    for load in loads:
        load.start()

    barrier = pltpu.get_barrier_semaphore()

    def greet(device):
        pl.semaphore_signal(barrier, inc=1, device_id=device, device_id_type=pl.DeviceIdType.MESH)

    greet(x_device)
    greet(y_device)
    greet(partner)

    @pl.when(inner)
    def _():
        greet(far_device)
        greet(end_device)

    @pl.when(jnp.logical_not(inner))
    def _():
        greet(next_device)

    @pl.when(z == 0)
    def _():
        greet(top_device)

    for load in loads:
        load.wait()
    floats = emb_ref[...].astype(jnp.float32)
    inverse = lax.rsqrt(jnp.mean(floats * floats, axis=1, keepdims=True) + 1e-06)
    unit = (floats * inverse).astype(jnp.bfloat16)
    own = jnp.where(inner, 1, 0)
    keys[own, 0] = unit
    buckets = bucket_ref[...].astype(jnp.float32)
    meta = jnp.concatenate([buckets, jnp.where(valid_ref[...] > 0, buckets, -1.0)], axis=0)
    key_meta[own, 0] = meta
    spot_meta[0] = meta

    pl.semaphore_wait(barrier, jnp.where(z > 0, 5, 4))

    def column(row):
        return jnp.transpose(jnp.broadcast_to(row, (rows, rows)))

    def terms(chosen, buckets, block, metas, itself):
        cosine = lax.dot_general(
            chosen, block, (((1,), (1,)), ((), ())), preferred_element_type=jnp.float32
        ) * (1.0 / features)
        factors = []
        peaks = None
        sums = None
        for index, meta in enumerate(metas):
            usable = buckets == meta[1:2, :]
            if index == itself:
                line = lax.broadcasted_iota(jnp.int32, (rows, rows), 0)
                lane = lax.broadcasted_iota(jnp.int32, (rows, rows), 1)
                usable = usable & (line != lane)
            values = cosine[:, index * rows : (index + 1) * rows]
            best = jnp.where(usable, values, -1.0)
            factor = jnp.where(usable, jnp.exp(sharpness * (values - 1.0)), 0.0)
            factors.append(factor.astype(jnp.bfloat16))
            peaks = best if peaks is None else jnp.maximum(peaks, best)
            sums = factor if sums is None else sums + factor
        summed = jnp.dot(
            jnp.concatenate(factors, axis=1), block, preferred_element_type=jnp.float32
        )
        return peaks, sums, summed

    def stat_rows(peaks, sums):
        top = jnp.max(jnp.transpose(peaks), axis=0, keepdims=True)
        mass = jnp.sum(jnp.transpose(sums), axis=0, keepdims=True)
        return jnp.concatenate([top, mass], axis=0)

    def run(place):
        is_inner = 0 < place < PLANES - 1
        me = 1 if is_inner else 0
        slots = (3, 4, 4, 3)[place]
        last = slots - 1
        own_rows = keys.at[me, 0]

        def z_copy(slot, target, part, device):
            ref = pl.ds(part * piece, piece)
            return remote(
                keys.at[slot, 0, ref], keys.at[target, 0, ref], z_send, z_recv.at[target, part],
                device,
            )

        def z_meta(slot, target, device):
            return remote(
                key_meta.at[slot, 0], key_meta.at[target, 0], zm_send, zm_recv.at[target], device
            )

        def c_copy(slot, part=None):
            ref = pl.ds(0, rows) if part is None else pl.ds(part * piece, piece)
            return remote(
                keys.at[slot, 0, ref], keys.at[slot, 1, ref], c_send, c_recv.at[slot], partner
            )

        def c_meta(slot):
            return remote(
                key_meta.at[slot, 0], key_meta.at[slot, 1], cm_send, cm_recv.at[slot], partner
            )

        def wait_partner(slot):
            arrived(key_meta.at[slot, 1], cm_recv.at[slot])
            arrived(keys.at[slot, 1], c_recv.at[slot])

        onward = {
            0: {0: [(0, next_device)]},
            1: {1: [(2, far_device), (1, end_device)], 0: [(3, far_device)], 2: [(2, end_device)]},
            2: {1: [(2, far_device)], 0: [(3, far_device)], 2: [(1, end_device)], 3: [(2, end_device)]},
            3: {0: [(0, next_device)]},
        }[place]

        def take_meta(slot):
            arrived(key_meta.at[slot, 0], zm_recv.at[slot])
            for target, device in onward.get(slot, ()):
                z_meta(slot, target, device).start()
            c_meta(slot).start()

        def take(slot, part):
            ref = keys.at[slot, 0, pl.ds(part * piece, piece)]
            arrived(ref, z_recv.at[slot, part])
            for target, device in onward.get(slot, ()):
                z_copy(slot, target, part, device).start()
            c_copy(slot, part).start()

        def q_copy(source, spot, side, recv, device, send=1):
            return remote(
                source.at[halves[side]], plane.at[spot - 1, 0, halves[side]], q_send.at[send],
                q_recv.at[recv], device,
            )

        def q_arrived(spot, side, recv):
            arrived(plane.at[spot - 1, 0, halves[side]], q_recv.at[recv])

        def q_meta(source, spot, device):
            return remote(
                spot_meta.at[source], spot_meta.at[spot], qm_send, qm_recv.at[spot - 1], device
            )

        def q_meta_arrived(spot):
            arrived(spot_meta.at[spot], qm_recv.at[spot - 1])

        for target, device in onward[me]:
            z_meta(me, target, device).start()
        for part in range(PIECES):
            for target, device in onward[me]:
                z_copy(me, target, part, device).start()
        q_meta(0, beside_x, x_device).start()
        q_meta(0, beside_y, y_device).start()
        q_copy(own_rows, beside_x, 0, 0, x_device, 0).start()
        q_copy(own_rows, beside_y, 1, 3, y_device, 0).start()
        c_meta(me).start()
        c_copy(me).start()
        query_col[0] = column(spot_meta[0, 0:1, :])
        sent(own_rows, q_send.at[0])
        q_copy(own_rows, beside_x, 1, 1, x_device).start()
        q_copy(own_rows, beside_y, 0, 2, y_device).start()

        def relay_q():
            q_meta_arrived(beside_x)
            q_meta(beside_x, corner, y_device).start()
            q_arrived(beside_x, 0, 0)
            q_copy(plane.at[beside_x - 1, 0], corner, 0, 4, y_device).start()
            q_meta_arrived(beside_y)
            q_arrived(beside_y, 1, 3)
            q_copy(plane.at[beside_y - 1, 0], corner, 1, 5, x_device).start()

        def pass_on(spot):
            if place > 1:
                remote(
                    plane.at[spot - 1, 0], plane.at[spot - 1, 1], f_send.at[0], f_recv.at[0], partner
                ).start()

        def finish_q(spot):
            if spot == beside_x:
                q_arrived(beside_x, 1, 1)
            elif spot == beside_y:
                q_arrived(beside_y, 0, 2)
            else:
                q_meta_arrived(corner)
                q_arrived(corner, 0, 4)
                q_arrived(corner, 1, 5)
                if place > 1:
                    remote(
                        spot_meta.at[1:SPOTS], plane_meta, f_send.at[1], f_recv.at[1], partner
                    ).start()
            pass_on(spot)
            query_col[spot] = column(spot_meta[spot, 0:1, :])

        def batch(spot, first, end):
            chosen = keys[me, 0] if spot == 0 else plane[spot - 1, 0]
            count = end - first
            itself = (me - first) * PAIR if spot == 0 and first <= me < end else None
            return terms(
                chosen,
                query_col[spot],
                keys[first:end].reshape(count * PAIR * rows, features),
                [key_meta[slot, side] for slot in range(first, end) for side in range(PAIR)],
                itself,
            )

        def early(spot):
            peak[spot], weight[spot], total[spot] = batch(spot, 0, last)

        def joint(first, end):
            block = keys[first:end].reshape((end - first) * PAIR * rows, features)
            metas = [key_meta[slot, side] for slot in range(first, end) for side in range(PAIR)]

            def of(begin, stop):
                count = (stop - begin) * rows
                shape = (stop - begin, rows)
                peaks, sums, summed = terms(
                    plane[begin - 1 : stop - 1, 0].reshape(count, features),
                    query_col[begin:stop].reshape(count, rows),
                    block, metas, None,
                )
                return (
                    peaks.reshape(*shape, rows), sums.reshape(*shape, rows),
                    summed.reshape(*shape, features),
                )

            return of

        def early_others():
            peak[1:SPOTS], weight[1:SPOTS], total[1:SPOTS] = joint(0, last)(1, SPOTS)

        def h_copy(side):
            ref = halves[side]
            return remote(
                help_out.at[ref], help_in.at[ref], h_send.at[0], h_recv.at[0],
                end_device if is_inner else first_device,
            )

        def h_stat():
            return remote(
                help_stat_out, help_stat_in, h_send.at[1], h_recv.at[1],
                end_device if is_inner else first_device,
            )

        def assist(sides=(0, 1)):
            slot = 0 if is_inner else last
            if 0 in sides:
                for ref, index in ((plane_meta, 1), (plane.at[:, 1], 0)):
                    arrived(ref, f_recv.at[index])
            of = slice(sides[0] * half, (sides[-1] + 1) * half)
            chosen = keys[slot, 0, of]
            buckets = column(key_meta[slot, 0, 0:1, :])[of]
            near = terms(
                chosen, buckets, keys[me].reshape(PAIR * rows, features),
                [key_meta[me, side] for side in range(PAIR)], None,
            )
            wider = terms(
                chosen, buckets, plane[...].reshape((SPOTS - 1) * PAIR * rows, features),
                [ref[spot] for spot in range(SPOTS - 1) for ref in (spot_meta.at[1:SPOTS], plane_meta)],
                None,
            )
            help_out[of] = (near[2] + wider[2]).astype(jnp.bfloat16)
            help_terms[0, of] = jnp.maximum(near[0], wider[0])
            help_terms[1, of] = near[1] + wider[1]
            for side in sides:
                h_copy(side).start()
            if 1 in sides:
                help_stat_out[...] = stat_rows(help_terms[0], help_terms[1])
                h_stat().start()

        def take_all(*order):
            for slot, part in order:
                take(slot, part)

        if place == 0:
            relay_q()
            take_meta(1)
            take_all((1, 0), (1, 1), (1, 2), (1, 3))
            finish_q(beside_x)
            finish_q(beside_y)
            wait_partner(0)
            wait_partner(1)
            early(0)
            take_meta(2)
            take(2, 0)
            finish_q(corner)
            early_others()
            take_all((2, 1), (2, 2), (2, 3))
        elif place == 1:
            take_meta(0)
            take(0, 0)
            take_meta(2)
            take_all((0, 1), (2, 0))
            relay_q()
            take_all((0, 2), (2, 1), (0, 3), (2, 2), (2, 3))
            finish_q(beside_x)
            finish_q(beside_y)
            for slot in range(last):
                wait_partner(slot)
            early(0)
            take_meta(3)
            take(3, 0)
            finish_q(corner)
            early_others()
            take_all((3, 1), (3, 2), (3, 3))
        elif place == 2:
            take_meta(2)
            take(2, 0)
            take_meta(0)
            take_all((2, 1), (0, 0), (2, 2))
            relay_q()
            take_all((0, 1), (2, 3), (0, 2))
            take_meta(3)
            take_all((3, 0), (0, 3), (3, 1), (3, 2))
            finish_q(beside_x)
            finish_q(beside_y)
            for slot in range(last):
                wait_partner(slot)
            finish_q(corner)
            take(3, 3)
            early(corner)
        else:
            relay_q()
            finish_q(beside_x)
            finish_q(beside_y)
            wait_partner(0)
            take_meta(1)
            take_all((1, 0), (1, 1), (1, 2), (1, 3))
            finish_q(corner)
            wait_partner(1)
            early(0)
            early_others()
            take_meta(2)
            take_all((2, 0), (2, 1), (2, 2), (2, 3))
            assist()

        wait_partner(last)

        def p_copy(spot, side):
            return remote(
                part_out.at[spot - 1, halves[side]], part_in.at[spot - 1, halves[side]],
                p_send.at[1], p_recv, x_device if spot == beside_x else y_device,
            )

        def corner_copy(side, turn):
            ref = pl.ds(side * half + turn * quarter, quarter)
            return remote(
                part_out.at[corner - 1, ref], part_in.at[corner - 1, ref],
                p_send.at[2 * turn], corner_recv.at[side], (x_device, y_device)[side],
            )

        def s_copy(spot, device, recv):
            return remote(stat_out.at[spot - 1], stat_in.at[spot - 1], s_send, recv, device)

        begun = (corner,) if place == 2 else (0, 1, 2, 3)

        def final(spot):
            if spot not in begun:
                return batch(spot, 0, slots)
            peaks, sums, summed = batch(spot, last, slots)
            return jnp.maximum(peak[spot], peaks), weight[spot] + sums, total[spot] + summed

        def send_stats(spot, peaks, sums):
            stat_out[spot - 1] = stat_rows(peaks, sums)
            s_copy(spot, x_device, sc_recv if spot == corner else s_recv).start()

        peaks, sums, summed = final(corner)
        part_out[corner - 1] = summed.astype(jnp.bfloat16)
        for turn in range(2):
            for side in range(2):
                corner_copy(side, turn).start()
        send_stats(corner, peaks, sums)
        both = (beside_x, beside_y)
        if place != 2:
            peaks, sums, summed = joint(last, slots)(1, 3)
            finals = [
                (
                    jnp.maximum(peak[spot], peaks[spot - 1]), weight[spot] + sums[spot - 1],
                    total[spot] + summed[spot - 1],
                )
                for spot in both
            ]
        else:
            finals = [final(spot) for spot in both]
        for spot, side, (peaks, sums, summed) in zip(both, (0, 1), finals):
            total[spot] = summed
            part_out[spot - 1, halves[side]] = summed[side * half : (side + 1) * half].astype(jnp.bfloat16)
            if spot == beside_x:
                send_stats(spot, peaks, sums)
            else:
                y_stats = stat_rows(peaks, sums)
        def own_final():
            peaks, sums, summed = final(0)
            total[0] = summed + keys[me, 0].astype(jnp.float32)
            return stat_rows(peaks, sums)

        if place != 2:
            own_stats = own_final()
        sent(part_out.at[corner - 1, halves[0]], p_send.at[0])
        for spot, side in zip(both, (0, 1)):
            p_copy(spot, side).start()
        if place == 2:
            own_stats = own_final()
            assist()
        arrived(stat_in.at[corner - 1], sc_recv)
        stat_out[beside_y - 1] = jnp.concatenate(
            [
                jnp.maximum(y_stats[0:1], stat_in[corner - 1, 0:1]),
                y_stats[1:2] + stat_in[corner - 1, 1:2],
            ],
            axis=0,
        )
        s_copy(beside_y, y_device, s_recv).start()
        for spot, side in ((beside_x, 1), (beside_y, 0)):
            arrived(part_in.at[corner - 1, halves[side]], corner_recv.at[side])
            part_out[spot - 1, halves[side]] = (
                total[spot, halves[side]] + part_in[corner - 1, halves[side]].astype(jnp.float32)
            ).astype(jnp.bfloat16)
            p_copy(spot, side).start()

        top, mass = own_stats[0:1], own_stats[1:2]
        if not is_inner:
            arrived(help_stat_in, h_recv.at[1])
            arrived(help_in, h_recv.at[0])
            top = jnp.maximum(top, help_stat_in[0:1])
            mass = mass + help_stat_in[1:2]
            total[0] += help_in[...].astype(jnp.float32)
        arrived(stat_in.at[0 : corner - 1], s_recv)
        for spot in (beside_x, beside_y):
            top = jnp.maximum(top, stat_in[spot - 1, 0:1])
            mass = mass + stat_in[spot - 1, 1:2]
        best_ref[...] = top
        below = column(1.0 + mass)[:, 0:1]
        arrived(part_in.at[0 : corner - 1], p_recv)
        result = total[0]
        for spot in (beside_x, beside_y):
            result = result + part_in[spot - 1].astype(jnp.float32)
        mean_ref[...] = (result / below).astype(jnp.bfloat16)

        blocks = keys.at[0:slots, 0]
        metas = key_meta.at[0:slots, 0]
        hops = sum(len(ways) for ways in onward.values())
        sent(keys.at[0:hops, 0], z_send)
        sent(key_meta.at[0:hops, 0], zm_send)
        sent(blocks, c_send)
        sent(metas, cm_send)
        sent(plane.at[0 : corner - 1, 0], q_send.at[1])
        sent(spot_meta.at[1:SPOTS], qm_send)
        sent(part_out.at[0 : corner - 1], p_send.at[1])
        sent(part_out.at[corner - 1, halves[0]], p_send.at[2])
        sent(stat_out, s_send)
        if place > 1:
            sent(plane.at[:, 0], f_send.at[0])
            sent(plane_meta, f_send.at[1])
            sent(help_out, h_send.at[0])
            sent(help_stat_out, h_send.at[1])

    for place in range(PLANES):
        pl.when(z == place)(functools.partial(run, place))


def finish_kernel(mean_ref, best_ref, mean_out, best_out, line, sem):
    line[...] = best_ref[0].astype(jnp.bfloat16)
    copies = [
        pltpu.make_async_copy(mean_ref, mean_out, sem.at[0]),
        pltpu.make_async_copy(line, best_out, sem.at[1]),
    ]
    for copy in copies:
        copy.start()
    for copy in copies:
        copy.wait()


def finish(mean, best):
    rows, features = mean.shape
    vmem = pl.BlockSpec(memory_space=pltpu.VMEM)
    hbm = pl.BlockSpec(memory_space=pltpu.HBM)
    return pl.pallas_call(
        finish_kernel,
        out_shape=(
            jax.ShapeDtypeStruct((rows, features), jnp.bfloat16),
            jax.ShapeDtypeStruct((rows,), jnp.bfloat16),
        ),
        in_specs=[vmem, vmem],
        out_specs=(hbm, hbm),
        scratch_shapes=[pltpu.VMEM((rows,), jnp.bfloat16), pltpu.SemaphoreType.DMA((2,))],
        compiler_params=pltpu.CompilerParams(vmem_limit_bytes=4_000_000),
    )(mean, best)


def dense(embeddings, bucket_ids, valid_rows):
    rows, features = embeddings.shape
    dma = pltpu.SemaphoreType.DMA
    vmem = pl.BlockSpec(memory_space=pltpu.VMEM)
    others = SPOTS - 1

    def bf16(*shape):
        return pltpu.VMEM((*shape, rows, features), jnp.bfloat16)

    def f32(*shape):
        return pltpu.VMEM(shape, jnp.float32)

    mean, best = pl.pallas_call(
        dense_kernel,
        out_shape=(
            jax.ShapeDtypeStruct((rows, features), jnp.bfloat16),
            jax.ShapeDtypeStruct((1, rows), jnp.float32),
        ),
        in_specs=[pl.BlockSpec(memory_space=pltpu.HBM)] * 3,
        out_specs=(vmem, vmem),
        scratch_shapes=[
            bf16(), pltpu.VMEM((1, rows), jnp.int32), pltpu.VMEM((1, rows), jnp.int32),
            bf16(PLANES, PAIR), f32(PLANES, PAIR, 2, rows), bf16(others, PAIR),
            f32(SPOTS, 2, rows), f32(others, 2, rows), f32(SPOTS, rows, rows),
            f32(SPOTS, rows, features), f32(SPOTS, rows, rows), f32(SPOTS, rows, rows),
            bf16(others), bf16(others), f32(others, 2, rows), f32(others, 2, rows),
            f32(2, rows, rows), bf16(), bf16(), f32(2, rows), f32(2, rows),
            dma((3,)), dma, dma((PLANES, PIECES)), dma, dma((PLANES,)),
            dma, dma((PLANES,)), dma, dma((PLANES,)),
            dma((2,)), dma((6,)), dma, dma((others,)), dma((2,)), dma((2,)),
            dma((3,)), dma((2,)), dma, dma, dma, dma, dma((2,)), dma((2,)),
        ],
        compiler_params=pltpu.CompilerParams(
            collective_id=0, has_side_effects=True, vmem_limit_bytes=GRANT
        ),
    )(
        *[
            pltpu.with_memory_space_constraint(value, pltpu.HBM)
            for value in (embeddings, bucket_ids.reshape(1, rows), valid_rows.reshape(1, rows))
        ]
    )
    return finish(mean, best)


def on_device(embeddings, bucket_ids, slot_ids, valid_rows):
    rows = embeddings.shape[0]
    groups = lax.axis_size("wide")
    blocks = lax.axis_size("blk")
    bucket_work = blocks * (2 * rows) ** 2
    dense_work = groups * blocks * rows**2
    fits = groups % PAIR == 0 and groups == PLANES * PAIR and blocks == PAIR * PAIR and rows == 128
    if fits and dense_work <= 4 * bucket_work:
        return dense(embeddings, bucket_ids, valid_rows)
    return by_bucket(embeddings, bucket_ids, slot_ids, valid_rows)


def solution(mesh):
    in_specs = (
        P(("wide", "blk"), None),
        P(("wide", "blk")),
        P(("wide", "blk")),
        P(("wide", "blk")),
    )
    out_specs = (P(("wide", "blk"), None), P(("wide", "blk")))
    return jax.shard_map(
        on_device, mesh=mesh, in_specs=in_specs, out_specs=out_specs, check_vma=False
    )
```

```python
import functools

import jax
import jax.numpy as jnp
from jax import lax
from jax.experimental import pallas as pl
from jax.experimental.pallas import tpu as pltpu
from jax.sharding import PartitionSpec as P

sharpness = 10.0


def from_behind(value, axis, steps):
    count = lax.axis_size(axis)
    pairs = [(source, (source + steps) % count) for source in range(count)]
    return lax.ppermute(value, axis, pairs)


def unit_rows(embeddings):
    float_rows = embeddings.astype(jnp.float32)
    inverse_norm = lax.rsqrt(jnp.mean(float_rows * float_rows, axis=1, keepdims=True) + 1e-06)
    return (float_rows * inverse_norm).astype(jnp.bfloat16)


def bucket_stats(queries, query_pos, key_rows, key_flags, key_pos):
    feature_count = queries.shape[1]
    cosine = (
        lax.dot_general(
            queries, key_rows, (((1,), (1,)), ((), ())), preferred_element_type=jnp.float32
        )
        / feature_count
    )
    usable = (key_flags[None, :] > 0) & (query_pos[:, None] != key_pos[None, :])
    best_cos = jnp.max(jnp.where(usable, cosine, -1.0), axis=1)
    weights = jnp.where(usable, jnp.exp(sharpness * (cosine - 1.0)), 0.0)
    weight_total = jnp.sum(weights, axis=1)
    summed = jnp.dot(weights.astype(jnp.bfloat16), key_rows, preferred_element_type=jnp.float32)
    return (best_cos, weight_total, summed)


def by_bucket(embeddings, bucket_ids, slot_ids, valid_rows):
    unit_vectors = unit_rows(embeddings)
    row_count, feature_count = unit_vectors.shape
    groups = lax.axis_size("wide")
    blocks = lax.axis_size("blk")
    slot_count = 2 * row_count // groups
    block_rows = groups * slot_count
    cell_ids = bucket_ids * slot_count + slot_ids
    outgoing = jnp.zeros((block_rows, feature_count), jnp.bfloat16).at[cell_ids].set(unit_vectors)
    flag_rows = (
        jnp.zeros((block_rows,), jnp.bfloat16).at[cell_ids].set(valid_rows.astype(jnp.bfloat16))
    )
    arrived, arrived_flags = (
        lax.all_to_all(
            outgoing.reshape(groups, slot_count, feature_count),
            "wide",
            split_axis=0,
            concat_axis=0,
            tiled=True,
        ),
        lax.all_to_all(
            flag_rows.reshape(groups, slot_count), "wide", split_axis=0, concat_axis=0, tiled=True
        ),
    )
    queries = arrived.reshape(block_rows, feature_count)
    query_flags = arrived_flags.reshape(block_rows)
    my_block = lax.axis_index("blk")
    query_pos = my_block * block_rows + jnp.arange(block_rows, dtype=jnp.int32)

    def absorb(running, key_rows, key_flags, key_start):
        key_pos = key_start + jnp.arange(key_rows.shape[0], dtype=jnp.int32)
        best_cos, weight_total, summed = bucket_stats(
            queries, query_pos, key_rows, key_flags, key_pos
        )
        return (jnp.maximum(running[0], best_cos), running[1] + weight_total, running[2] + summed)

    initial = (
        jnp.full((block_rows,), -1.0, jnp.float32),
        jnp.zeros((block_rows,), jnp.float32),
        jnp.zeros((block_rows, feature_count), jnp.float32),
    )
    key_rows, key_flags = (queries, query_flags)
    running = absorb(initial, key_rows, key_flags, my_block * block_rows)
    for turn_index in range(1, blocks):
        key_rows, key_flags = from_behind((key_rows, key_flags), "blk", 1)
        running = absorb(
            running, key_rows, key_flags, (my_block - turn_index) % blocks * block_rows
        )
    best_cos, weight_total, summed = running
    mean_rows = ((queries.astype(jnp.float32) + summed) / (1.0 + weight_total[:, None])).astype(
        jnp.bfloat16
    )
    back_mean, back_best = (
        lax.all_to_all(
            mean_rows.reshape(groups, slot_count, feature_count),
            "wide",
            split_axis=0,
            concat_axis=0,
            tiled=True,
        ),
        lax.all_to_all(
            best_cos.astype(jnp.bfloat16).reshape(groups, slot_count),
            "wide",
            split_axis=0,
            concat_axis=0,
            tiled=True,
        ),
    )
    neighbour_mean = back_mean.reshape(block_rows, feature_count)[cell_ids]
    max_cosine = back_best.reshape(block_rows)[cell_ids]
    return (neighbour_mean, max_cosine)


PAIR = 2
PLANES = 4
SPOTS = PAIR * PAIR
PIECES = 8
GRANT = 56_240_000


def dense_kernel(
    emb_hbm, bucket_hbm, valid_hbm, mean_ref, best_ref,
    emb_ref, bucket_ref, valid_ref,
    keys, key_meta, plane, spot_meta, plane_meta, query_col, total, peak, weight,
    part_out, part_in, stat_out, stat_in, help_out, help_in, help_stat_out, help_stat_in,
    ready, load_sem, z_send, z_recv, zm_recv, c_send, c_recv, cm_recv,
    q_send, q_recv, qm_recv, f_send, f_recv,
    p_send, corner_recv, p_recv, sc_recv, s_recv, h_send, h_recv, small_send,
):
    rows, features = emb_ref.shape
    piece = rows // PIECES
    half, quarter = rows // 2, rows // 4
    halves = (pl.ds(0, half), pl.ds(half, half))
    wide, blk = lax.axis_index("wide"), lax.axis_index("blk")
    z, y = lax.div(wide, PAIR), lax.rem(wide, PAIR)
    x, core = lax.div(blk, PAIR), lax.rem(blk, PAIR)
    beside_x, beside_y, corner = 1, 2, 3

    def at(z_at, y_at, x_at, core_at):
        return (z_at * PAIR + y_at, x_at * PAIR + core_at)

    partner = at(z, y, x, 1 - core)
    x_device = at(z, y, 1 - x, core)
    y_device = at(z, 1 - y, x, core)
    inner = (z > 0) & (z < PLANES - 1)
    lower = z < PLANES // 2
    across_z = PLANES - 1 - z
    end_device = at(jnp.where(lower, 0, PLANES - 1), y, x, core)
    next_device = at(jnp.where(lower, 1, PLANES - 2), y, x, core)
    far_device = at(across_z, y, x, core)
    first_device = at(0, y, x, core)
    top_device = at(PLANES - 1, y, x, core)

    def remote(source, target, send, recv, device):
        return pltpu.make_async_remote_copy(
            src_ref=source, dst_ref=target, send_sem=send, recv_sem=recv,
            device_id=device, device_id_type=pl.DeviceIdType.MESH,
        )

    def arrived(ref, recv):
        remote(ref, ref, recv, recv, partner).wait_recv()

    def sent(ref, send):
        remote(ref, ref, send, send, partner).wait_send()

    loads = [
        pltpu.make_async_copy(source, target, load_sem.at[index])
        for index, (source, target) in enumerate(
            ((emb_hbm, emb_ref), (bucket_hbm, bucket_ref), (valid_hbm, valid_ref))
        )
    ]
    for load in loads:
        load.start()

    barrier = pltpu.get_barrier_semaphore()

    def greet(device):
        pl.semaphore_signal(barrier, inc=1, device_id=device, device_id_type=pl.DeviceIdType.MESH)

    greet(x_device)
    greet(y_device)
    greet(partner)

    @pl.when(z < PLANES - 1)
    def _():
        greet(at(z + 1, y, x, core))

    @pl.when(z == 1)
    def _():
        greet(first_device)

    @pl.when(z == 0)
    def _():
        greet(top_device)

    for load in loads:
        load.wait()
    floats = emb_ref[...].astype(jnp.float32)
    inverse = lax.rsqrt(jnp.mean(floats * floats, axis=1, keepdims=True) + 1e-06)
    unit = (floats * inverse).astype(jnp.bfloat16)
    own = jnp.where(inner, 1, 0)
    keys[own, 0] = unit
    buckets = bucket_ref[...].astype(jnp.float32)
    meta = jnp.concatenate([buckets, jnp.where(valid_ref[...] > 0, buckets, -1.0)], axis=0)
    key_meta[own, 0] = meta
    spot_meta[0] = meta

    pl.semaphore_wait(barrier, jnp.where(z == PLANES - 1, 5, 4))

    @pl.when(z >= 2)
    def _():
        pl.semaphore_signal(
            ready, inc=1, device_id=at(z - 1, y, x, core), device_id_type=pl.DeviceIdType.MESH
        )

    def column(row):
        return jnp.transpose(jnp.broadcast_to(row, (rows, rows)))

    def terms(chosen, buckets, block, metas, itself):
        cosine = lax.dot_general(
            chosen, block, (((1,), (1,)), ((), ())), preferred_element_type=jnp.float32
        ) * (1.0 / features)
        factors = []
        peaks = None
        sums = None
        for index, meta in enumerate(metas):
            usable = buckets == meta[1:2, :]
            if index == itself:
                line = lax.broadcasted_iota(jnp.int32, (rows, rows), 0)
                lane = lax.broadcasted_iota(jnp.int32, (rows, rows), 1)
                usable = usable & (line != lane)
            values = cosine[:, index * rows : (index + 1) * rows]
            best = jnp.where(usable, values, -1.0)
            factor = jnp.where(usable, jnp.exp(sharpness * (values - 1.0)), 0.0)
            factors.append(factor.astype(jnp.bfloat16))
            peaks = best if peaks is None else jnp.maximum(peaks, best)
            sums = factor if sums is None else sums + factor
        summed = jnp.dot(
            jnp.concatenate(factors, axis=1), block, preferred_element_type=jnp.float32
        )
        return peaks, sums, summed

    def stat_rows(peaks, sums):
        top = jnp.max(jnp.transpose(peaks), axis=0, keepdims=True)
        mass = jnp.sum(jnp.transpose(sums), axis=0, keepdims=True)
        return jnp.concatenate([top, mass], axis=0)

    def run(place):
        is_inner = 0 < place < PLANES - 1
        me = 1 if is_inner else 0
        slots = (3, 4, 3, 2)[place]
        last = slots - 1
        own_rows = keys.at[me, 0]

        def z_copy(slot, target, part, device):
            ref = pl.ds(part * piece, piece)
            return remote(
                keys.at[slot, 0, ref], keys.at[target, 0, ref], z_send, z_recv.at[(0, 1, 2, 1)[target], part],
                device,
            )

        def z_meta(slot, target, device):
            return remote(
                key_meta.at[slot, 0], key_meta.at[target, 0], small_send, zm_recv.at[target], device
            )

        def c_copy(slot, part=None):
            ref = pl.ds(0, rows) if part is None else pl.ds(part * piece, piece)
            return remote(
                keys.at[slot, 0, ref], keys.at[slot, 1, ref], c_send, c_recv.at[slot], partner
            )

        def c_meta(slot):
            return remote(
                key_meta.at[slot, 0], key_meta.at[slot, 1], small_send, cm_recv.at[slot], partner
            )

        def wait_partner(slot):
            arrived(key_meta.at[slot, 1], cm_recv.at[slot])
            arrived(keys.at[slot, 1], c_recv.at[slot])

        onward = {
            0: {0: [(0, next_device)]},
            1: {1: [(1, end_device)], 0: [(2, far_device)], 2: [(2, end_device)]},
            2: {1: [(2, far_device)], 0: [(3, far_device)], 2: [(1, end_device)]},
            3: {0: [(0, next_device)]},
        }[place]
        helps = {
            0: [],
            1: [(2, far_device, 0), (3, top_device, 1)],
            2: [(0, end_device, 0)],
            3: [(1, first_device, 0)],
        }[place]
        helpers = (1, 0, 1, 2)[place]

        def take_meta(slot):
            arrived(key_meta.at[slot, 0], zm_recv.at[slot])
            for target, device in onward.get(slot, ()):
                z_meta(slot, target, device).start()
            c_meta(slot).start()

        def take(slot, part):
            for step in range(PIECES // 4):
                take_piece(slot, part * (PIECES // 4) + step)

        def take_piece(slot, part):
            ref = keys.at[slot, 0, pl.ds(part * piece, piece)]
            arrived(ref, z_recv.at[(0, 1, 2, 1)[slot], part])
            for target, device in onward.get(slot, ()):
                z_copy(slot, target, part, device).start()
            c_copy(slot, part).start()

        def q_copy(source, spot, side, recv, device, send=1):
            return remote(
                source.at[halves[side]], plane.at[spot - 1, 0, halves[side]], q_send.at[send],
                q_recv.at[recv], device,
            )

        def q_arrived(spot, side, recv):
            arrived(plane.at[spot - 1, 0, halves[side]], q_recv.at[recv])

        def q_meta(source, spot, device):
            return remote(
                spot_meta.at[source], spot_meta.at[spot], small_send, qm_recv.at[spot - 1], device
            )

        def q_meta_arrived(spot):
            arrived(spot_meta.at[spot], qm_recv.at[spot - 1])

        for target, device in onward[me]:
            z_meta(me, target, device).start()
        for part in range(PIECES):
            for target, device in onward[me]:
                z_copy(me, target, part, device).start()
        q_meta(0, beside_x, x_device).start()
        q_meta(0, beside_y, y_device).start()
        q_copy(own_rows, beside_x, 0, 0, x_device, 0).start()
        q_copy(own_rows, beside_y, 1, 3, y_device, 0).start()
        c_meta(me).start()
        c_copy(me).start()
        query_col[0] = column(spot_meta[0, 0:1, :])
        sent(own_rows, q_send.at[0])
        q_copy(own_rows, beside_x, 1, 1, x_device).start()
        q_copy(own_rows, beside_y, 0, 2, y_device).start()

        def relay_q():
            q_meta_arrived(beside_x)
            q_meta(beside_x, corner, y_device).start()
            q_arrived(beside_x, 0, 0)
            q_copy(plane.at[beside_x - 1, 0], corner, 0, 4, y_device).start()
            q_meta_arrived(beside_y)
            q_arrived(beside_y, 1, 3)
            q_copy(plane.at[beside_y - 1, 0], corner, 1, 5, x_device).start()

        def pass_on(spot):
            if place > 0:
                remote(
                    plane.at[spot - 1, 0], plane.at[spot - 1, 1], f_send, f_recv.at[0], partner
                ).start()

        def finish_q(spot):
            if spot == beside_x:
                q_arrived(beside_x, 1, 1)
            elif spot == beside_y:
                q_arrived(beside_y, 0, 2)
            else:
                q_meta_arrived(corner)
                q_arrived(corner, 0, 4)
                q_arrived(corner, 1, 5)
                if place > 0:
                    remote(
                        spot_meta.at[1:SPOTS], plane_meta, small_send, f_recv.at[1], partner
                    ).start()
            pass_on(spot)
            query_col[spot] = column(spot_meta[spot, 0:1, :])

        def batch(spot, first, end):
            chosen = keys[me, 0] if spot == 0 else plane[spot - 1, 0]
            count = end - first
            itself = (me - first) * PAIR if spot == 0 and first <= me < end else None
            return terms(
                chosen,
                query_col[spot],
                keys[first:end].reshape(count * PAIR * rows, features),
                [key_meta[slot, side] for slot in range(first, end) for side in range(PAIR)],
                itself,
            )

        def early(spot):
            peak[spot], weight[spot], total[spot] = batch(spot, 0, last)

        def joint(first, end):
            block = keys[first:end].reshape((end - first) * PAIR * rows, features)
            metas = [key_meta[slot, side] for slot in range(first, end) for side in range(PAIR)]

            def of(begin, stop):
                count = (stop - begin) * rows
                shape = (stop - begin, rows)
                peaks, sums, summed = terms(
                    plane[begin - 1 : stop - 1, 0].reshape(count, features),
                    query_col[begin:stop].reshape(count, rows),
                    block, metas, None,
                )
                return (
                    peaks.reshape(*shape, rows), sums.reshape(*shape, rows),
                    summed.reshape(*shape, features),
                )

            return of

        def early_others():
            peak[1:SPOTS], weight[1:SPOTS], total[1:SPOTS] = joint(0, last)(1, SPOTS)

        def assist(turn):
            slot, device, index = helps[turn]
            if turn == 0:
                arrived(plane_meta, f_recv.at[1])
                arrived(plane.at[:, 1], f_recv.at[0])
            chosen = keys[slot, 0]
            buckets = column(key_meta[slot, 0, 0:1, :])
            near = terms(
                chosen, buckets, keys[me].reshape(PAIR * rows, features),
                [key_meta[me, side] for side in range(PAIR)], None,
            )
            wider = terms(
                chosen, buckets, plane[...].reshape((SPOTS - 1) * PAIR * rows, features),
                [ref[spot] for spot in range(SPOTS - 1) for ref in (spot_meta.at[1:SPOTS], plane_meta)],
                None,
            )
            help_out[turn] = (near[2] + wider[2]).astype(jnp.bfloat16)
            remote(
                help_out.at[turn], help_in.at[index], h_send, h_recv.at[index, 0], device
            ).start()
            help_stat_out[turn] = stat_rows(jnp.maximum(near[0], wider[0]), near[1] + wider[1])
            remote(
                help_stat_out.at[turn], help_stat_in.at[index], small_send, h_recv.at[index, 1],
                device,
            ).start()

        def take_all(*order):
            for slot, part in order:
                take(slot, part)

        if place == 0:
            relay_q()
            take_meta(1)
            take_all((1, 0), (1, 1), (1, 2), (1, 3))
            finish_q(beside_x)
            finish_q(beside_y)
            wait_partner(0)
            wait_partner(1)
            early(0)
            take_meta(2)
            take(2, 0)
            finish_q(corner)
            early_others()
            take_all((2, 1), (2, 2), (2, 3))
        elif place == 1:
            pl.semaphore_wait(ready, 1)
            take_meta(0)
            take(0, 0)
            take_meta(2)
            take_all((0, 1), (2, 0))
            relay_q()
            take_all((0, 2), (2, 1), (0, 3), (2, 2), (2, 3))
            finish_q(beside_x)
            finish_q(beside_y)
            for slot in range(last):
                wait_partner(slot)
            early(0)
            take_meta(3)
            take(3, 0)
            finish_q(corner)
            early_others()
            take_all((3, 1), (3, 2))
            assist(0)
            take(3, 3)
        elif place == 2:
            take_meta(0)
            take(0, 0)
            pl.semaphore_wait(ready, 1)
            take_meta(2)
            relay_q()
            take_all((2, 0), (0, 1), (2, 1), (0, 2), (2, 2), (0, 3), (2, 3))
            finish_q(beside_x)
            finish_q(beside_y)
            for slot in range(last):
                wait_partner(slot)
            finish_q(corner)
        else:
            relay_q()
            finish_q(beside_x)
            finish_q(beside_y)
            wait_partner(0)
            take_meta(1)
            take(1, 0)
            early(0)
            take(1, 1)
            finish_q(corner)
            early_others()
            take_all((1, 2), (1, 3))
            assist(0)

        wait_partner(last)

        def p_copy(spot, side):
            return remote(
                part_out.at[spot - 1, halves[side]], part_in.at[spot - 1, halves[side]],
                p_send.at[1], p_recv, x_device if spot == beside_x else y_device,
            )

        def corner_copy(side, turn):
            ref = pl.ds(side * half + turn * quarter, quarter)
            return remote(
                part_out.at[corner - 1, ref], part_in.at[corner - 1, ref],
                p_send.at[2 * turn], corner_recv.at[side], (x_device, y_device)[side],
            )

        def s_copy(spot, device, recv):
            return remote(stat_out.at[spot - 1], stat_in.at[spot - 1], small_send, recv, device)

        begun = () if place == 2 else (0, 1, 2, 3)

        def final(spot):
            if spot not in begun:
                return batch(spot, 0, slots)
            peaks, sums, summed = batch(spot, last, slots)
            return jnp.maximum(peak[spot], peaks), weight[spot] + sums, total[spot] + summed

        def send_stats(spot, peaks, sums):
            stat_out[spot - 1] = stat_rows(peaks, sums)
            s_copy(spot, x_device, sc_recv if spot == corner else s_recv).start()

        peaks, sums, summed = final(corner)
        part_out[corner - 1] = summed.astype(jnp.bfloat16)
        for turn in range(2):
            for side in range(2):
                corner_copy(side, turn).start()
        send_stats(corner, peaks, sums)
        if place == 2:
            assist(0)
        both = (beside_x, beside_y)
        peaks, sums, summed = joint(0 if place == 2 else last, slots)(1, 3)
        finals = [(peaks[index], sums[index], summed[index]) for index in range(2)]
        if place != 2:
            finals = [
                (jnp.maximum(peak[spot], top), weight[spot] + mass, total[spot] + whole)
                for spot, (top, mass, whole) in zip(both, finals)
            ]
        for spot, side, (peaks, sums, summed) in zip(both, (0, 1), finals):
            total[spot] = summed
            part_out[spot - 1, halves[side]] = summed[side * half : (side + 1) * half].astype(jnp.bfloat16)
            if spot == beside_x:
                send_stats(spot, peaks, sums)
            else:
                y_stats = stat_rows(peaks, sums)
        def own_final():
            peaks, sums, summed = final(0)
            total[0] = summed + keys[me, 0].astype(jnp.float32)
            return stat_rows(peaks, sums)

        own_stats = own_final()
        sent(part_out.at[corner - 1, halves[0]], p_send.at[0])
        for spot, side in zip(both, (0, 1)):
            p_copy(spot, side).start()
        if place == 1:
            assist(1)
        arrived(stat_in.at[corner - 1], sc_recv)
        stat_out[beside_y - 1] = jnp.concatenate(
            [
                jnp.maximum(y_stats[0:1], stat_in[corner - 1, 0:1]),
                y_stats[1:2] + stat_in[corner - 1, 1:2],
            ],
            axis=0,
        )
        s_copy(beside_y, y_device, s_recv).start()
        for spot, side in ((beside_x, 1), (beside_y, 0)):
            arrived(part_in.at[corner - 1, halves[side]], corner_recv.at[side])
            part_out[spot - 1, halves[side]] = (
                total[spot, halves[side]] + part_in[corner - 1, halves[side]].astype(jnp.float32)
            ).astype(jnp.bfloat16)
            p_copy(spot, side).start()

        top, mass = own_stats[0:1], own_stats[1:2]
        for index in range(helpers):
            arrived(help_stat_in.at[index], h_recv.at[index, 1])
            arrived(help_in.at[index], h_recv.at[index, 0])
            top = jnp.maximum(top, help_stat_in[index, 0:1])
            mass = mass + help_stat_in[index, 1:2]
            total[0] += help_in[index].astype(jnp.float32)
        arrived(stat_in.at[0 : corner - 1], s_recv)
        for spot in (beside_x, beside_y):
            top = jnp.maximum(top, stat_in[spot - 1, 0:1])
            mass = mass + stat_in[spot - 1, 1:2]
        best_ref[...] = top
        below = column(1.0 + mass)[:, 0:1]
        arrived(part_in.at[0 : corner - 1], p_recv)
        result = total[0]
        for spot in (beside_x, beside_y):
            result = result + part_in[spot - 1].astype(jnp.float32)
        mean_ref[...] = (result / below).astype(jnp.bfloat16)

        hops = sum(len(ways) for ways in onward.values())
        sent(keys.at[0:hops, 0], z_send)
        sent(keys.at[0:slots, 0], c_send)
        sent(plane.at[0 : corner - 1, 0], q_send.at[1])
        sent(part_out.at[0 : corner - 1], p_send.at[1])
        sent(part_out.at[corner - 1, halves[0]], p_send.at[2])
        pairs = hops + slots + 3 + 3 + (3 if place > 0 else 0) + len(helps)
        sent(peak.at[0, pl.ds(0, 2 * pairs)], small_send)
        if place > 0:
            sent(plane.at[:, 0], f_send)
            sent(help_out.at[0 : len(helps)], h_send)

    for place in range(PLANES):
        pl.when(z == place)(functools.partial(run, place))


def finish_kernel(mean_ref, best_ref, mean_out, best_out, line, sem):
    line[...] = best_ref[0].astype(jnp.bfloat16)
    copies = [
        pltpu.make_async_copy(mean_ref, mean_out, sem.at[0]),
        pltpu.make_async_copy(line, best_out, sem.at[1]),
    ]
    for copy in copies:
        copy.start()
    for copy in copies:
        copy.wait()


def finish(mean, best):
    rows, features = mean.shape
    vmem = pl.BlockSpec(memory_space=pltpu.VMEM)
    hbm = pl.BlockSpec(memory_space=pltpu.HBM)
    return pl.pallas_call(
        finish_kernel,
        out_shape=(
            jax.ShapeDtypeStruct((rows, features), jnp.bfloat16),
            jax.ShapeDtypeStruct((rows,), jnp.bfloat16),
        ),
        in_specs=[vmem, vmem],
        out_specs=(hbm, hbm),
        scratch_shapes=[pltpu.VMEM((rows,), jnp.bfloat16), pltpu.SemaphoreType.DMA((2,))],
        compiler_params=pltpu.CompilerParams(vmem_limit_bytes=4_000_000),
    )(mean, best)


def dense(embeddings, bucket_ids, valid_rows):
    rows, features = embeddings.shape
    dma = pltpu.SemaphoreType.DMA
    vmem = pl.BlockSpec(memory_space=pltpu.VMEM)
    others = SPOTS - 1

    def bf16(*shape):
        return pltpu.VMEM((*shape, rows, features), jnp.bfloat16)

    def f32(*shape):
        return pltpu.VMEM(shape, jnp.float32)

    mean, best = pl.pallas_call(
        dense_kernel,
        out_shape=(
            jax.ShapeDtypeStruct((rows, features), jnp.bfloat16),
            jax.ShapeDtypeStruct((1, rows), jnp.float32),
        ),
        in_specs=[pl.BlockSpec(memory_space=pltpu.HBM)] * 3,
        out_specs=(vmem, vmem),
        scratch_shapes=[
            bf16(), pltpu.VMEM((1, rows), jnp.int32), pltpu.VMEM((1, rows), jnp.int32),
            bf16(PLANES, PAIR), f32(PLANES, PAIR, 2, rows), bf16(others, PAIR),
            f32(SPOTS, 2, rows), f32(others, 2, rows), f32(SPOTS, rows, rows),
            f32(SPOTS, rows, features), f32(SPOTS, rows, rows), f32(SPOTS, rows, rows),
            bf16(others), bf16(others), f32(others, 2, rows), f32(others, 2, rows),
            bf16(2), bf16(2), f32(2, 2, rows), f32(2, 2, rows),
            pltpu.SemaphoreType.REGULAR, dma((3,)), dma, dma((PLANES - 1, PIECES)), dma((PLANES,)),
            dma, dma((PLANES,)), dma((PLANES,)),
            dma((2,)), dma((6,)), dma((others,)), dma, dma((2,)),
            dma((3,)), dma((2,)), dma, dma, dma, dma, dma((2, 2)), dma,
        ],
        compiler_params=pltpu.CompilerParams(
            collective_id=0, has_side_effects=True, vmem_limit_bytes=GRANT
        ),
    )(
        *[
            pltpu.with_memory_space_constraint(value, pltpu.HBM)
            for value in (embeddings, bucket_ids.reshape(1, rows), valid_rows.reshape(1, rows))
        ]
    )
    return finish(mean, best)


def on_device(embeddings, bucket_ids, slot_ids, valid_rows):
    rows = embeddings.shape[0]
    groups = lax.axis_size("wide")
    blocks = lax.axis_size("blk")
    bucket_work = blocks * (2 * rows) ** 2
    dense_work = groups * blocks * rows**2
    fits = groups % PAIR == 0 and groups == PLANES * PAIR and blocks == PAIR * PAIR and rows == 128
    if fits and dense_work <= 4 * bucket_work:
        return dense(embeddings, bucket_ids, valid_rows)
    return by_bucket(embeddings, bucket_ids, slot_ids, valid_rows)


def solution(mesh):
    in_specs = (
        P(("wide", "blk"), None),
        P(("wide", "blk")),
        P(("wide", "blk")),
        P(("wide", "blk")),
    )
    out_specs = (P(("wide", "blk"), None), P(("wide", "blk")))
    return jax.shard_map(
        on_device, mesh=mesh, in_specs=in_specs, out_specs=out_specs, check_vma=False
    )
```

```python
import functools

import jax
import jax.numpy as jnp
from jax import lax
from jax.experimental import pallas as pl
from jax.experimental.pallas import tpu as pltpu
from jax.sharding import PartitionSpec as P

sharpness = 10.0


def from_behind(value, axis, steps):
    count = lax.axis_size(axis)
    pairs = [(source, (source + steps) % count) for source in range(count)]
    return lax.ppermute(value, axis, pairs)


def unit_rows(embeddings):
    float_rows = embeddings.astype(jnp.float32)
    inverse_norm = lax.rsqrt(jnp.mean(float_rows * float_rows, axis=1, keepdims=True) + 1e-06)
    return (float_rows * inverse_norm).astype(jnp.bfloat16)


def bucket_stats(queries, query_pos, key_rows, key_flags, key_pos):
    feature_count = queries.shape[1]
    cosine = (
        lax.dot_general(
            queries, key_rows, (((1,), (1,)), ((), ())), preferred_element_type=jnp.float32
        )
        / feature_count
    )
    usable = (key_flags[None, :] > 0) & (query_pos[:, None] != key_pos[None, :])
    best_cos = jnp.max(jnp.where(usable, cosine, -1.0), axis=1)
    weights = jnp.where(usable, jnp.exp(sharpness * (cosine - 1.0)), 0.0)
    weight_total = jnp.sum(weights, axis=1)
    summed = jnp.dot(weights.astype(jnp.bfloat16), key_rows, preferred_element_type=jnp.float32)
    return (best_cos, weight_total, summed)


def by_bucket(embeddings, bucket_ids, slot_ids, valid_rows):
    unit_vectors = unit_rows(embeddings)
    row_count, feature_count = unit_vectors.shape
    groups = lax.axis_size("wide")
    blocks = lax.axis_size("blk")
    slot_count = 2 * row_count // groups
    block_rows = groups * slot_count
    cell_ids = bucket_ids * slot_count + slot_ids
    outgoing = jnp.zeros((block_rows, feature_count), jnp.bfloat16).at[cell_ids].set(unit_vectors)
    flag_rows = (
        jnp.zeros((block_rows,), jnp.bfloat16).at[cell_ids].set(valid_rows.astype(jnp.bfloat16))
    )
    arrived, arrived_flags = (
        lax.all_to_all(
            outgoing.reshape(groups, slot_count, feature_count),
            "wide",
            split_axis=0,
            concat_axis=0,
            tiled=True,
        ),
        lax.all_to_all(
            flag_rows.reshape(groups, slot_count), "wide", split_axis=0, concat_axis=0, tiled=True
        ),
    )
    queries = arrived.reshape(block_rows, feature_count)
    query_flags = arrived_flags.reshape(block_rows)
    my_block = lax.axis_index("blk")
    query_pos = my_block * block_rows + jnp.arange(block_rows, dtype=jnp.int32)

    def absorb(running, key_rows, key_flags, key_start):
        key_pos = key_start + jnp.arange(key_rows.shape[0], dtype=jnp.int32)
        best_cos, weight_total, summed = bucket_stats(
            queries, query_pos, key_rows, key_flags, key_pos
        )
        return (jnp.maximum(running[0], best_cos), running[1] + weight_total, running[2] + summed)

    initial = (
        jnp.full((block_rows,), -1.0, jnp.float32),
        jnp.zeros((block_rows,), jnp.float32),
        jnp.zeros((block_rows, feature_count), jnp.float32),
    )
    key_rows, key_flags = (queries, query_flags)
    running = absorb(initial, key_rows, key_flags, my_block * block_rows)
    for turn_index in range(1, blocks):
        key_rows, key_flags = from_behind((key_rows, key_flags), "blk", 1)
        running = absorb(
            running, key_rows, key_flags, (my_block - turn_index) % blocks * block_rows
        )
    best_cos, weight_total, summed = running
    mean_rows = ((queries.astype(jnp.float32) + summed) / (1.0 + weight_total[:, None])).astype(
        jnp.bfloat16
    )
    back_mean, back_best = (
        lax.all_to_all(
            mean_rows.reshape(groups, slot_count, feature_count),
            "wide",
            split_axis=0,
            concat_axis=0,
            tiled=True,
        ),
        lax.all_to_all(
            best_cos.astype(jnp.bfloat16).reshape(groups, slot_count),
            "wide",
            split_axis=0,
            concat_axis=0,
            tiled=True,
        ),
    )
    neighbour_mean = back_mean.reshape(block_rows, feature_count)[cell_ids]
    max_cosine = back_best.reshape(block_rows)[cell_ids]
    return (neighbour_mean, max_cosine)


PAIR = 2
PLANES = 4
SPOTS = PAIR * PAIR
PIECES = 8
GRANT = 56_240_000


def dense_kernel(
    emb_hbm, bucket_hbm, valid_hbm, mean_ref, best_ref,
    emb_ref, bucket_ref, valid_ref,
    keys, key_meta, plane, spot_meta, plane_meta, query_col, total, peak, weight,
    part_out, part_in, stat_out, stat_in, help_out, help_in, help_stat_out, help_stat_in,
    ready, load_sem, z_send, z_recv, zm_recv, c_send, c_recv, cm_recv,
    q_send, q_recv, qm_recv, f_send, f_recv,
    p_send, corner_recv, p_recv, sc_recv, s_recv, h_send, h_recv, small_send,
):
    rows, features = emb_ref.shape
    piece = rows // PIECES
    half, quarter = rows // 2, rows // 4
    halves = (pl.ds(0, half), pl.ds(half, half))
    wide, blk = lax.axis_index("wide"), lax.axis_index("blk")
    z, y = lax.div(wide, PAIR), lax.rem(wide, PAIR)
    x, core = lax.div(blk, PAIR), lax.rem(blk, PAIR)
    beside_x, beside_y, corner = 1, 2, 3

    def at(z_at, y_at, x_at, core_at):
        return (z_at * PAIR + y_at, x_at * PAIR + core_at)

    partner = at(z, y, x, 1 - core)
    x_device = at(z, y, 1 - x, core)
    y_device = at(z, 1 - y, x, core)
    inner = (z > 0) & (z < PLANES - 1)
    lower = z < PLANES // 2
    across_z = PLANES - 1 - z
    end_device = at(jnp.where(lower, 0, PLANES - 1), y, x, core)
    next_device = at(jnp.where(lower, 1, PLANES - 2), y, x, core)
    far_device = at(across_z, y, x, core)
    first_device = at(0, y, x, core)
    top_device = at(PLANES - 1, y, x, core)

    def remote(source, target, send, recv, device):
        return pltpu.make_async_remote_copy(
            src_ref=source, dst_ref=target, send_sem=send, recv_sem=recv,
            device_id=device, device_id_type=pl.DeviceIdType.MESH,
        )

    def arrived(ref, recv):
        remote(ref, ref, recv, recv, partner).wait_recv()

    def sent(ref, send):
        remote(ref, ref, send, send, partner).wait_send()

    loads = [
        pltpu.make_async_copy(source, target, load_sem.at[index])
        for index, (source, target) in enumerate(
            ((emb_hbm, emb_ref), (bucket_hbm, bucket_ref), (valid_hbm, valid_ref))
        )
    ]
    for load in loads:
        load.start()

    barrier = pltpu.get_barrier_semaphore()

    def greet(device):
        pl.semaphore_signal(barrier, inc=1, device_id=device, device_id_type=pl.DeviceIdType.MESH)

    greet(x_device)
    greet(y_device)
    greet(partner)

    @pl.when(z < PLANES - 1)
    def _():
        greet(at(z + 1, y, x, core))

    @pl.when(z == 1)
    def _():
        greet(first_device)

    @pl.when(z == 0)
    def _():
        greet(top_device)

    for load in loads:
        load.wait()
    floats = emb_ref[...].astype(jnp.float32)
    inverse = lax.rsqrt(jnp.mean(floats * floats, axis=1, keepdims=True) + 1e-06)
    unit = (floats * inverse).astype(jnp.bfloat16)
    own = jnp.where(inner, 1, 0)
    keys[own, 0] = unit
    buckets = bucket_ref[...].astype(jnp.float32)
    meta = jnp.concatenate([buckets, jnp.where(valid_ref[...] > 0, buckets, -1.0)], axis=0)
    key_meta[own, 0] = meta
    spot_meta[0] = meta

    pl.semaphore_wait(barrier, jnp.where(z == PLANES - 1, 5, 4))

    @pl.when(z >= 2)
    def _():
        pl.semaphore_signal(
            ready, inc=1, device_id=at(z - 1, y, x, core), device_id_type=pl.DeviceIdType.MESH
        )

    def column(row):
        return jnp.transpose(jnp.broadcast_to(row, (rows, rows)))

    def terms(chosen, buckets, block, metas, itself):
        cosine = lax.dot_general(
            chosen, block, (((1,), (1,)), ((), ())), preferred_element_type=jnp.float32
        ) * (1.0 / features)
        factors = []
        peaks = None
        sums = None
        for index, meta in enumerate(metas):
            usable = buckets == meta[1:2, :]
            if index == itself:
                line = lax.broadcasted_iota(jnp.int32, (rows, rows), 0)
                lane = lax.broadcasted_iota(jnp.int32, (rows, rows), 1)
                usable = usable & (line != lane)
            values = cosine[:, index * rows : (index + 1) * rows]
            best = jnp.where(usable, values, -1.0)
            factor = jnp.where(usable, jnp.exp(sharpness * (values - 1.0)), 0.0)
            factors.append(factor.astype(jnp.bfloat16))
            peaks = best if peaks is None else jnp.maximum(peaks, best)
            sums = factor if sums is None else sums + factor
        summed = jnp.dot(
            jnp.concatenate(factors, axis=1), block, preferred_element_type=jnp.float32
        )
        return peaks, sums, summed

    def stat_rows(peaks, sums):
        top = jnp.max(jnp.transpose(peaks), axis=0, keepdims=True)
        mass = jnp.sum(jnp.transpose(sums), axis=0, keepdims=True)
        return jnp.concatenate([top, mass], axis=0)

    def run(place):
        is_inner = 0 < place < PLANES - 1
        me = 1 if is_inner else 0
        slots = (3, 4, 3, 2)[place]
        last = slots - 1
        own_rows = keys.at[me, 0]

        def z_copy(slot, target, part, device):
            ref = pl.ds(part * piece, piece)
            return remote(
                keys.at[slot, 0, ref], keys.at[target, 0, ref], z_send, z_recv.at[(0, 1, 2, 1)[target], part],
                device,
            )

        def z_meta(slot, target, device):
            return remote(
                key_meta.at[slot, 0], key_meta.at[target, 0], small_send, zm_recv.at[(0, 1, 2, 1)[target]], device
            )

        def c_copy(slot, part=None):
            ref = pl.ds(0, rows) if part is None else pl.ds(part * piece, piece)
            return remote(
                keys.at[slot, 0, ref], keys.at[slot, 1, ref], c_send, c_recv.at[slot], partner
            )

        def c_meta(slot):
            return remote(
                key_meta.at[slot, 0], key_meta.at[slot, 1], small_send, cm_recv.at[slot], partner
            )

        def wait_partner(slot):
            arrived(key_meta.at[slot, 1], cm_recv.at[slot])
            arrived(keys.at[slot, 1], c_recv.at[slot])

        onward = {
            0: {0: [(0, next_device)]},
            1: {1: [(1, end_device)], 0: [(2, far_device)], 2: [(2, end_device)]},
            2: {1: [(2, far_device)], 0: [(3, far_device)], 2: [(1, end_device)]},
            3: {0: [(0, next_device)]},
        }[place]
        helps = {
            0: [],
            1: [(2, far_device, 0), (3, top_device, 1)],
            2: [(0, end_device, 0)],
            3: [(1, first_device, 0)],
        }[place]
        helpers = (1, 0, 1, 2)[place]

        def take_meta(slot):
            arrived(key_meta.at[slot, 0], zm_recv.at[(0, 1, 2, 1)[slot]])
            for target, device in onward.get(slot, ()):
                z_meta(slot, target, device).start()
            c_meta(slot).start()

        def take(slot, part):
            for step in range(PIECES // 4):
                take_piece(slot, part * (PIECES // 4) + step)

        def take_piece(slot, part):
            ref = keys.at[slot, 0, pl.ds(part * piece, piece)]
            arrived(ref, z_recv.at[(0, 1, 2, 1)[slot], part])
            for target, device in onward.get(slot, ()):
                z_copy(slot, target, part, device).start()
            c_copy(slot, part).start()

        def q_copy(source, spot, side, recv, device, send=1):
            return remote(
                source.at[halves[side]], plane.at[spot - 1, 0, halves[side]], q_send.at[send],
                q_recv.at[recv], device,
            )

        def q_arrived(spot, side, recv):
            arrived(plane.at[spot - 1, 0, halves[side]], q_recv.at[recv])

        def q_meta(source, spot, device):
            return remote(
                spot_meta.at[source], spot_meta.at[spot], small_send, qm_recv.at[spot - 1], device
            )

        def q_meta_arrived(spot):
            arrived(spot_meta.at[spot], qm_recv.at[spot - 1])

        for target, device in onward[me]:
            z_meta(me, target, device).start()
        for part in range(PIECES):
            for target, device in onward[me]:
                z_copy(me, target, part, device).start()
        q_meta(0, beside_x, x_device).start()
        q_meta(0, beside_y, y_device).start()
        q_copy(own_rows, beside_x, 0, 0, x_device, 0).start()
        q_copy(own_rows, beside_y, 1, 1, y_device, 0).start()
        c_meta(me).start()
        c_copy(me).start()
        query_col[0] = column(spot_meta[0, 0:1, :])
        sent(own_rows, q_send.at[0])
        q_copy(own_rows, beside_x, 1, 2, x_device).start()
        q_copy(own_rows, beside_y, 0, 2, y_device).start()

        def relay_q():
            q_meta_arrived(beside_x)
            q_meta(beside_x, corner, y_device).start()
            q_arrived(beside_x, 0, 0)
            q_copy(plane.at[beside_x - 1, 0], corner, 0, 3, y_device).start()
            q_meta_arrived(beside_y)
            q_arrived(beside_y, 1, 1)
            q_copy(plane.at[beside_y - 1, 0], corner, 1, 3, x_device).start()

        def pass_on(spot):
            if place > 0:
                remote(
                    plane.at[spot - 1, 0], plane.at[spot - 1, 1], f_send, f_recv.at[0], partner
                ).start()

        def finish_q(spot):
            if spot == beside_x:
                arrived(plane.at[beside_y - 1, 0], q_recv.at[2])
            elif spot == corner:
                q_meta_arrived(corner)
                arrived(plane.at[corner - 1, 0], q_recv.at[3])
                if place > 0:
                    remote(
                        spot_meta.at[1:SPOTS], plane_meta, small_send, f_recv.at[1], partner
                    ).start()
            pass_on(spot)
            query_col[spot] = column(spot_meta[spot, 0:1, :])

        def batch(spot, first, end):
            chosen = keys[me, 0] if spot == 0 else plane[spot - 1, 0]
            count = end - first
            itself = (me - first) * PAIR if spot == 0 and first <= me < end else None
            return terms(
                chosen,
                query_col[spot],
                keys[first:end].reshape(count * PAIR * rows, features),
                [key_meta[slot, side] for slot in range(first, end) for side in range(PAIR)],
                itself,
            )

        def early(spot):
            peak[spot], weight[spot], total[spot] = batch(spot, 0, last)

        def joint(first, end):
            block = keys[first:end].reshape((end - first) * PAIR * rows, features)
            metas = [key_meta[slot, side] for slot in range(first, end) for side in range(PAIR)]

            def of(begin, stop):
                count = (stop - begin) * rows
                shape = (stop - begin, rows)
                peaks, sums, summed = terms(
                    plane[begin - 1 : stop - 1, 0].reshape(count, features),
                    query_col[begin:stop].reshape(count, rows),
                    block, metas, None,
                )
                return (
                    peaks.reshape(*shape, rows), sums.reshape(*shape, rows),
                    summed.reshape(*shape, features),
                )

            return of

        def early_others():
            peak[1:SPOTS], weight[1:SPOTS], total[1:SPOTS] = joint(0, last)(1, SPOTS)

        def assist(turn):
            slot, device, index = helps[turn]
            if turn == 0:
                arrived(plane_meta, f_recv.at[1])
                arrived(plane.at[:, 1], f_recv.at[0])
            chosen = keys[slot, 0]
            buckets = column(key_meta[slot, 0, 0:1, :])
            near = terms(
                chosen, buckets, keys[me].reshape(PAIR * rows, features),
                [key_meta[me, side] for side in range(PAIR)], None,
            )
            wider = terms(
                chosen, buckets, plane[...].reshape((SPOTS - 1) * PAIR * rows, features),
                [ref[spot] for spot in range(SPOTS - 1) for ref in (spot_meta.at[1:SPOTS], plane_meta)],
                None,
            )
            help_out[turn] = (near[2] + wider[2]).astype(jnp.bfloat16)
            remote(
                help_out.at[turn], help_in.at[index], h_send, h_recv.at[index, 0], device
            ).start()
            help_stat_out[turn] = stat_rows(jnp.maximum(near[0], wider[0]), near[1] + wider[1])
            remote(
                help_stat_out.at[turn], help_stat_in.at[index], small_send, h_recv.at[index, 1],
                device,
            ).start()

        def take_all(*order):
            for slot, part in order:
                take(slot, part)

        if place == 0:
            relay_q()
            take_meta(1)
            take_all((1, 0), (1, 1), (1, 2), (1, 3))
            finish_q(beside_x)
            finish_q(beside_y)
            wait_partner(0)
            wait_partner(1)
            early(0)
            take_meta(2)
            take(2, 0)
            finish_q(corner)
            early_others()
            take_all((2, 1), (2, 2), (2, 3))
        elif place == 1:
            pl.semaphore_wait(ready, 1)
            take_meta(0)
            take(0, 0)
            take_meta(2)
            take_all((0, 1), (2, 0))
            relay_q()
            take_all((0, 2), (2, 1), (0, 3), (2, 2), (2, 3))
            finish_q(beside_x)
            finish_q(beside_y)
            for slot in range(last):
                wait_partner(slot)
            early(0)
            take_meta(3)
            take(3, 0)
            finish_q(corner)
            early_others()
            take_all((3, 1), (3, 2), (3, 3))
            assist(0)
        elif place == 2:
            take_meta(0)
            take(0, 0)
            pl.semaphore_wait(ready, 1)
            take_meta(2)
            relay_q()
            take_all((2, 0), (0, 1), (2, 1), (0, 2), (2, 2), (0, 3), (2, 3))
            finish_q(beside_x)
            finish_q(beside_y)
            for slot in range(last):
                wait_partner(slot)
            finish_q(corner)
        else:
            relay_q()
            finish_q(beside_x)
            finish_q(beside_y)
            wait_partner(0)
            take_meta(1)
            take(1, 0)
            early(0)
            take(1, 1)
            finish_q(corner)
            early_others()
            take_all((1, 2), (1, 3))
            assist(0)

        def one_side(side):
            return terms(
                plane[corner - 1, 0], query_col[corner], keys[last, side], [key_meta[last, side]], None
            )

        def corner_with(terms_of):
            peaks, sums, summed = terms_of
            return (
                jnp.maximum(peak[corner], peaks), weight[corner] + sums, total[corner] + summed
            )

        if place == 0:
            peak[corner], weight[corner], total[corner] = corner_with(one_side(0))
        wait_partner(last)

        def p_copy(spot, ref):
            return remote(
                part_out.at[spot - 1, ref], part_in.at[spot - 1, ref],
                p_send.at[1], p_recv, x_device if spot == beside_x else y_device,
            )

        def corner_copy(side, turn):
            ref = pl.ds(side * half + turn * quarter, quarter)
            return remote(
                part_out.at[corner - 1, ref], part_in.at[corner - 1, ref],
                p_send.at[2 * turn], corner_recv.at[side, turn], (x_device, y_device)[side],
            )

        def s_copy(spot, device, recv):
            return remote(stat_out.at[spot - 1], stat_in.at[spot - 1], small_send, recv, device)

        begun = () if place == 2 else (0, 1, 2, 3)

        def final(spot):
            if spot not in begun:
                return batch(spot, 0, slots)
            peaks, sums, summed = batch(spot, last, slots)
            return jnp.maximum(peak[spot], peaks), weight[spot] + sums, total[spot] + summed

        def send_stats(spot, peaks, sums):
            stat_out[spot - 1] = stat_rows(peaks, sums)
            s_copy(spot, x_device, sc_recv if spot == corner else s_recv).start()

        peaks, sums, summed = corner_with(one_side(1)) if place == 0 else final(corner)
        part_out[corner - 1] = summed.astype(jnp.bfloat16)
        for turn in range(2):
            for side in range(2):
                corner_copy(side, turn).start()
        send_stats(corner, peaks, sums)
        if place == 2:
            assist(0)
        both = (beside_x, beside_y)
        peaks, sums, summed = joint(0 if place == 2 else last, slots)(1, 3)
        finals = [(peaks[index], sums[index], summed[index]) for index in range(2)]
        if place != 2:
            finals = [
                (jnp.maximum(peak[spot], top), weight[spot] + mass, total[spot] + whole)
                for spot, (top, mass, whole) in zip(both, finals)
            ]
        for spot, side, (peaks, sums, summed) in zip(both, (0, 1), finals):
            total[spot] = summed
            part_out[spot - 1, halves[side]] = summed[side * half : (side + 1) * half].astype(jnp.bfloat16)
            if spot == beside_x:
                send_stats(spot, peaks, sums)
            else:
                y_stats = stat_rows(peaks, sums)
        def own_final():
            peaks, sums, summed = final(0)
            total[0] = summed + keys[me, 0].astype(jnp.float32)
            return stat_rows(peaks, sums)

        if place == 1:
            assist(1)
        else:
            own_stats = own_final()
        sent(part_out.at[corner - 1, halves[0]], p_send.at[0])
        for spot, side in zip(both, (0, 1)):
            p_copy(spot, halves[side]).start()
        if place == 1:
            own_stats = own_final()
        arrived(stat_in.at[corner - 1], sc_recv)
        stat_out[beside_y - 1] = jnp.concatenate(
            [
                jnp.maximum(y_stats[0:1], stat_in[corner - 1, 0:1]),
                y_stats[1:2] + stat_in[corner - 1, 1:2],
            ],
            axis=0,
        )
        s_copy(beside_y, y_device, s_recv).start()
        for turn in range(2):
            for spot, side in ((beside_x, 1), (beside_y, 0)):
                ref = pl.ds(side * half + turn * quarter, quarter)
                arrived(part_in.at[corner - 1, ref], corner_recv.at[side, turn])
                part_out[spot - 1, ref] = (
                    total[spot, ref] + part_in[corner - 1, ref].astype(jnp.float32)
                ).astype(jnp.bfloat16)
                p_copy(spot, ref).start()

        top, mass = own_stats[0:1], own_stats[1:2]
        for index in range(helpers):
            arrived(help_stat_in.at[index], h_recv.at[index, 1])
            arrived(help_in.at[index], h_recv.at[index, 0])
            top = jnp.maximum(top, help_stat_in[index, 0:1])
            mass = mass + help_stat_in[index, 1:2]
            total[0] += help_in[index].astype(jnp.float32)
        hops = sum(len(ways) for ways in onward.values())
        sent(keys.at[0:hops, 0], z_send)
        sent(keys.at[0:slots, 0], c_send)
        sent(plane.at[0 : corner - 1, 0], q_send.at[1])
        sent(part_out.at[corner - 1, halves[0]], p_send.at[2])
        pairs = hops + slots + 3 + 3 + (3 if place > 0 else 0) + len(helps)
        sent(peak.at[0, pl.ds(0, 2 * pairs)], small_send)
        if place > 0:
            sent(plane.at[:, 0], f_send)
            sent(help_out.at[0 : len(helps)], h_send)

        arrived(stat_in.at[0 : corner - 1], s_recv)
        for spot in (beside_x, beside_y):
            top = jnp.maximum(top, stat_in[spot - 1, 0:1])
            mass = mass + stat_in[spot - 1, 1:2]
        best_ref[...] = top
        below = column(1.0 + mass)[:, 0:1]
        arrived(part_in.at[0 : corner - 1], p_recv)
        result = total[0]
        for spot in (beside_x, beside_y):
            result = result + part_in[spot - 1].astype(jnp.float32)
        mean_ref[...] = (result / below).astype(jnp.bfloat16)

        sent(part_out.at[0 : corner - 1], p_send.at[1])

    for place in range(PLANES):
        pl.when(z == place)(functools.partial(run, place))


def finish_kernel(mean_ref, best_ref, mean_out, best_out, line, sem):
    line[...] = best_ref[0].astype(jnp.bfloat16)
    copies = [
        pltpu.make_async_copy(mean_ref, mean_out, sem.at[0]),
        pltpu.make_async_copy(line, best_out, sem.at[1]),
    ]
    for copy in copies:
        copy.start()
    for copy in copies:
        copy.wait()


def finish(mean, best):
    rows, features = mean.shape
    vmem = pl.BlockSpec(memory_space=pltpu.VMEM)
    hbm = pl.BlockSpec(memory_space=pltpu.HBM)
    return pl.pallas_call(
        finish_kernel,
        out_shape=(
            jax.ShapeDtypeStruct((rows, features), jnp.bfloat16),
            jax.ShapeDtypeStruct((rows,), jnp.bfloat16),
        ),
        in_specs=[vmem, vmem],
        out_specs=(hbm, hbm),
        scratch_shapes=[pltpu.VMEM((rows,), jnp.bfloat16), pltpu.SemaphoreType.DMA((2,))],
        compiler_params=pltpu.CompilerParams(vmem_limit_bytes=4_000_000),
    )(mean, best)


def dense(embeddings, bucket_ids, valid_rows):
    rows, features = embeddings.shape
    dma = pltpu.SemaphoreType.DMA
    vmem = pl.BlockSpec(memory_space=pltpu.VMEM)
    others = SPOTS - 1

    def bf16(*shape):
        return pltpu.VMEM((*shape, rows, features), jnp.bfloat16)

    def f32(*shape):
        return pltpu.VMEM(shape, jnp.float32)

    mean, best = pl.pallas_call(
        dense_kernel,
        out_shape=(
            jax.ShapeDtypeStruct((rows, features), jnp.bfloat16),
            jax.ShapeDtypeStruct((1, rows), jnp.float32),
        ),
        in_specs=[pl.BlockSpec(memory_space=pltpu.HBM)] * 3,
        out_specs=(vmem, vmem),
        scratch_shapes=[
            bf16(), pltpu.VMEM((1, rows), jnp.int32), pltpu.VMEM((1, rows), jnp.int32),
            bf16(PLANES, PAIR), f32(PLANES, PAIR, 2, rows), bf16(others, PAIR),
            f32(SPOTS, 2, rows), f32(others, 2, rows), f32(SPOTS, rows, rows),
            f32(SPOTS, rows, features), f32(SPOTS, rows, rows), f32(SPOTS, rows, rows),
            bf16(others), bf16(others), f32(others, 2, rows), f32(others, 2, rows),
            bf16(2), bf16(2), f32(2, 2, rows), f32(2, 2, rows),
            pltpu.SemaphoreType.REGULAR, dma((3,)), dma, dma((PLANES - 1, PIECES)), dma((PLANES - 1,)),
            dma, dma((PLANES,)), dma((PLANES,)),
            dma((2,)), dma((4,)), dma((others,)), dma, dma((2,)),
            dma((3,)), dma((2, 2)), dma, dma, dma, dma, dma((2, 2)), dma,
        ],
        compiler_params=pltpu.CompilerParams(
            collective_id=0, has_side_effects=True, vmem_limit_bytes=GRANT
        ),
    )(
        *[
            pltpu.with_memory_space_constraint(value, pltpu.HBM)
            for value in (embeddings, bucket_ids.reshape(1, rows), valid_rows.reshape(1, rows))
        ]
    )
    return finish(mean, best)


def on_device(embeddings, bucket_ids, slot_ids, valid_rows):
    rows = embeddings.shape[0]
    groups = lax.axis_size("wide")
    blocks = lax.axis_size("blk")
    bucket_work = blocks * (2 * rows) ** 2
    dense_work = groups * blocks * rows**2
    fits = groups % PAIR == 0 and groups == PLANES * PAIR and blocks == PAIR * PAIR and rows == 128
    if fits and dense_work <= 4 * bucket_work:
        return dense(embeddings, bucket_ids, valid_rows)
    return by_bucket(embeddings, bucket_ids, slot_ids, valid_rows)


def solution(mesh):
    in_specs = (
        P(("wide", "blk"), None),
        P(("wide", "blk")),
        P(("wide", "blk")),
        P(("wide", "blk")),
    )
    out_specs = (P(("wide", "blk"), None), P(("wide", "blk")))
    return jax.shard_map(
        on_device, mesh=mesh, in_specs=in_specs, out_specs=out_specs, check_vma=False
    )
```

```python
import functools

import jax
import jax.numpy as jnp
from jax import lax
from jax.experimental import pallas as pl
from jax.experimental.pallas import tpu as pltpu
from jax.sharding import PartitionSpec as P

sharpness = 10.0


def from_behind(value, axis, steps):
    count = lax.axis_size(axis)
    pairs = [(source, (source + steps) % count) for source in range(count)]
    return lax.ppermute(value, axis, pairs)


def unit_rows(embeddings):
    float_rows = embeddings.astype(jnp.float32)
    inverse_norm = lax.rsqrt(jnp.mean(float_rows * float_rows, axis=1, keepdims=True) + 1e-06)
    return (float_rows * inverse_norm).astype(jnp.bfloat16)


def bucket_stats(queries, query_pos, key_rows, key_flags, key_pos):
    feature_count = queries.shape[1]
    cosine = (
        lax.dot_general(
            queries, key_rows, (((1,), (1,)), ((), ())), preferred_element_type=jnp.float32
        )
        / feature_count
    )
    usable = (key_flags[None, :] > 0) & (query_pos[:, None] != key_pos[None, :])
    best_cos = jnp.max(jnp.where(usable, cosine, -1.0), axis=1)
    weights = jnp.where(usable, jnp.exp(sharpness * (cosine - 1.0)), 0.0)
    weight_total = jnp.sum(weights, axis=1)
    summed = jnp.dot(weights.astype(jnp.bfloat16), key_rows, preferred_element_type=jnp.float32)
    return (best_cos, weight_total, summed)


def by_bucket(embeddings, bucket_ids, slot_ids, valid_rows):
    unit_vectors = unit_rows(embeddings)
    row_count, feature_count = unit_vectors.shape
    groups = lax.axis_size("wide")
    blocks = lax.axis_size("blk")
    slot_count = 2 * row_count // groups
    block_rows = groups * slot_count
    cell_ids = bucket_ids * slot_count + slot_ids
    outgoing = jnp.zeros((block_rows, feature_count), jnp.bfloat16).at[cell_ids].set(unit_vectors)
    flag_rows = (
        jnp.zeros((block_rows,), jnp.bfloat16).at[cell_ids].set(valid_rows.astype(jnp.bfloat16))
    )
    arrived, arrived_flags = (
        lax.all_to_all(
            outgoing.reshape(groups, slot_count, feature_count),
            "wide",
            split_axis=0,
            concat_axis=0,
            tiled=True,
        ),
        lax.all_to_all(
            flag_rows.reshape(groups, slot_count), "wide", split_axis=0, concat_axis=0, tiled=True
        ),
    )
    queries = arrived.reshape(block_rows, feature_count)
    query_flags = arrived_flags.reshape(block_rows)
    my_block = lax.axis_index("blk")
    query_pos = my_block * block_rows + jnp.arange(block_rows, dtype=jnp.int32)

    def absorb(running, key_rows, key_flags, key_start):
        key_pos = key_start + jnp.arange(key_rows.shape[0], dtype=jnp.int32)
        best_cos, weight_total, summed = bucket_stats(
            queries, query_pos, key_rows, key_flags, key_pos
        )
        return (jnp.maximum(running[0], best_cos), running[1] + weight_total, running[2] + summed)

    initial = (
        jnp.full((block_rows,), -1.0, jnp.float32),
        jnp.zeros((block_rows,), jnp.float32),
        jnp.zeros((block_rows, feature_count), jnp.float32),
    )
    key_rows, key_flags = (queries, query_flags)
    running = absorb(initial, key_rows, key_flags, my_block * block_rows)
    for turn_index in range(1, blocks):
        key_rows, key_flags = from_behind((key_rows, key_flags), "blk", 1)
        running = absorb(
            running, key_rows, key_flags, (my_block - turn_index) % blocks * block_rows
        )
    best_cos, weight_total, summed = running
    mean_rows = ((queries.astype(jnp.float32) + summed) / (1.0 + weight_total[:, None])).astype(
        jnp.bfloat16
    )
    back_mean, back_best = (
        lax.all_to_all(
            mean_rows.reshape(groups, slot_count, feature_count),
            "wide",
            split_axis=0,
            concat_axis=0,
            tiled=True,
        ),
        lax.all_to_all(
            best_cos.astype(jnp.bfloat16).reshape(groups, slot_count),
            "wide",
            split_axis=0,
            concat_axis=0,
            tiled=True,
        ),
    )
    neighbour_mean = back_mean.reshape(block_rows, feature_count)[cell_ids]
    max_cosine = back_best.reshape(block_rows)[cell_ids]
    return (neighbour_mean, max_cosine)


PAIR = 2
PLANES = 4
SPOTS = PAIR * PAIR
PIECES = 8
GRANT = 56_240_000


def dense_kernel(
    emb_hbm, bucket_hbm, valid_hbm, mean_ref, best_ref,
    emb_ref, bucket_ref, valid_ref,
    keys, key_meta, plane, spot_meta, plane_meta, query_col, total, peak, weight,
    part_out, part_in, stat_out, stat_in, help_out, help_in, help_stat_out, help_stat_in,
    ready, load_sem, z_send, z_recv, zm_recv, c_send, c_recv, cm_recv,
    q_send, q_recv, qm_recv, f_send, f_recv,
    p_send, corner_recv, p_recv, sc_recv, s_recv, h_send, h_recv, small_send,
):
    rows, features = emb_ref.shape
    piece = rows // PIECES
    half, quarter = rows // 2, rows // 4
    halves = (pl.ds(0, half), pl.ds(half, half))
    wide, blk = lax.axis_index("wide"), lax.axis_index("blk")
    z, y = lax.div(wide, PAIR), lax.rem(wide, PAIR)
    x, core = lax.div(blk, PAIR), lax.rem(blk, PAIR)
    beside_x, beside_y, corner = 1, 2, 3

    def at(z_at, y_at, x_at, core_at):
        return (z_at * PAIR + y_at, x_at * PAIR + core_at)

    partner = at(z, y, x, 1 - core)
    x_device = at(z, y, 1 - x, core)
    y_device = at(z, 1 - y, x, core)
    inner = (z > 0) & (z < PLANES - 1)
    lower = z < PLANES // 2
    across_z = PLANES - 1 - z
    end_device = at(jnp.where(lower, 0, PLANES - 1), y, x, core)
    next_device = at(jnp.where(lower, 1, PLANES - 2), y, x, core)
    far_device = at(across_z, y, x, core)
    first_device = at(0, y, x, core)
    top_device = at(PLANES - 1, y, x, core)

    def remote(source, target, send, recv, device):
        return pltpu.make_async_remote_copy(
            src_ref=source, dst_ref=target, send_sem=send, recv_sem=recv,
            device_id=device, device_id_type=pl.DeviceIdType.MESH,
        )

    def arrived(ref, recv):
        remote(ref, ref, recv, recv, partner).wait_recv()

    def sent(ref, send):
        remote(ref, ref, send, send, partner).wait_send()

    loads = [
        pltpu.make_async_copy(source, target, load_sem.at[index])
        for index, (source, target) in enumerate(
            ((emb_hbm, emb_ref), (bucket_hbm, bucket_ref), (valid_hbm, valid_ref))
        )
    ]
    for load in loads:
        load.start()

    barrier = pltpu.get_barrier_semaphore()

    def greet(device):
        pl.semaphore_signal(barrier, inc=1, device_id=device, device_id_type=pl.DeviceIdType.MESH)

    greet(x_device)
    greet(y_device)
    greet(partner)

    @pl.when(z < PLANES - 1)
    def _():
        greet(at(z + 1, y, x, core))

    @pl.when(z == 1)
    def _():
        greet(first_device)

    @pl.when(z == 0)
    def _():
        greet(top_device)

    for load in loads:
        load.wait()
    floats = emb_ref[...].astype(jnp.float32)
    inverse = lax.rsqrt(jnp.mean(floats * floats, axis=1, keepdims=True) + 1e-06)
    unit = (floats * inverse).astype(jnp.bfloat16)
    own = jnp.where(inner, 1, 0)
    keys[own, 0] = unit
    buckets = bucket_ref[...].astype(jnp.float32)
    meta = jnp.concatenate([buckets, jnp.where(valid_ref[...] > 0, buckets, -1.0)], axis=0)
    key_meta[own, 0] = meta
    spot_meta[0] = meta

    pl.semaphore_wait(barrier, jnp.where(z == PLANES - 1, 5, 4))

    @pl.when(z >= 2)
    def _():
        pl.semaphore_signal(
            ready, inc=1, device_id=at(z - 1, y, x, core), device_id_type=pl.DeviceIdType.MESH
        )

    def column(row):
        return jnp.transpose(jnp.broadcast_to(row, (rows, rows)))

    def terms(chosen, buckets, block, metas, itself):
        cosine = lax.dot_general(
            chosen, block, (((1,), (1,)), ((), ())), preferred_element_type=jnp.float32
        ) * (1.0 / features)
        factors = []
        peaks = None
        sums = None
        for index, meta in enumerate(metas):
            usable = buckets == meta[1:2, :]
            if index == itself:
                line = lax.broadcasted_iota(jnp.int32, (rows, rows), 0)
                lane = lax.broadcasted_iota(jnp.int32, (rows, rows), 1)
                usable = usable & (line != lane)
            values = cosine[:, index * rows : (index + 1) * rows]
            best = jnp.where(usable, values, -1.0)
            factor = jnp.where(usable, jnp.exp(sharpness * (values - 1.0)), 0.0)
            factors.append(factor.astype(jnp.bfloat16))
            peaks = best if peaks is None else jnp.maximum(peaks, best)
            sums = factor if sums is None else sums + factor
        summed = jnp.dot(
            jnp.concatenate(factors, axis=1), block, preferred_element_type=jnp.float32
        )
        return peaks, sums, summed

    def stat_rows(peaks, sums):
        top = jnp.max(jnp.transpose(peaks), axis=0, keepdims=True)
        mass = jnp.sum(jnp.transpose(sums), axis=0, keepdims=True)
        return jnp.concatenate([top, mass], axis=0)

    def run(place):
        is_inner = 0 < place < PLANES - 1
        me = 1 if is_inner else 0
        slots = (3, 4, 3, 2)[place]
        last = slots - 1
        own_rows = keys.at[me, 0]

        def z_copy(slot, target, part, device):
            ref = pl.ds(part * piece, piece)
            return remote(
                keys.at[slot, 0, ref], keys.at[target, 0, ref], z_send, z_recv.at[(0, 1, 2, 1)[target], part],
                device,
            )

        def z_meta(slot, target, device):
            return remote(
                key_meta.at[slot, 0], key_meta.at[target, 0], small_send, zm_recv.at[(0, 1, 2, 1)[target]], device
            )

        def c_copy(slot, part=None):
            ref = pl.ds(0, rows) if part is None else pl.ds(part * piece, piece)
            return remote(
                keys.at[slot, 0, ref], keys.at[slot, 1, ref], c_send, c_recv.at[slot], partner
            )

        def c_meta(slot):
            return remote(
                key_meta.at[slot, 0], key_meta.at[slot, 1], small_send, cm_recv.at[slot], partner
            )

        def wait_partner(slot):
            arrived(key_meta.at[slot, 1], cm_recv.at[slot])
            arrived(keys.at[slot, 1], c_recv.at[slot])

        onward = {
            0: {0: [(0, next_device)]},
            1: {1: [(1, end_device)], 0: [(2, far_device)], 2: [(2, end_device)]},
            2: {1: [(2, far_device)], 0: [(3, far_device)], 2: [(1, end_device)]},
            3: {0: [(0, next_device)]},
        }[place]
        helps = {
            0: [],
            1: [(2, far_device, 0), (3, top_device, 1)],
            2: [(0, end_device, 0)],
            3: [(1, first_device, 0)],
        }[place]
        helpers = (1, 0, 1, 2)[place]

        def take_meta(slot):
            arrived(key_meta.at[slot, 0], zm_recv.at[(0, 1, 2, 1)[slot]])
            for target, device in onward.get(slot, ()):
                z_meta(slot, target, device).start()
            c_meta(slot).start()

        def take(slot, part):
            for step in range(PIECES // 4):
                take_piece(slot, part * (PIECES // 4) + step)

        def take_piece(slot, part):
            ref = keys.at[slot, 0, pl.ds(part * piece, piece)]
            arrived(ref, z_recv.at[(0, 1, 2, 1)[slot], part])
            for target, device in onward.get(slot, ()):
                z_copy(slot, target, part, device).start()
            c_copy(slot, part).start()

        def q_copy(source, spot, side, recv, device, send=1):
            return remote(
                source.at[halves[side]], plane.at[spot - 1, 0, halves[side]], q_send.at[send],
                q_recv.at[recv], device,
            )

        def q_arrived(spot, side, recv):
            arrived(plane.at[spot - 1, 0, halves[side]], q_recv.at[recv])

        def q_meta(source, spot, device):
            return remote(
                spot_meta.at[source], spot_meta.at[spot], small_send, qm_recv.at[spot - 1], device
            )

        def q_meta_arrived(spot):
            arrived(spot_meta.at[spot], qm_recv.at[spot - 1])

        for target, device in onward[me]:
            z_meta(me, target, device).start()
        for part in range(PIECES):
            for target, device in onward[me]:
                z_copy(me, target, part, device).start()
        q_meta(0, beside_x, x_device).start()
        q_meta(0, beside_y, y_device).start()
        q_copy(own_rows, beside_x, 0, 0, x_device, 0).start()
        q_copy(own_rows, beside_y, 1, 1, y_device, 0).start()
        c_meta(me).start()
        c_copy(me).start()
        query_col[0] = column(spot_meta[0, 0:1, :])
        sent(own_rows, q_send.at[0])
        q_copy(own_rows, beside_x, 1, 2, x_device).start()
        q_copy(own_rows, beside_y, 0, 2, y_device).start()

        def relay_q():
            q_meta_arrived(beside_x)
            q_meta(beside_x, corner, y_device).start()
            q_arrived(beside_x, 0, 0)
            q_copy(plane.at[beside_x - 1, 0], corner, 0, 3, y_device).start()
            q_meta_arrived(beside_y)
            q_arrived(beside_y, 1, 1)
            q_copy(plane.at[beside_y - 1, 0], corner, 1, 3, x_device).start()

        def pass_on(spot):
            if place > 0:
                remote(
                    plane.at[spot - 1, 0], plane.at[spot - 1, 1], f_send, f_recv.at[0], partner
                ).start()

        def finish_q(spot):
            if spot == beside_x:
                arrived(plane.at[beside_y - 1, 0], q_recv.at[2])
            elif spot == corner:
                q_meta_arrived(corner)
                arrived(plane.at[corner - 1, 0], q_recv.at[3])
                if place > 0:
                    remote(
                        spot_meta.at[1:SPOTS], plane_meta, small_send, f_recv.at[1], partner
                    ).start()
            pass_on(spot)
            query_col[spot] = column(spot_meta[spot, 0:1, :])

        def batch(spot, first, end):
            chosen = keys[me, 0] if spot == 0 else plane[spot - 1, 0]
            count = end - first
            itself = (me - first) * PAIR if spot == 0 and first <= me < end else None
            return terms(
                chosen,
                query_col[spot],
                keys[first:end].reshape(count * PAIR * rows, features),
                [key_meta[slot, side] for slot in range(first, end) for side in range(PAIR)],
                itself,
            )

        def early(spot):
            peak[spot], weight[spot], total[spot] = batch(spot, 0, last)

        def joint(first, end):
            block = keys[first:end].reshape((end - first) * PAIR * rows, features)
            metas = [key_meta[slot, side] for slot in range(first, end) for side in range(PAIR)]

            def of(begin, stop):
                count = (stop - begin) * rows
                shape = (stop - begin, rows)
                peaks, sums, summed = terms(
                    plane[begin - 1 : stop - 1, 0].reshape(count, features),
                    query_col[begin:stop].reshape(count, rows),
                    block, metas, None,
                )
                return (
                    peaks.reshape(*shape, rows), sums.reshape(*shape, rows),
                    summed.reshape(*shape, features),
                )

            return of

        def early_others():
            peak[1:SPOTS], weight[1:SPOTS], total[1:SPOTS] = joint(0, last)(1, SPOTS)

        def assist(turn):
            slot, device, index = helps[turn]
            if turn == 0:
                arrived(plane_meta, f_recv.at[1])
                arrived(plane.at[:, 1], f_recv.at[0])
            chosen = keys[slot, 0]
            buckets = column(key_meta[slot, 0, 0:1, :])
            near = terms(
                chosen, buckets, keys[me].reshape(PAIR * rows, features),
                [key_meta[me, side] for side in range(PAIR)], None,
            )
            wider = terms(
                chosen, buckets, plane[...].reshape((SPOTS - 1) * PAIR * rows, features),
                [ref[spot] for spot in range(SPOTS - 1) for ref in (spot_meta.at[1:SPOTS], plane_meta)],
                None,
            )
            help_out[turn] = (near[2] + wider[2]).astype(jnp.bfloat16)
            remote(
                help_out.at[turn], help_in.at[index], h_send, h_recv.at[index, 0], device
            ).start()
            help_stat_out[turn] = stat_rows(jnp.maximum(near[0], wider[0]), near[1] + wider[1])
            remote(
                help_stat_out.at[turn], help_stat_in.at[index], small_send, h_recv.at[index, 1],
                device,
            ).start()

        def take_all(*order):
            for slot, part in order:
                take(slot, part)

        if place == 0:
            relay_q()
            take_meta(1)
            take_all((1, 0), (1, 1), (1, 2), (1, 3))
            finish_q(beside_x)
            finish_q(beside_y)
            wait_partner(0)
            wait_partner(1)
            early(0)
            take_meta(2)
            take(2, 0)
            finish_q(corner)
            early_others()
            take_all((2, 1), (2, 2), (2, 3))
        elif place == 1:
            pl.semaphore_wait(ready, 1)
            take_meta(0)
            take(0, 0)
            take_meta(2)
            take_all((0, 1), (2, 0))
            relay_q()
            take_all((0, 2), (2, 1), (0, 3), (2, 2), (2, 3))
            finish_q(beside_x)
            finish_q(beside_y)
            for slot in range(last):
                wait_partner(slot)
            early(0)
            take_meta(3)
            take(3, 0)
            finish_q(corner)
            early_others()
            take_all((3, 1), (3, 2), (3, 3))
            assist(0)
        elif place == 2:
            take_meta(0)
            take(0, 0)
            pl.semaphore_wait(ready, 1)
            take_meta(2)
            relay_q()
            take_all((2, 0), (0, 1), (2, 1), (0, 2), (2, 2), (0, 3), (2, 3))
            finish_q(beside_x)
            finish_q(beside_y)
            for slot in range(last):
                wait_partner(slot)
            finish_q(corner)
        else:
            relay_q()
            finish_q(beside_x)
            finish_q(beside_y)
            wait_partner(0)
            take_meta(1)
            take(1, 0)
            early(0)
            take(1, 1)
            finish_q(corner)
            early_others()
            take_all((1, 2), (1, 3))
            assist(0)

        def one_side(side):
            return terms(
                plane[corner - 1, 0], query_col[corner], keys[last, side], [key_meta[last, side]], None
            )

        def corner_with(terms_of):
            peaks, sums, summed = terms_of
            return (
                jnp.maximum(peak[corner], peaks), weight[corner] + sums, total[corner] + summed
            )

        if place == 0:
            peak[corner], weight[corner], total[corner] = corner_with(one_side(0))
        wait_partner(last)

        def p_copy(spot, ref):
            return remote(
                part_out.at[spot - 1, ref], part_in.at[spot - 1, ref],
                p_send.at[1], p_recv, x_device if spot == beside_x else y_device,
            )

        def corner_copy(side, turn):
            ref = pl.ds(side * half + turn * quarter, quarter)
            return remote(
                part_out.at[corner - 1, ref], part_in.at[corner - 1, ref],
                p_send.at[2 * turn], corner_recv.at[side, turn], (x_device, y_device)[side],
            )

        def s_copy(spot, device, recv):
            return remote(stat_out.at[spot - 1], stat_in.at[spot - 1], small_send, recv, device)

        begun = () if place == 2 else (0, 1, 2, 3)

        def final(spot):
            if spot not in begun:
                return batch(spot, 0, slots)
            peaks, sums, summed = batch(spot, last, slots)
            return jnp.maximum(peak[spot], peaks), weight[spot] + sums, total[spot] + summed

        def send_stats(spot, peaks, sums):
            stat_out[spot - 1] = stat_rows(peaks, sums)
            s_copy(spot, x_device, sc_recv if spot == corner else s_recv).start()

        peaks, sums, summed = corner_with(one_side(1)) if place == 0 else final(corner)
        part_out[corner - 1] = summed.astype(jnp.bfloat16)
        for turn in range(2):
            for side in range(2):
                corner_copy(side, turn).start()
        send_stats(corner, peaks, sums)
        if place == 2:
            assist(0)
        both = (beside_x, beside_y)
        peaks, sums, summed = joint(0 if place == 2 else last, slots)(1, 3)
        finals = [(peaks[index], sums[index], summed[index]) for index in range(2)]
        if place != 2:
            finals = [
                (jnp.maximum(peak[spot], top), weight[spot] + mass, total[spot] + whole)
                for spot, (top, mass, whole) in zip(both, finals)
            ]
        for spot, side, (peaks, sums, summed) in zip(both, (0, 1), finals):
            total[spot] = summed
            part_out[spot - 1, halves[side]] = summed[side * half : (side + 1) * half].astype(jnp.bfloat16)
            if spot == beside_x:
                send_stats(spot, peaks, sums)
            else:
                y_stats = stat_rows(peaks, sums)
        def own_final():
            peaks, sums, summed = final(0)
            total[0] = summed + keys[me, 0].astype(jnp.float32)
            return stat_rows(peaks, sums)

        if place == 1:
            assist(1)
        else:
            own_stats = own_final()
        sent(part_out.at[corner - 1, halves[0]], p_send.at[0])
        for spot, side in zip(both, (0, 1)):
            p_copy(spot, halves[side]).start()
        if place == 1:
            own_stats = own_final()
        for turn in range(2):
            for spot, side in ((beside_x, 1), (beside_y, 0)):
                ref = pl.ds(side * half + turn * quarter, quarter)
                arrived(part_in.at[corner - 1, ref], corner_recv.at[side, turn])
                part_out[spot - 1, ref] = (
                    total[spot, ref] + part_in[corner - 1, ref].astype(jnp.float32)
                ).astype(jnp.bfloat16)
                p_copy(spot, ref).start()
            if turn == 0:
                arrived(stat_in.at[corner - 1], sc_recv)
                stat_out[beside_y - 1] = jnp.concatenate(
                    [
                        jnp.maximum(y_stats[0:1], stat_in[corner - 1, 0:1]),
                        y_stats[1:2] + stat_in[corner - 1, 1:2],
                    ],
                    axis=0,
                )
                s_copy(beside_y, y_device, s_recv).start()

        top, mass = own_stats[0:1], own_stats[1:2]
        for index in range(helpers):
            arrived(help_stat_in.at[index], h_recv.at[index, 1])
            arrived(help_in.at[index], h_recv.at[index, 0])
            top = jnp.maximum(top, help_stat_in[index, 0:1])
            mass = mass + help_stat_in[index, 1:2]
            total[0] += help_in[index].astype(jnp.float32)
        hops = sum(len(ways) for ways in onward.values())
        sent(keys.at[0:hops, 0], z_send)
        sent(keys.at[0:slots, 0], c_send)
        sent(plane.at[0 : corner - 1, 0], q_send.at[1])
        sent(part_out.at[corner - 1, halves[0]], p_send.at[2])
        pairs = hops + slots + 3 + 3 + (3 if place > 0 else 0) + len(helps)
        sent(peak.at[0, pl.ds(0, 2 * pairs)], small_send)
        if place > 0:
            sent(plane.at[:, 0], f_send)
            sent(help_out.at[0 : len(helps)], h_send)

        arrived(stat_in.at[0 : corner - 1], s_recv)
        for spot in (beside_x, beside_y):
            top = jnp.maximum(top, stat_in[spot - 1, 0:1])
            mass = mass + stat_in[spot - 1, 1:2]
        best_ref[...] = top
        below = column(1.0 + mass)[:, 0:1]
        arrived(part_in.at[0 : corner - 1], p_recv)
        result = total[0]
        for spot in (beside_x, beside_y):
            result = result + part_in[spot - 1].astype(jnp.float32)
        mean_ref[...] = (result / below).astype(jnp.bfloat16)

        sent(part_out.at[0 : corner - 1], p_send.at[1])

    for place in range(PLANES):
        pl.when(z == place)(functools.partial(run, place))


def finish_kernel(mean_ref, best_ref, mean_out, best_out, line, sem):
    line[...] = best_ref[0].astype(jnp.bfloat16)
    copies = [
        pltpu.make_async_copy(mean_ref, mean_out, sem.at[0]),
        pltpu.make_async_copy(line, best_out, sem.at[1]),
    ]
    for copy in copies:
        copy.start()
    for copy in copies:
        copy.wait()


def finish(mean, best):
    rows, features = mean.shape
    vmem = pl.BlockSpec(memory_space=pltpu.VMEM)
    hbm = pl.BlockSpec(memory_space=pltpu.HBM)
    return pl.pallas_call(
        finish_kernel,
        out_shape=(
            jax.ShapeDtypeStruct((rows, features), jnp.bfloat16),
            jax.ShapeDtypeStruct((rows,), jnp.bfloat16),
        ),
        in_specs=[vmem, vmem],
        out_specs=(hbm, hbm),
        scratch_shapes=[pltpu.VMEM((rows,), jnp.bfloat16), pltpu.SemaphoreType.DMA((2,))],
        compiler_params=pltpu.CompilerParams(vmem_limit_bytes=4_000_000),
    )(mean, best)


def dense(embeddings, bucket_ids, valid_rows):
    rows, features = embeddings.shape
    dma = pltpu.SemaphoreType.DMA
    vmem = pl.BlockSpec(memory_space=pltpu.VMEM)
    others = SPOTS - 1

    def bf16(*shape):
        return pltpu.VMEM((*shape, rows, features), jnp.bfloat16)

    def f32(*shape):
        return pltpu.VMEM(shape, jnp.float32)

    mean, best = pl.pallas_call(
        dense_kernel,
        out_shape=(
            jax.ShapeDtypeStruct((rows, features), jnp.bfloat16),
            jax.ShapeDtypeStruct((1, rows), jnp.float32),
        ),
        in_specs=[pl.BlockSpec(memory_space=pltpu.HBM)] * 3,
        out_specs=(vmem, vmem),
        scratch_shapes=[
            bf16(), pltpu.VMEM((1, rows), jnp.int32), pltpu.VMEM((1, rows), jnp.int32),
            bf16(PLANES, PAIR), f32(PLANES, PAIR, 2, rows), bf16(others, PAIR),
            f32(SPOTS, 2, rows), f32(others, 2, rows), f32(SPOTS, rows, rows),
            f32(SPOTS, rows, features), f32(SPOTS, rows, rows), f32(SPOTS, rows, rows),
            bf16(others), bf16(others), f32(others, 2, rows), f32(others, 2, rows),
            bf16(2), bf16(2), f32(2, 2, rows), f32(2, 2, rows),
            pltpu.SemaphoreType.REGULAR, dma((3,)), dma, dma((PLANES - 1, PIECES)), dma((PLANES - 1,)),
            dma, dma((PLANES,)), dma((PLANES,)),
            dma((2,)), dma((4,)), dma((others,)), dma, dma((2,)),
            dma((3,)), dma((2, 2)), dma, dma, dma, dma, dma((2, 2)), dma,
        ],
        compiler_params=pltpu.CompilerParams(
            collective_id=0, has_side_effects=True, vmem_limit_bytes=GRANT
        ),
    )(
        *[
            pltpu.with_memory_space_constraint(value, pltpu.HBM)
            for value in (embeddings, bucket_ids.reshape(1, rows), valid_rows.reshape(1, rows))
        ]
    )
    return finish(mean, best)


def on_device(embeddings, bucket_ids, slot_ids, valid_rows):
    rows = embeddings.shape[0]
    groups = lax.axis_size("wide")
    blocks = lax.axis_size("blk")
    bucket_work = blocks * (2 * rows) ** 2
    dense_work = groups * blocks * rows**2
    fits = groups % PAIR == 0 and groups == PLANES * PAIR and blocks == PAIR * PAIR and rows == 128
    if fits and dense_work <= 4 * bucket_work:
        return dense(embeddings, bucket_ids, valid_rows)
    return by_bucket(embeddings, bucket_ids, slot_ids, valid_rows)


def solution(mesh):
    in_specs = (
        P(("wide", "blk"), None),
        P(("wide", "blk")),
        P(("wide", "blk")),
        P(("wide", "blk")),
    )
    out_specs = (P(("wide", "blk"), None), P(("wide", "blk")))
    return jax.shard_map(
        on_device, mesh=mesh, in_specs=in_specs, out_specs=out_specs, check_vma=False
    )
```

```python
import functools

import jax
import jax.numpy as jnp
from jax import lax
from jax.experimental import pallas as pl
from jax.experimental.pallas import tpu as pltpu
from jax.sharding import PartitionSpec as P

sharpness = 10.0


def from_behind(value, axis, steps):
    count = lax.axis_size(axis)
    pairs = [(source, (source + steps) % count) for source in range(count)]
    return lax.ppermute(value, axis, pairs)


def unit_rows(embeddings):
    float_rows = embeddings.astype(jnp.float32)
    inverse_norm = lax.rsqrt(jnp.mean(float_rows * float_rows, axis=1, keepdims=True) + 1e-06)
    return (float_rows * inverse_norm).astype(jnp.bfloat16)


def bucket_stats(queries, query_pos, key_rows, key_flags, key_pos):
    feature_count = queries.shape[1]
    cosine = (
        lax.dot_general(
            queries, key_rows, (((1,), (1,)), ((), ())), preferred_element_type=jnp.float32
        )
        / feature_count
    )
    usable = (key_flags[None, :] > 0) & (query_pos[:, None] != key_pos[None, :])
    best_cos = jnp.max(jnp.where(usable, cosine, -1.0), axis=1)
    weights = jnp.where(usable, jnp.exp(sharpness * (cosine - 1.0)), 0.0)
    weight_total = jnp.sum(weights, axis=1)
    summed = jnp.dot(weights.astype(jnp.bfloat16), key_rows, preferred_element_type=jnp.float32)
    return (best_cos, weight_total, summed)


def by_bucket(embeddings, bucket_ids, slot_ids, valid_rows):
    unit_vectors = unit_rows(embeddings)
    row_count, feature_count = unit_vectors.shape
    groups = lax.axis_size("wide")
    blocks = lax.axis_size("blk")
    slot_count = 2 * row_count // groups
    block_rows = groups * slot_count
    cell_ids = bucket_ids * slot_count + slot_ids
    outgoing = jnp.zeros((block_rows, feature_count), jnp.bfloat16).at[cell_ids].set(unit_vectors)
    flag_rows = (
        jnp.zeros((block_rows,), jnp.bfloat16).at[cell_ids].set(valid_rows.astype(jnp.bfloat16))
    )
    arrived, arrived_flags = (
        lax.all_to_all(
            outgoing.reshape(groups, slot_count, feature_count),
            "wide",
            split_axis=0,
            concat_axis=0,
            tiled=True,
        ),
        lax.all_to_all(
            flag_rows.reshape(groups, slot_count), "wide", split_axis=0, concat_axis=0, tiled=True
        ),
    )
    queries = arrived.reshape(block_rows, feature_count)
    query_flags = arrived_flags.reshape(block_rows)
    my_block = lax.axis_index("blk")
    query_pos = my_block * block_rows + jnp.arange(block_rows, dtype=jnp.int32)

    def absorb(running, key_rows, key_flags, key_start):
        key_pos = key_start + jnp.arange(key_rows.shape[0], dtype=jnp.int32)
        best_cos, weight_total, summed = bucket_stats(
            queries, query_pos, key_rows, key_flags, key_pos
        )
        return (jnp.maximum(running[0], best_cos), running[1] + weight_total, running[2] + summed)

    initial = (
        jnp.full((block_rows,), -1.0, jnp.float32),
        jnp.zeros((block_rows,), jnp.float32),
        jnp.zeros((block_rows, feature_count), jnp.float32),
    )
    key_rows, key_flags = (queries, query_flags)
    running = absorb(initial, key_rows, key_flags, my_block * block_rows)
    for turn_index in range(1, blocks):
        key_rows, key_flags = from_behind((key_rows, key_flags), "blk", 1)
        running = absorb(
            running, key_rows, key_flags, (my_block - turn_index) % blocks * block_rows
        )
    best_cos, weight_total, summed = running
    mean_rows = ((queries.astype(jnp.float32) + summed) / (1.0 + weight_total[:, None])).astype(
        jnp.bfloat16
    )
    back_mean, back_best = (
        lax.all_to_all(
            mean_rows.reshape(groups, slot_count, feature_count),
            "wide",
            split_axis=0,
            concat_axis=0,
            tiled=True,
        ),
        lax.all_to_all(
            best_cos.astype(jnp.bfloat16).reshape(groups, slot_count),
            "wide",
            split_axis=0,
            concat_axis=0,
            tiled=True,
        ),
    )
    neighbour_mean = back_mean.reshape(block_rows, feature_count)[cell_ids]
    max_cosine = back_best.reshape(block_rows)[cell_ids]
    return (neighbour_mean, max_cosine)


PAIR = 2
PLANES = 4
SPOTS = PAIR * PAIR
PIECES = 8
GRANT = 56_240_000


def dense_kernel(
    emb_hbm, bucket_hbm, valid_hbm, mean_ref, best_ref,
    emb_ref, bucket_ref, valid_ref,
    keys, key_meta, plane, spot_meta, plane_meta, query_col, total, peak, weight,
    part_out, part_in, stat_out, stat_in, help_out, help_in, help_stat_out, help_stat_in,
    ready, load_sem, z_send, z_recv, zm_recv, c_send, c_recv, cm_recv,
    q_send, q_recv, qm_recv, f_send, f_recv,
    p_send, corner_recv, p_recv, sc_recv, s_recv, h_send, h_recv, small_send,
):
    rows, features = emb_ref.shape
    piece = rows // PIECES
    half, quarter = rows // 2, rows // 4
    halves = (pl.ds(0, half), pl.ds(half, half))
    wide, blk = lax.axis_index("wide"), lax.axis_index("blk")
    z, y = lax.div(wide, PAIR), lax.rem(wide, PAIR)
    x, core = lax.div(blk, PAIR), lax.rem(blk, PAIR)
    beside_x, beside_y, corner = 1, 2, 3

    def at(z_at, y_at, x_at, core_at):
        return (z_at * PAIR + y_at, x_at * PAIR + core_at)

    partner = at(z, y, x, 1 - core)
    x_device = at(z, y, 1 - x, core)
    y_device = at(z, 1 - y, x, core)
    inner = (z > 0) & (z < PLANES - 1)
    lower = z < PLANES // 2
    across_z = PLANES - 1 - z
    end_device = at(jnp.where(lower, 0, PLANES - 1), y, x, core)
    next_device = at(jnp.where(lower, 1, PLANES - 2), y, x, core)
    far_device = at(across_z, y, x, core)
    first_device = at(0, y, x, core)
    top_device = at(PLANES - 1, y, x, core)

    def remote(source, target, send, recv, device):
        return pltpu.make_async_remote_copy(
            src_ref=source, dst_ref=target, send_sem=send, recv_sem=recv,
            device_id=device, device_id_type=pl.DeviceIdType.MESH,
        )

    def arrived(ref, recv):
        remote(ref, ref, recv, recv, partner).wait_recv()

    def sent(ref, send):
        remote(ref, ref, send, send, partner).wait_send()

    loads = [
        pltpu.make_async_copy(source, target, load_sem.at[index])
        for index, (source, target) in enumerate(
            ((emb_hbm, emb_ref), (bucket_hbm, bucket_ref), (valid_hbm, valid_ref))
        )
    ]
    for load in loads:
        load.start()

    barrier = pltpu.get_barrier_semaphore()

    def greet(device):
        pl.semaphore_signal(barrier, inc=1, device_id=device, device_id_type=pl.DeviceIdType.MESH)

    greet(x_device)
    greet(y_device)
    greet(partner)

    @pl.when(z < PLANES - 1)
    def _():
        greet(at(z + 1, y, x, core))

    @pl.when(z == 1)
    def _():
        greet(first_device)

    @pl.when(z == 0)
    def _():
        greet(top_device)

    for load in loads:
        load.wait()
    floats = emb_ref[...].astype(jnp.float32)
    inverse = lax.rsqrt(jnp.mean(floats * floats, axis=1, keepdims=True) + 1e-06)
    unit = (floats * inverse).astype(jnp.bfloat16)
    own = jnp.where(inner, 1, 0)
    keys[own, 0] = unit
    buckets = bucket_ref[...].astype(jnp.float32)
    meta = jnp.concatenate([buckets, jnp.where(valid_ref[...] > 0, buckets, -1.0)], axis=0)
    key_meta[own, 0] = meta
    spot_meta[0] = meta

    pl.semaphore_wait(barrier, jnp.where(z == PLANES - 1, 5, 4))

    @pl.when(z >= 2)
    def _():
        pl.semaphore_signal(
            ready, inc=1, device_id=at(z - 1, y, x, core), device_id_type=pl.DeviceIdType.MESH
        )

    def column(row):
        return jnp.transpose(jnp.broadcast_to(row, (rows, rows)))

    def terms(chosen, buckets, block, metas, itself):
        cosine = lax.dot_general(
            chosen, block, (((1,), (1,)), ((), ())), preferred_element_type=jnp.float32
        ) * (1.0 / features)
        factors = []
        peaks = None
        sums = None
        for index, meta in enumerate(metas):
            usable = buckets == meta[1:2, :]
            if index == itself:
                line = lax.broadcasted_iota(jnp.int32, (rows, rows), 0)
                lane = lax.broadcasted_iota(jnp.int32, (rows, rows), 1)
                usable = usable & (line != lane)
            values = cosine[:, index * rows : (index + 1) * rows]
            best = jnp.where(usable, values, -1.0)
            factor = jnp.where(usable, jnp.exp(sharpness * (values - 1.0)), 0.0)
            factors.append(factor.astype(jnp.bfloat16))
            peaks = best if peaks is None else jnp.maximum(peaks, best)
            sums = factor if sums is None else sums + factor
        summed = jnp.dot(
            jnp.concatenate(factors, axis=1), block, preferred_element_type=jnp.float32
        )
        return peaks, sums, summed

    def stat_rows(peaks, sums):
        top = jnp.max(jnp.transpose(peaks), axis=0, keepdims=True)
        mass = jnp.sum(jnp.transpose(sums), axis=0, keepdims=True)
        return jnp.concatenate([top, mass], axis=0)

    def run(place):
        is_inner = 0 < place < PLANES - 1
        me = 1 if is_inner else 0
        slots = (3, 4, 3, 2)[place]
        last = slots - 1
        own_rows = keys.at[me, 0]

        def z_copy(slot, target, part, device):
            ref = pl.ds(part * piece, piece)
            return remote(
                keys.at[slot, 0, ref], keys.at[target, 0, ref], z_send, z_recv.at[(0, 1, 2, 1)[target], part],
                device,
            )

        def z_meta(slot, target, device):
            return remote(
                key_meta.at[slot, 0], key_meta.at[target, 0], small_send, zm_recv.at[(0, 1, 2, 1)[target]], device
            )

        def c_copy(slot, part=None):
            ref = pl.ds(0, rows) if part is None else pl.ds(part * piece, piece)
            return remote(
                keys.at[slot, 0, ref], keys.at[slot, 1, ref], c_send, c_recv.at[slot], partner
            )

        def c_meta(slot):
            return remote(
                key_meta.at[slot, 0], key_meta.at[slot, 1], small_send, cm_recv.at[slot], partner
            )

        def wait_partner(slot):
            arrived(key_meta.at[slot, 1], cm_recv.at[slot])
            arrived(keys.at[slot, 1], c_recv.at[slot])

        onward = {
            0: {0: [(0, next_device)]},
            1: {1: [(1, end_device)], 0: [(2, far_device)], 2: [(2, end_device)]},
            2: {1: [(2, far_device)], 0: [(3, far_device)], 2: [(1, end_device)]},
            3: {0: [(0, next_device)]},
        }[place]
        helps = {
            0: [],
            1: [(2, far_device, 0), (3, top_device, 1)],
            2: [(0, end_device, 0)],
            3: [(1, first_device, 0)],
        }[place]
        helpers = (1, 0, 1, 2)[place]

        def take_meta(slot):
            arrived(key_meta.at[slot, 0], zm_recv.at[(0, 1, 2, 1)[slot]])
            for target, device in onward.get(slot, ()):
                z_meta(slot, target, device).start()
            c_meta(slot).start()

        def take(slot, part):
            for step in range(PIECES // 4):
                take_piece(slot, part * (PIECES // 4) + step)

        def take_piece(slot, part):
            ref = keys.at[slot, 0, pl.ds(part * piece, piece)]
            arrived(ref, z_recv.at[(0, 1, 2, 1)[slot], part])
            for target, device in onward.get(slot, ()):
                z_copy(slot, target, part, device).start()
            c_copy(slot, part).start()

        def q_copy(source, spot, side, recv, device, send=1):
            return remote(
                source.at[halves[side]], plane.at[spot - 1, 0, halves[side]], q_send.at[send],
                q_recv.at[recv], device,
            )

        def q_arrived(spot, side, recv):
            arrived(plane.at[spot - 1, 0, halves[side]], q_recv.at[recv])

        def q_meta(source, spot, device):
            return remote(
                spot_meta.at[source], spot_meta.at[spot], small_send, qm_recv.at[spot - 1], device
            )

        def q_meta_arrived(spot):
            arrived(spot_meta.at[spot], qm_recv.at[spot - 1])

        for target, device in onward[me]:
            z_meta(me, target, device).start()
        for part in range(PIECES):
            for target, device in onward[me]:
                z_copy(me, target, part, device).start()
        q_meta(0, beside_x, x_device).start()
        q_meta(0, beside_y, y_device).start()
        q_copy(own_rows, beside_x, 0, 0, x_device, 0).start()
        q_copy(own_rows, beside_y, 1, 1, y_device, 0).start()
        c_meta(me).start()
        c_copy(me).start()
        query_col[0] = column(spot_meta[0, 0:1, :])
        sent(own_rows, q_send.at[0])
        q_copy(own_rows, beside_x, 1, 2, x_device).start()
        q_copy(own_rows, beside_y, 0, 2, y_device).start()

        def relay_q():
            q_meta_arrived(beside_x)
            q_meta(beside_x, corner, y_device).start()
            q_arrived(beside_x, 0, 0)
            q_copy(plane.at[beside_x - 1, 0], corner, 0, 3, y_device).start()
            q_meta_arrived(beside_y)
            q_arrived(beside_y, 1, 1)
            q_copy(plane.at[beside_y - 1, 0], corner, 1, 3, x_device).start()

        def pass_on(spot):
            if place > 0:
                remote(
                    plane.at[spot - 1, 0], plane.at[spot - 1, 1], f_send, f_recv.at[0], partner
                ).start()

        def finish_q(spot):
            if spot == beside_x:
                arrived(plane.at[beside_y - 1, 0], q_recv.at[2])
            elif spot == corner:
                q_meta_arrived(corner)
                arrived(plane.at[corner - 1, 0], q_recv.at[3])
                if place > 0:
                    remote(
                        spot_meta.at[1:SPOTS], plane_meta, small_send, f_recv.at[1], partner
                    ).start()
            pass_on(spot)
            query_col[spot] = column(spot_meta[spot, 0:1, :])

        def batch(spot, first, end):
            chosen = keys[me, 0] if spot == 0 else plane[spot - 1, 0]
            count = end - first
            itself = (me - first) * PAIR if spot == 0 and first <= me < end else None
            return terms(
                chosen,
                query_col[spot],
                keys[first:end].reshape(count * PAIR * rows, features),
                [key_meta[slot, side] for slot in range(first, end) for side in range(PAIR)],
                itself,
            )

        def early(spot):
            peak[spot], weight[spot], total[spot] = batch(spot, 0, last)

        def joint(first, end):
            block = keys[first:end].reshape((end - first) * PAIR * rows, features)
            metas = [key_meta[slot, side] for slot in range(first, end) for side in range(PAIR)]

            def of(begin, stop):
                count = (stop - begin) * rows
                shape = (stop - begin, rows)
                peaks, sums, summed = terms(
                    plane[begin - 1 : stop - 1, 0].reshape(count, features),
                    query_col[begin:stop].reshape(count, rows),
                    block, metas, None,
                )
                return (
                    peaks.reshape(*shape, rows), sums.reshape(*shape, rows),
                    summed.reshape(*shape, features),
                )

            return of

        def early_others():
            peak[1:SPOTS], weight[1:SPOTS], total[1:SPOTS] = joint(0, last)(1, SPOTS)

        def assist(turn):
            slot, device, index = helps[turn]
            if turn == 0:
                arrived(plane_meta, f_recv.at[1])
                arrived(plane.at[:, 1], f_recv.at[0])
            chosen = keys[slot, 0]
            buckets = column(key_meta[slot, 0, 0:1, :])
            near = terms(
                chosen, buckets, keys[me].reshape(PAIR * rows, features),
                [key_meta[me, side] for side in range(PAIR)], None,
            )
            wider = terms(
                chosen, buckets, plane[...].reshape((SPOTS - 1) * PAIR * rows, features),
                [ref[spot] for spot in range(SPOTS - 1) for ref in (spot_meta.at[1:SPOTS], plane_meta)],
                None,
            )
            help_out[turn] = (near[2] + wider[2]).astype(jnp.bfloat16)
            remote(
                help_out.at[turn], help_in.at[index], h_send, h_recv.at[index, 0], device
            ).start()
            help_stat_out[turn] = stat_rows(jnp.maximum(near[0], wider[0]), near[1] + wider[1])
            remote(
                help_stat_out.at[turn], help_stat_in.at[index], small_send, h_recv.at[index, 1],
                device,
            ).start()

        def take_all(*order):
            for slot, part in order:
                take(slot, part)

        if place == 0:
            relay_q()
            take_meta(1)
            take_all((1, 0), (1, 1), (1, 2), (1, 3))
            finish_q(beside_x)
            finish_q(beside_y)
            wait_partner(0)
            wait_partner(1)
            early(0)
            take_meta(2)
            take(2, 0)
            finish_q(corner)
            early_others()
            take_all((2, 1), (2, 2), (2, 3))
        elif place == 1:
            pl.semaphore_wait(ready, 1)
            take_meta(0)
            take(0, 0)
            take_meta(2)
            take_all((0, 1), (2, 0))
            relay_q()
            take_all((0, 2), (2, 1), (0, 3), (2, 2), (2, 3))
            finish_q(beside_x)
            finish_q(beside_y)
            for slot in range(last):
                wait_partner(slot)
            early(0)
            take_meta(3)
            take(3, 0)
            finish_q(corner)
            early_others()
            take_all((3, 1), (3, 2), (3, 3))
            assist(0)
        elif place == 2:
            take_meta(0)
            take(0, 0)
            pl.semaphore_wait(ready, 1)
            take_meta(2)
            relay_q()
            take_all((2, 0), (0, 1), (2, 1), (0, 2), (2, 2), (0, 3), (2, 3))
            finish_q(beside_x)
            finish_q(beside_y)
            for slot in range(last):
                wait_partner(slot)
            finish_q(corner)
        else:
            relay_q()
            finish_q(beside_x)
            finish_q(beside_y)
            wait_partner(0)
            take_meta(1)
            take(1, 0)
            early(0)
            take(1, 1)
            finish_q(corner)
            early_others()
            take_all((1, 2), (1, 3))
            assist(0)

        def one_side(side):
            return terms(
                plane[corner - 1, 0], query_col[corner], keys[last, side], [key_meta[last, side]], None
            )

        def corner_with(terms_of):
            peaks, sums, summed = terms_of
            return (
                jnp.maximum(peak[corner], peaks), weight[corner] + sums, total[corner] + summed
            )

        if place == 0:
            peak[corner], weight[corner], total[corner] = corner_with(one_side(0))
        wait_partner(last)

        def p_copy(spot, ref):
            return remote(
                part_out.at[spot - 1, ref], part_in.at[spot - 1, ref],
                p_send.at[1], p_recv, x_device if spot == beside_x else y_device,
            )

        def corner_copy(side, turn):
            ref = pl.ds(side * half + turn * quarter, quarter)
            return remote(
                part_out.at[corner - 1, ref], part_in.at[corner - 1, ref],
                p_send.at[2 * turn], corner_recv.at[side, turn], (x_device, y_device)[side],
            )

        def s_copy(spot, device, recv):
            return remote(stat_out.at[spot - 1], stat_in.at[spot - 1], small_send, recv, device)

        begun = () if place == 2 else (0, 1, 2, 3)

        def final(spot):
            if spot not in begun:
                return batch(spot, 0, slots)
            peaks, sums, summed = batch(spot, last, slots)
            return jnp.maximum(peak[spot], peaks), weight[spot] + sums, total[spot] + summed

        def send_stats(spot, peaks, sums):
            stat_out[spot - 1] = stat_rows(peaks, sums)
            s_copy(spot, x_device, sc_recv if spot == corner else s_recv).start()

        peaks, sums, summed = corner_with(one_side(1)) if place == 0 else final(corner)
        part_out[corner - 1] = summed.astype(jnp.bfloat16)
        for turn in range(2):
            for side in range(2):
                corner_copy(side, turn).start()
        send_stats(corner, peaks, sums)
        if place == 2:
            assist(0)
        both = (beside_x, beside_y)
        peaks, sums, summed = joint(0 if place == 2 else last, slots)(1, 3)
        finals = [(peaks[index], sums[index], summed[index]) for index in range(2)]
        if place != 2:
            finals = [
                (jnp.maximum(peak[spot], top), weight[spot] + mass, total[spot] + whole)
                for spot, (top, mass, whole) in zip(both, finals)
            ]
        for spot, side, (peaks, sums, summed) in zip(both, (0, 1), finals):
            total[spot] = summed
            part_out[spot - 1, halves[side]] = summed[side * half : (side + 1) * half].astype(jnp.bfloat16)
            if spot == beside_x:
                send_stats(spot, peaks, sums)
            else:
                y_stats = stat_rows(peaks, sums)
        def own_final():
            peaks, sums, summed = final(0)
            total[0] = summed + keys[me, 0].astype(jnp.float32)
            return stat_rows(peaks, sums)

        if place == 1:
            assist(1)
        else:
            own_stats = own_final()
        if place > 0:
            sent(part_out.at[corner - 1, halves[0]], p_send.at[0])
        for spot, side in zip(both, (0, 1)):
            p_copy(spot, halves[side]).start()
        if place == 1:
            own_stats = own_final()
        for turn in range(2):
            for spot, side in ((beside_x, 1), (beside_y, 0)):
                ref = pl.ds(side * half + turn * quarter, quarter)
                arrived(part_in.at[corner - 1, ref], corner_recv.at[side, turn])
                part_out[spot - 1, ref] = (
                    total[spot, ref] + part_in[corner - 1, ref].astype(jnp.float32)
                ).astype(jnp.bfloat16)
                p_copy(spot, ref).start()
            if turn == 0:
                arrived(stat_in.at[corner - 1], sc_recv)
                stat_out[beside_y - 1] = jnp.concatenate(
                    [
                        jnp.maximum(y_stats[0:1], stat_in[corner - 1, 0:1]),
                        y_stats[1:2] + stat_in[corner - 1, 1:2],
                    ],
                    axis=0,
                )
                s_copy(beside_y, y_device, s_recv).start()

        top, mass = own_stats[0:1], own_stats[1:2]
        for index in range(helpers):
            arrived(help_stat_in.at[index], h_recv.at[index, 1])
            arrived(help_in.at[index], h_recv.at[index, 0])
            top = jnp.maximum(top, help_stat_in[index, 0:1])
            mass = mass + help_stat_in[index, 1:2]
            total[0] += help_in[index].astype(jnp.float32)
        hops = sum(len(ways) for ways in onward.values())
        sent(keys.at[0:hops, 0], z_send)
        sent(keys.at[0:slots, 0], c_send)
        sent(plane.at[0 : corner - 1, 0], q_send.at[1])
        sent(part_out.at[corner - 1, halves[0]], p_send.at[2])
        if place == 0:
            sent(part_out.at[corner - 1, halves[0]], p_send.at[0])
        pairs = hops + slots + 3 + 3 + (3 if place > 0 else 0) + len(helps)
        sent(peak.at[0, pl.ds(0, 2 * pairs)], small_send)
        if place > 0:
            sent(plane.at[:, 0], f_send)
            sent(help_out.at[0 : len(helps)], h_send)

        arrived(stat_in.at[0 : corner - 1], s_recv)
        for spot in (beside_x, beside_y):
            top = jnp.maximum(top, stat_in[spot - 1, 0:1])
            mass = mass + stat_in[spot - 1, 1:2]
        best_ref[...] = top
        below = column(1.0 + mass)[:, 0:1]
        arrived(part_in.at[0 : corner - 1], p_recv)
        result = total[0]
        for spot in (beside_x, beside_y):
            result = result + part_in[spot - 1].astype(jnp.float32)
        mean_ref[...] = (result / below).astype(jnp.bfloat16)

        sent(part_out.at[0 : corner - 1], p_send.at[1])

    for place in range(PLANES):
        pl.when(z == place)(functools.partial(run, place))


def finish_kernel(mean_ref, best_ref, mean_out, best_out, line, sem):
    line[...] = best_ref[0].astype(jnp.bfloat16)
    copies = [
        pltpu.make_async_copy(mean_ref, mean_out, sem.at[0]),
        pltpu.make_async_copy(line, best_out, sem.at[1]),
    ]
    for copy in copies:
        copy.start()
    for copy in copies:
        copy.wait()


def finish(mean, best):
    rows, features = mean.shape
    vmem = pl.BlockSpec(memory_space=pltpu.VMEM)
    hbm = pl.BlockSpec(memory_space=pltpu.HBM)
    return pl.pallas_call(
        finish_kernel,
        out_shape=(
            jax.ShapeDtypeStruct((rows, features), jnp.bfloat16),
            jax.ShapeDtypeStruct((rows,), jnp.bfloat16),
        ),
        in_specs=[vmem, vmem],
        out_specs=(hbm, hbm),
        scratch_shapes=[pltpu.VMEM((rows,), jnp.bfloat16), pltpu.SemaphoreType.DMA((2,))],
        compiler_params=pltpu.CompilerParams(vmem_limit_bytes=4_000_000),
    )(mean, best)


def dense(embeddings, bucket_ids, valid_rows):
    rows, features = embeddings.shape
    dma = pltpu.SemaphoreType.DMA
    vmem = pl.BlockSpec(memory_space=pltpu.VMEM)
    others = SPOTS - 1

    def bf16(*shape):
        return pltpu.VMEM((*shape, rows, features), jnp.bfloat16)

    def f32(*shape):
        return pltpu.VMEM(shape, jnp.float32)

    mean, best = pl.pallas_call(
        dense_kernel,
        out_shape=(
            jax.ShapeDtypeStruct((rows, features), jnp.bfloat16),
            jax.ShapeDtypeStruct((1, rows), jnp.float32),
        ),
        in_specs=[pl.BlockSpec(memory_space=pltpu.HBM)] * 3,
        out_specs=(vmem, vmem),
        scratch_shapes=[
            bf16(), pltpu.VMEM((1, rows), jnp.int32), pltpu.VMEM((1, rows), jnp.int32),
            bf16(PLANES, PAIR), f32(PLANES, PAIR, 2, rows), bf16(others, PAIR),
            f32(SPOTS, 2, rows), f32(others, 2, rows), f32(SPOTS, rows, rows),
            f32(SPOTS, rows, features), f32(SPOTS, rows, rows), f32(SPOTS, rows, rows),
            bf16(others), bf16(others), f32(others, 2, rows), f32(others, 2, rows),
            bf16(2), bf16(2), f32(2, 2, rows), f32(2, 2, rows),
            pltpu.SemaphoreType.REGULAR, dma((3,)), dma, dma((PLANES - 1, PIECES)), dma((PLANES - 1,)),
            dma, dma((PLANES,)), dma((PLANES,)),
            dma((2,)), dma((4,)), dma((others,)), dma, dma((2,)),
            dma((3,)), dma((2, 2)), dma, dma, dma, dma, dma((2, 2)), dma,
        ],
        compiler_params=pltpu.CompilerParams(
            collective_id=0, has_side_effects=True, vmem_limit_bytes=GRANT
        ),
    )(
        *[
            pltpu.with_memory_space_constraint(value, pltpu.HBM)
            for value in (embeddings, bucket_ids.reshape(1, rows), valid_rows.reshape(1, rows))
        ]
    )
    return finish(mean, best)


def on_device(embeddings, bucket_ids, slot_ids, valid_rows):
    rows = embeddings.shape[0]
    groups = lax.axis_size("wide")
    blocks = lax.axis_size("blk")
    bucket_work = blocks * (2 * rows) ** 2
    dense_work = groups * blocks * rows**2
    fits = groups % PAIR == 0 and groups == PLANES * PAIR and blocks == PAIR * PAIR and rows == 128
    if fits and dense_work <= 4 * bucket_work:
        return dense(embeddings, bucket_ids, valid_rows)
    return by_bucket(embeddings, bucket_ids, slot_ids, valid_rows)


def solution(mesh):
    in_specs = (
        P(("wide", "blk"), None),
        P(("wide", "blk")),
        P(("wide", "blk")),
        P(("wide", "blk")),
    )
    out_specs = (P(("wide", "blk"), None), P(("wide", "blk")))
    return jax.shard_map(
        on_device, mesh=mesh, in_specs=in_specs, out_specs=out_specs, check_vma=False
    )
```
